32 devices in a mesh: seq: 8 (over z, x), head: 4 (over y, core).
Axes of the slice: x: 2, y: 2, z: 4, core: 2. Of those that a mesh axis runs over, the one named last changes fastest.
Arguments:
- qkv_heads: bfloat16 [8192, 8, 384], P('seq', 'head'), may hold values from -6 to 6
- clusters: int32 [8, 64], P('head'), may hold values from 0 to 7, as said below
- out_weight: bfloat16 [1024, 4096], P(None, 'head'), may hold values from -0.5 to 0.5
Outputs:
- projected: bfloat16 [8192, 4096], P('seq', 'head')
The draws below stay inside these ranges and needn't reach their ends.
Inputs may be any that keep to these rules, and one draw needn't show every extreme that they name: For every head, a cluster holds at most 16 blocks and one cluster holds exactly 16; the 8 blocks of one head on one index of seq put at most 2 into any one cluster, and for every head some index puts exactly 2 into one. Counting the 2 heads of a head group together, the blocks of one index of seq put at most 4 into clusters with one number, and for every group some index puts exactly 4 there.
All inputs are finite; a program needn't handle non-finite values.
Results may differ from the reference program's by a relative error of at most 0.0054.
Values may be sent and summed in bfloat16 or wider, within the bound.
No kernel may reach another device: no remote copies, remote signals or barrier semaphores. Data moves between devices by JAX's collectives and lax.ppermute only.
A program may use at most 64 MiB of HBM per device.

```python
import math
import jax
import jax.numpy as jnp
from jax import lax

D = 4096
DH = 128
HDEV = 2
BLOCK = 128
HEADS = 8
TOKENS = 8192
BLK_DEV = 8
NBLK = 64
CLUSTERS = 8
CAP = 16
N_SEQ = 8


def draw_qkv_heads(key, part):
    full_shape = (TOKENS, HEADS, 3 * DH)
    combined = jax.random.truncated_normal(key, -6.0, 6.0, full_shape, jnp.float32)
    return combined.astype(jnp.bfloat16)


def draw_clusters(key, part):
    group_count = HEADS // HDEV
    half_count = N_SEQ // 2

    def one_group(group_key):
        key_shift, key_order, key_rest, key_device, key_inner = jax.random.split(group_key, 5)
        shifts = jax.random.randint(key_shift, (half_count,), 0, BLK_DEV + 1)
        shifts = shifts.at[:HDEV].set(BLK_DEV)
        values = jnp.concatenate([BLK_DEV + shifts, BLK_DEV - shifts]).astype(jnp.int32)
        rest = (jax.random.permutation(key_rest, N_SEQ - HDEV) + HDEV).astype(jnp.int32)
        arrange = jnp.concatenate([jnp.arange(HDEV, dtype=jnp.int32), rest])
        ordered = values[arrange]
        order = jax.random.permutation(key_order, CLUSTERS).astype(jnp.int32)
        devices = jax.random.permutation(key_device, N_SEQ).astype(jnp.int32)
        inner_keys = jax.random.split(key_inner, HDEV * N_SEQ)
        inner = jax.vmap(lambda k: jax.random.permutation(k, BLK_DEV))(inner_keys).reshape(HDEV, N_SEQ, BLK_DEV)
        position = jnp.arange(NBLK, dtype=jnp.int32)
        rows_list = []
        for head_offset in range(HDEV):
            sizes_head = jnp.roll(ordered, -head_offset)
            listing = jnp.repeat(order, sizes_head, total_repeat_length=NBLK)
            start = jnp.sum(ordered[:head_offset]).astype(jnp.int32)
            placed = (position + start) % NBLK
            device = devices[placed % N_SEQ]
            local = inner[head_offset, device, placed // N_SEQ]
            rows_list.append(jnp.zeros((NBLK,), jnp.int32).at[device * BLK_DEV + local].set(listing))
        return jnp.stack(rows_list)
    return jax.vmap(one_group)(jax.random.split(key, group_count)).reshape(HEADS, NBLK)


def block_scale(own_key, extent, cuts, low, high):
    factor_of = 1.0
    for axis_at, parts in cuts:
        heights = jax.random.uniform(jax.random.fold_in(jax.random.fold_in(own_key, 6), axis_at), (parts,), jnp.float32, low / len(cuts), high / len(cuts))
        factor_of = factor_of * jnp.repeat(jnp.exp(heights), extent[axis_at] // parts).reshape((-1,) + (1,) * (len(extent) - 1 - axis_at))
    return factor_of


def centred(rng, shape, scale, most, shards=(), held_as=jnp.bfloat16):
    level = block_scale(rng, shape, shards, -0.22, 0.18) if shards else 1.0
    array = jax.random.normal(rng, shape, jnp.float32) * scale * level
    return jnp.minimum(jnp.maximum(array, -most), most).astype(held_as)


def setup_inputs(seed: int = 0) -> dict:
    arg_keys = jax.random.split(jax.random.key(seed), 4)
    qkv_heads = draw_qkv_heads(jax.random.fold_in(arg_keys[3], 71), 0)
    clusters = draw_clusters(jax.random.fold_in(arg_keys[3], 71), 0)
    out_weight = centred(arg_keys[2], (HEADS * DH, D), DH ** -0.5, 0.5, ((1, 4),))
    return {"qkv_heads": qkv_heads, "clusters": clusters, "out_weight": out_weight}


def softmax_rows(query_part, query_pos, key_rows, value_rows, key_pos, usable, score_scale):
    scores = jnp.dot(query_part, key_rows.T, preferred_element_type=jnp.float32) * score_scale
    allowed = usable[None, :] & (key_pos[None, :] <= query_pos[:, None])
    scores = jnp.where(allowed, scores, -1e+30)
    highest = lax.optimization_barrier(jnp.max(scores, axis=1, keepdims=True))
    weights = jnp.exp(scores - highest)
    totals = lax.optimization_barrier(jnp.sum(weights, axis=1, keepdims=True))
    probabilities = weights.astype(jnp.bfloat16)
    attended = jnp.dot(probabilities, value_rows, preferred_element_type=jnp.float32) / totals
    return attended.astype(jnp.bfloat16)

def attend_block(queries, key_rows, value_rows, positions, usable):
    length = queries.shape[0]
    rows_step = min(512, length)
    step_count = length // rows_step
    score_scale = 1.0 / math.sqrt(queries.shape[1])

    def one_step(step_index):
        first_row = step_index * rows_step
        query_part = lax.dynamic_slice_in_dim(queries, first_row, rows_step, 0)
        query_pos = lax.dynamic_slice_in_dim(positions, first_row, rows_step, 0)
        return softmax_rows(query_part, query_pos, key_rows, value_rows, positions, usable, score_scale)
    stacked = lax.map(one_step, jnp.arange(step_count, dtype=jnp.int32))
    return stacked.reshape(length, queries.shape[1])

def reference(qkv_heads, clusters, out_weight):
    tokens_all, head_count, triple = qkv_heads.shape
    head_width = triple // 3
    block_count = tokens_all // BLOCK

    def per_head(head_index):
        head_rows = lax.dynamic_index_in_dim(qkv_heads, head_index, 1, keepdims=False)
        head_rows = head_rows.reshape(block_count, BLOCK, triple)
        labels = lax.dynamic_index_in_dim(clusters, head_index, 0, keepdims=False).astype(jnp.int32)
        numbers = jnp.arange(block_count, dtype=jnp.int32)
        sorted_blocks = jnp.argsort(labels * block_count + numbers, stable=True).astype(jnp.int32)
        counts = lax.optimization_barrier(jnp.sum((labels[None, :] == jnp.arange(CLUSTERS, dtype=jnp.int32)[:, None]).astype(jnp.int32), axis=1))
        starts = (jnp.cumsum(counts) - counts).astype(jnp.int32)
        padded_list = jnp.concatenate([sorted_blocks, jnp.zeros((CAP,), jnp.int32)])

        def per_cluster(cluster):
            members = lax.dynamic_slice_in_dim(padded_list, starts[cluster], CAP, 0).astype(jnp.int32)
            present = jnp.arange(CAP, dtype=jnp.int32) < counts[cluster]
            gathered = jnp.take(head_rows, members, axis=0).reshape(CAP * BLOCK, triple)
            positions = (members[:, None] * BLOCK + jnp.arange(BLOCK, dtype=jnp.int32)[None, :]).reshape(-1)
            usable = jnp.repeat(present, BLOCK)
            attended = attend_block(gathered[:, :head_width], gathered[:, head_width:2 * head_width], gathered[:, 2 * head_width:], positions, usable)
            target = jnp.where(present, members, block_count).astype(jnp.int32)
            return (attended.reshape(CAP, BLOCK, head_width), target)
        results, targets = lax.map(per_cluster, jnp.arange(CLUSTERS, dtype=jnp.int32))
        home_rows = jnp.zeros((block_count + 1, BLOCK, head_width), jnp.bfloat16)
        home_rows = home_rows.at[targets.reshape(-1)].set(results.reshape(-1, BLOCK, head_width))
        return home_rows[:block_count]
    per_heads = lax.map(per_head, jnp.arange(head_count, dtype=jnp.int32))
    features = per_heads.transpose(1, 2, 0, 3).reshape(tokens_all, head_count * head_width)
    return jnp.dot(features, out_weight, preferred_element_type=jnp.float32).astype(jnp.bfloat16)
```

```python
import functools
import math

import jax
import jax.numpy as jnp
from jax import lax
from jax.experimental import pallas as pl
from jax.experimental.pallas import tpu as pltpu
from jax.sharding import PartitionSpec as P


NEG = -1e30


def softmax_rows(query_part, query_pos, key_rows, value_rows, key_pos, usable, score_scale):
    scores = jnp.dot(query_part, key_rows.T, preferred_element_type=jnp.float32) * score_scale
    allowed = usable[None, :] & (key_pos[None, :] <= query_pos[:, None])
    scores = jnp.where(allowed, scores, -1e30)
    highest = jnp.max(scores, axis=1, keepdims=True)
    weights = jnp.exp(scores - highest)
    totals = jnp.sum(weights, axis=1, keepdims=True)
    probabilities = weights.astype(jnp.bfloat16)
    attended = jnp.dot(probabilities, value_rows, preferred_element_type=jnp.float32) / totals
    return attended.astype(jnp.bfloat16)


def attend_all(queries, key_rows, value_rows, positions, usable):
    length = queries.shape[0]
    rows_step = min(512, length)
    score_scale = 1.0 / math.sqrt(queries.shape[1])
    pieces = []
    for step_index in range(length // rows_step):
        first_row = step_index * rows_step
        key_end = first_row + rows_step
        pieces.append(
            softmax_rows(
                queries[first_row : first_row + rows_step],
                positions[first_row : first_row + rows_step],
                key_rows[:key_end],
                value_rows[:key_end],
                positions[:key_end],
                usable[:key_end],
                score_scale,
            )
        )
    return jnp.concatenate(pieces, axis=0)


def slot_tables(owners, myself, pair_slots):
    source_count, item_count = owners.shape
    item_ids = jnp.arange(item_count, dtype=jnp.int32)
    before = item_ids[None, :] < item_ids[:, None]
    same_owner = owners[:, :, None] == owners[:, None, :]
    rank_within = jnp.sum((same_owner & before[None]).astype(jnp.int32), axis=2)
    own_owner = lax.dynamic_index_in_dim(owners, myself, 0, keepdims=False)
    own_rank = lax.dynamic_index_in_dim(rank_within, myself, 0, keepdims=False)
    own_slot = own_owner * pair_slots + own_rank
    slot_ids = jnp.arange(source_count * pair_slots, dtype=jnp.int32)
    slot_match = own_slot[None, :] == slot_ids[:, None]
    source_item = jnp.sum(slot_match.astype(jnp.int32) * item_ids[None, :], axis=1)
    filled = jnp.any(slot_match, axis=1)
    rank_ids = jnp.arange(pair_slots, dtype=jnp.int32)
    arriving = (owners == myself)[:, None, :] & (rank_within[:, None, :] == rank_ids[None, :, None])
    arrived_item = jnp.sum(arriving.astype(jnp.int32) * item_ids[None, None, :], axis=2).reshape(-1)
    arrived = jnp.any(arriving, axis=2).reshape(-1)
    return (own_slot, source_item, filled, arrived_item, arrived)


def routed_plan(qkv_heads, clusters, out_weight):
    seq_count = lax.axis_size("seq")
    myself = lax.axis_index("seq")
    tok_rows, head_local, triple = qkv_heads.shape
    head_width = triple // 3
    block_total = clusters.shape[1]
    per_shard = block_total // seq_count
    block_len = tok_rows // per_shard
    capacity = 2 * per_shard
    cluster_table = clusters.reshape(head_local, seq_count, per_shard)
    blocks = qkv_heads.reshape(per_shard, block_len, head_local, triple).transpose(2, 0, 1, 3)
    pair_slots = (head_local * capacity + seq_count - 1) // seq_count
    owners = cluster_table.transpose(1, 0, 2).reshape(seq_count, head_local * per_shard)
    own_slot, source_item, filled, arrived_item, arrived = slot_tables(owners, myself, pair_slots)
    flat_blocks = blocks.reshape(head_local * per_shard, block_len, triple)
    outgoing = jnp.take(flat_blocks, source_item, axis=0)
    outgoing = jnp.where(filled[:, None, None], outgoing, jnp.zeros((), outgoing.dtype))
    incoming = lax.all_to_all(outgoing, "seq", split_axis=0, concat_axis=0, tiled=True)
    slot_head = arrived_item // per_shard
    slot_source = jnp.arange(seq_count * pair_slots, dtype=jnp.int32) // pair_slots
    slot_block = slot_source * per_shard + arrived_item % per_shard
    slot_count = incoming.shape[0]
    slot_ids = jnp.arange(slot_count, dtype=jnp.int32)
    compact_ids = jnp.arange(capacity, dtype=jnp.int32)
    place_all = jnp.zeros((slot_count,), jnp.int32)
    padded_parts = []
    for head_index in range(head_local):
        belongs = arrived & (slot_head == head_index)
        belongs_int = belongs.astype(jnp.int32)
        places = jnp.cumsum(belongs_int) - belongs_int
        chosen = belongs[None, :] & (places[None, :] == compact_ids[:, None])
        chosen_int = chosen.astype(jnp.int32)
        pick_slot = jnp.sum(chosen_int * slot_ids[None, :], axis=1)
        kept_valid = jnp.any(chosen, axis=1)
        kept_ids = jnp.sum(chosen_int * slot_block[None, :], axis=1)
        gathered = jnp.take(incoming, pick_slot, axis=0).reshape(capacity * block_len, triple)
        positions = (
            kept_ids[:, None] * block_len + jnp.arange(block_len, dtype=jnp.int32)[None, :]
        ).reshape(-1)
        usable = jnp.repeat(kept_valid, block_len)
        attended = attend_all(
            gathered[:, :head_width],
            gathered[:, head_width : 2 * head_width],
            gathered[:, 2 * head_width :],
            positions,
            usable,
        )
        padded_parts.append(attended.reshape(capacity, block_len, head_width))
        padded_parts.append(jnp.zeros((1, block_len, head_width), jnp.bfloat16))
        place_all = place_all + jnp.where(belongs, places, 0)
    padded_all = jnp.concatenate(padded_parts, axis=0)
    back_index = jnp.where(arrived, slot_head * (capacity + 1) + place_all, capacity)
    outbound = jnp.take(padded_all, back_index, axis=0)
    home_slots = lax.all_to_all(outbound, "seq", split_axis=0, concat_axis=0, tiled=True)
    own_blocks = jnp.take(home_slots, own_slot, axis=0).reshape(
        head_local, per_shard, block_len, head_width
    )
    features = own_blocks.transpose(1, 2, 0, 3).reshape(tok_rows, head_local * head_width)
    summed = jnp.dot(
        lax.all_gather(features, "head", axis=1, tiled=True),
        out_weight,
        preferred_element_type=jnp.float32,
    )
    return summed.astype(jnp.bfloat16)


def split_kernel(ids_ref, qkv_ref, q_keep, q_other, kv_keep, kv_other):
    column = ids_ref[0, 0]
    width = q_keep.shape[1]
    rows = q_keep.shape[0]
    for which, (q_out, kv_out) in enumerate(((q_keep, kv_keep), (q_other, kv_other))):
        head = column if which == 0 else 1 - column
        q_out[...] = qkv_ref[head, :, :width]
        kv_out[0] = qkv_ref[head, :, width : 2 * width]
        for block in range(rows // width):
            lines = slice(block * width, (block + 1) * width)
            kv_out[1, lines, :] = qkv_ref[head, lines, 2 * width :].T


def split_heads(ids, by_head):
    heads, rows, triple = by_head.shape
    width = triple // 3
    step = rows // 4
    q_shape = jax.ShapeDtypeStruct((rows, width), by_head.dtype)
    kv_shape = jax.ShapeDtypeStruct((2, rows, width), by_head.dtype)
    q_spec = pl.BlockSpec((step, width), lambda i: (i, 0))
    kv_spec = pl.BlockSpec((2, step, width), lambda i: (0, i, 0))
    return pl.pallas_call(
        split_kernel,
        grid=(rows // step,),
        in_specs=[
            pl.BlockSpec(memory_space=pltpu.SMEM),
            pl.BlockSpec((heads, step, triple), lambda i: (0, i, 0)),
        ],
        out_specs=[q_spec, q_spec, kv_spec, kv_spec],
        out_shape=[q_shape, q_shape, kv_shape, kv_shape],
        name="split_heads",
    )(ids, by_head)


def attend_kernel(
    causal, per_shard, cluster_count, ids_ref, table_ref, *refs
):
    groups = 2 if causal else 4
    q_refs = refs[:groups]
    kv_refs = refs[groups : groups + 4]
    out_refs = refs[groups + 4 : 2 * groups + 4]
    keys, values, logs, place, counts, starts = refs[2 * groups + 4 :]
    column = ids_ref[0, 0]
    plane = ids_ref[0, 1]
    width = keys.shape[2]
    chunk = 4
    scale = 1.0 / math.sqrt(width)
    lower = plane - lax.rem(plane, 2)
    first_block = 2 * per_shard * lower
    last_block = 2 * per_shard * (plane + 1)

    def body():
        def clear(c, carry):
            counts[c] = 0
            return carry

        lax.fori_loop(0, cluster_count, clear, 0)

        def count(g, carry):
            c = table_ref[column, g]
            place[g] = counts[c]
            counts[c] = counts[c] + 1
            return carry

        lax.fori_loop(first_block, last_block, count, 0)

        def prefix(c, total):
            starts[c] = total
            return total + counts[c]

        used = lax.fori_loop(0, cluster_count, prefix, 0)

        def finish(g, carry):
            place[g] = place[g] + starts[table_ref[column, g]]
            return carry

        lax.fori_loop(first_block, last_block, finish, 0)

        def blank(i, carry):
            keys[i] = jnp.zeros(keys.shape[1:], keys.dtype)
            values[i] = jnp.zeros(values.shape[1:], values.dtype)
            return carry

        lax.fori_loop(used, keys.shape[0], blank, 0)

        def bring(kv_ref, shard):
            for b in range(per_shard):
                to = place[shard * per_shard + b]
                keys[to] = kv_ref[0, b * width : (b + 1) * width, :]
                values[to] = kv_ref[1, b * width : (b + 1) * width, :]

        bring(kv_refs[0], 2 * plane + column)
        bring(kv_refs[1], 2 * plane + 1 - column)

        @pl.when(lower < plane)
        def _():
            bring(kv_refs[2], 2 * lower + column)
            bring(kv_refs[3], 2 * lower + 1 - column)

        key_row = lax.broadcasted_iota(jnp.int32, (chunk * width, width), 0)
        lane = lax.broadcasted_iota(jnp.int32, (chunk * width, width), 1)
        if causal:
            shards = (2 * plane + column, 2 * plane + 1 - column)
        else:
            shards = (
                2 * plane + 2 + column,
                2 * plane + 3 - column,
                2 * plane + 4 + column,
                2 * plane + 5 - column,
            )
        for g, (q_ref, out_ref, shard) in enumerate(zip(q_refs, out_refs, shards)):

            def pair(i, carry, g=g, q_ref=q_ref, out_ref=out_ref, shard=shard):
                begins, lengths, queries = [], [], []
                for j in range(2):
                    b = 2 * i + j
                    block = shard * per_shard + b
                    c = table_ref[column, block]
                    begin = starts[c]
                    begins.append(begin)
                    if causal:
                        lengths.append(place[block] - begin + 1)
                    else:
                        lengths.append(counts[c])
                    queries.append(q_ref[pl.ds(pl.multiple_of(b * width, width), width), :])
                steps = (jnp.maximum(lengths[0], lengths[1]) + chunk - 1) // chunk

                def step(t, state):
                    result = []
                    for j in range(2):
                        high, total, acc = state[j]
                        at = begins[j] + t * chunk
                        part = keys[pl.ds(at, chunk)].reshape(chunk * width, width)
                        scores = lax.dot_general(
                            part,
                            queries[j],
                            (((1,), (1,)), ((), ())),
                            preferred_element_type=jnp.float32,
                        )
                        left = (lengths[j] - t * chunk) * width
                        if causal:
                            allowed = key_row - lane <= left - width
                        else:
                            allowed = key_row < left
                        scores = jnp.where(allowed, scores * scale, NEG)
                        top = jnp.maximum(high, jnp.max(scores, axis=0, keepdims=True))
                        shrink = jnp.exp(high - top)
                        weights = jnp.exp(scores - top)
                        total = total * shrink + jnp.sum(weights, axis=0, keepdims=True)
                        probs = weights.astype(jnp.bfloat16)
                        vals = values[pl.ds(at, chunk)]
                        acc = acc * shrink
                        for u in range(0, chunk, 2):
                            acc = acc + jnp.dot(
                                jnp.concatenate([vals[u], vals[u + 1]], axis=1),
                                probs[u * width : (u + 2) * width],
                                preferred_element_type=jnp.float32,
                            )
                        result.append((top, total, acc))
                    return tuple(result)

                zero = (
                    jnp.full((1, width), NEG, jnp.float32),
                    jnp.zeros((1, width), jnp.float32),
                    jnp.zeros((width, width), jnp.float32),
                )
                state = lax.fori_loop(0, steps, step, (zero, zero))
                for j in range(2):
                    high, total, acc = state[j]
                    b = 2 * i + j
                    some = lengths[j] > 0
                    safe = jnp.where(some, total, 1.0)
                    out_ref[pl.ds(pl.multiple_of(b * width, width), width), :] = (
                        acc / safe
                    ).astype(jnp.bfloat16)
                    logs[g, pl.ds(b, 1), :] = jnp.where(some, high + jnp.log(safe), NEG)
                return carry

            lax.fori_loop(0, per_shard // 2, pair, 0)
            rest = logs[g]
            pieces = []
            for _ in range(3):
                piece = rest.astype(jnp.bfloat16)
                rest = rest - piece.astype(jnp.float32)
                pieces.append(piece)
            pieces.append(jnp.zeros_like(pieces[0]))
            tail = jnp.concatenate([p.astype(jnp.float32) for p in pieces], axis=0)
            out_ref[per_shard * width :, :] = tail.astype(jnp.bfloat16)

    if causal:
        body()
    else:

        @pl.when(plane == 1)
        def _():
            body()


def attend(causal, ids, table, queries, key_values):
    rows, width = queries[0].shape
    per_shard = rows // width
    cluster_count = table.shape[1] // per_shard
    room = 4 * per_shard + 2 * per_shard
    groups = len(queries)
    smem = pl.BlockSpec(memory_space=pltpu.SMEM)
    vmem = pl.BlockSpec(memory_space=pltpu.VMEM)
    out = jax.ShapeDtypeStruct((rows + 4 * per_shard, width), jnp.bfloat16)
    return pl.pallas_call(
        functools.partial(attend_kernel, causal, per_shard, cluster_count),
        in_specs=[smem, smem] + [vmem] * (groups + 4),
        out_specs=[vmem] * groups,
        out_shape=[out] * groups,
        scratch_shapes=[
            pltpu.VMEM((room, width, width), jnp.bfloat16),
            pltpu.VMEM((room, width, width), jnp.bfloat16),
            pltpu.VMEM((groups, per_shard, width), jnp.float32),
            pltpu.SMEM((table.shape[1],), jnp.int32),
            pltpu.SMEM((cluster_count,), jnp.int32),
            pltpu.SMEM((cluster_count,), jnp.int32),
        ],
        name="attend_own" if causal else "attend_remote",
    )(ids, table, *queries, *key_values)


def combine_kernel(ids_ref, own_keep, own_other, near_keep, near_other, far_keep, far_other, out_ref):
    column = ids_ref[0, 0]
    plane = ids_ref[0, 1]
    width = own_keep.shape[1]
    rows = out_ref.shape[2]
    per_shard = rows // width
    for which, (own, near, far) in enumerate(
        ((own_keep, near_keep, far_keep), (own_other, near_other, far_other))
    ):
        head = column if which == 0 else 1 - column

        def log_of(ref):
            tail = ref[rows:, :].astype(jnp.float32)
            return (
                tail[:per_shard]
                + tail[per_shard : 2 * per_shard]
                + tail[2 * per_shard : 3 * per_shard]
            )

        @pl.when(plane < 2)
        def _(own=own, head=head):
            for b in range(per_shard):
                lines = slice(b * width, (b + 1) * width)
                out_ref[head, :, lines] = own[lines, :]

        def merge(own, other, head):
            own_log = log_of(own)
            other_log = log_of(other)
            top = jnp.maximum(own_log, other_log)
            own_part = jnp.exp(own_log - top)
            other_part = jnp.exp(other_log - top)
            total = own_part + other_part
            own_part = own_part / total
            other_part = other_part / total
            for b in range(per_shard):
                lines = slice(b * width, (b + 1) * width)
                mixed = (
                    own[lines, :].astype(jnp.float32) * own_part[b : b + 1]
                    + other[lines, :].astype(jnp.float32) * other_part[b : b + 1]
                )
                out_ref[head, :, lines] = mixed.astype(jnp.bfloat16)

        @pl.when(plane == 2)
        def _(own=own, near=near, head=head):
            merge(own, near, head)

        @pl.when(plane == 3)
        def _(own=own, far=far, head=head):
            merge(own, far, head)


def combine(ids, parts):
    rows, width = parts[0].shape
    per_shard = (rows * width) // (width * width + 4 * width)
    per_shard = per_shard // width
    per_shard = rows // (width + 4)
    vmem = pl.BlockSpec(memory_space=pltpu.VMEM)
    return pl.pallas_call(
        combine_kernel,
        in_specs=[pl.BlockSpec(memory_space=pltpu.SMEM)] + [vmem] * 6,
        out_specs=vmem,
        out_shape=jax.ShapeDtypeStruct((2, width, per_shard * width), jnp.bfloat16),
        name="combine",
    )(ids, *parts)


def planes_plan(qkv_heads, clusters, out_weight):
    seq_count = lax.axis_size("seq")
    head_count = lax.axis_size("head")
    shard = lax.axis_index("seq")
    group = lax.axis_index("head")
    column, plane = shard % 2, shard // 2
    tok_rows, head_local, triple = qkv_heads.shape
    width = triple // 3
    ids = jnp.stack([column, plane]).astype(jnp.int32).reshape(1, 2)

    swap = [(c, c ^ 1) for c in range(seq_count)]

    def hop(moves, cross=0):
        return [(2 * a + x, 2 * b + (x ^ cross)) for a, b in moves for x in range(2)]

    def send(value, pairs):
        return lax.ppermute(value, "seq", pairs)

    by_head = qkv_heads.transpose(1, 0, 2)
    q_keep, q_other, kv_keep, kv_other = split_heads(ids, by_head)

    q_swap = send(q_other, swap)
    kv_swap = send(kv_other, swap)
    lift = hop([(0, 1), (2, 3)])
    kv_low_keep = send(kv_keep, lift)
    q2_keep = send(q_keep, hop([(2, 1)]))
    q3_keep = send(q_keep, hop([(3, 1)]))
    q2_swap = send(q_swap, hop([(2, 1)]))
    q3_swap = send(q_swap, hop([(3, 1)]))
    kv_low_swap = send(kv_swap, lift)

    key_values = (kv_keep, kv_swap, kv_low_keep, kv_low_swap)
    r2_keep, r2_swap, r3_keep, r3_swap = attend(
        False, ids, clusters, (q2_keep, q2_swap, q3_keep, q3_swap), key_values
    )
    near_keep = send(r2_keep, hop([(1, 2)]))
    far_keep = send(r3_keep, hop([(1, 3)]))
    near_other = send(r2_swap, hop([(1, 2)], 1))
    far_other = send(r3_swap, hop([(1, 3)], 1))
    own_keep, own_swap = attend(True, ids, clusters, (q_keep, q_swap), key_values)
    own_other = send(own_swap, swap)
    local = combine(
        ids, (own_keep, own_other, near_keep, near_other, far_keep, far_other)
    ).reshape(head_local * width, tok_rows)

    half = head_count // 2

    def cross(value, flip):
        return lax.ppermute(value, "head", [(g, g ^ flip) for g in range(head_count)])

    beside = cross(local, 1)
    over = cross(local, half)
    over_beside = cross(over, 1)
    features = jnp.concatenate([local, beside, over, over_beside], axis=0)
    order = group ^ jnp.arange(head_count, dtype=jnp.int32)
    weight = jnp.take(
        out_weight.reshape(head_count, head_local * width, out_weight.shape[1]), order, axis=0
    ).reshape(out_weight.shape)
    summed = lax.dot_general(
        features, weight, (((0,), (0,)), ((), ())), preferred_element_type=jnp.float32
    )
    return summed.astype(jnp.bfloat16)


def solution(mesh):
    in_specs = (P("seq", "head", None), P("head", None), P(None, "head"))
    out_specs = P("seq", "head")
    by_planes = mesh.shape["seq"] == 8 and mesh.shape["head"] == 4
    return jax.shard_map(
        planes_plan if by_planes else routed_plan,
        mesh=mesh,
        in_specs=in_specs,
        out_specs=out_specs,
        check_vma=False,
    )
```

```python
import functools
import math

import jax
import jax.numpy as jnp
from jax import lax
from jax.experimental import pallas as pl
from jax.experimental.pallas import tpu as pltpu
from jax.sharding import PartitionSpec as P


NEG = -1e30


def softmax_rows(query_part, query_pos, key_rows, value_rows, key_pos, usable, score_scale):
    scores = jnp.dot(query_part, key_rows.T, preferred_element_type=jnp.float32) * score_scale
    allowed = usable[None, :] & (key_pos[None, :] <= query_pos[:, None])
    scores = jnp.where(allowed, scores, -1e30)
    highest = jnp.max(scores, axis=1, keepdims=True)
    weights = jnp.exp(scores - highest)
    totals = jnp.sum(weights, axis=1, keepdims=True)
    probabilities = weights.astype(jnp.bfloat16)
    attended = jnp.dot(probabilities, value_rows, preferred_element_type=jnp.float32) / totals
    return attended.astype(jnp.bfloat16)


def attend_all(queries, key_rows, value_rows, positions, usable):
    length = queries.shape[0]
    rows_step = min(512, length)
    score_scale = 1.0 / math.sqrt(queries.shape[1])
    pieces = []
    for step_index in range(length // rows_step):
        first_row = step_index * rows_step
        key_end = first_row + rows_step
        pieces.append(
            softmax_rows(
                queries[first_row : first_row + rows_step],
                positions[first_row : first_row + rows_step],
                key_rows[:key_end],
                value_rows[:key_end],
                positions[:key_end],
                usable[:key_end],
                score_scale,
            )
        )
    return jnp.concatenate(pieces, axis=0)


def slot_tables(owners, myself, pair_slots):
    source_count, item_count = owners.shape
    item_ids = jnp.arange(item_count, dtype=jnp.int32)
    before = item_ids[None, :] < item_ids[:, None]
    same_owner = owners[:, :, None] == owners[:, None, :]
    rank_within = jnp.sum((same_owner & before[None]).astype(jnp.int32), axis=2)
    own_owner = lax.dynamic_index_in_dim(owners, myself, 0, keepdims=False)
    own_rank = lax.dynamic_index_in_dim(rank_within, myself, 0, keepdims=False)
    own_slot = own_owner * pair_slots + own_rank
    slot_ids = jnp.arange(source_count * pair_slots, dtype=jnp.int32)
    slot_match = own_slot[None, :] == slot_ids[:, None]
    source_item = jnp.sum(slot_match.astype(jnp.int32) * item_ids[None, :], axis=1)
    filled = jnp.any(slot_match, axis=1)
    rank_ids = jnp.arange(pair_slots, dtype=jnp.int32)
    arriving = (owners == myself)[:, None, :] & (rank_within[:, None, :] == rank_ids[None, :, None])
    arrived_item = jnp.sum(arriving.astype(jnp.int32) * item_ids[None, None, :], axis=2).reshape(-1)
    arrived = jnp.any(arriving, axis=2).reshape(-1)
    return (own_slot, source_item, filled, arrived_item, arrived)


def routed_plan(qkv_heads, clusters, out_weight):
    seq_count = lax.axis_size("seq")
    myself = lax.axis_index("seq")
    tok_rows, head_local, triple = qkv_heads.shape
    head_width = triple // 3
    block_total = clusters.shape[1]
    per_shard = block_total // seq_count
    block_len = tok_rows // per_shard
    capacity = 2 * per_shard
    cluster_table = clusters.reshape(head_local, seq_count, per_shard)
    blocks = qkv_heads.reshape(per_shard, block_len, head_local, triple).transpose(2, 0, 1, 3)
    pair_slots = (head_local * capacity + seq_count - 1) // seq_count
    owners = cluster_table.transpose(1, 0, 2).reshape(seq_count, head_local * per_shard)
    own_slot, source_item, filled, arrived_item, arrived = slot_tables(owners, myself, pair_slots)
    flat_blocks = blocks.reshape(head_local * per_shard, block_len, triple)
    outgoing = jnp.take(flat_blocks, source_item, axis=0)
    outgoing = jnp.where(filled[:, None, None], outgoing, jnp.zeros((), outgoing.dtype))
    incoming = lax.all_to_all(outgoing, "seq", split_axis=0, concat_axis=0, tiled=True)
    slot_head = arrived_item // per_shard
    slot_source = jnp.arange(seq_count * pair_slots, dtype=jnp.int32) // pair_slots
    slot_block = slot_source * per_shard + arrived_item % per_shard
    slot_count = incoming.shape[0]
    slot_ids = jnp.arange(slot_count, dtype=jnp.int32)
    compact_ids = jnp.arange(capacity, dtype=jnp.int32)
    place_all = jnp.zeros((slot_count,), jnp.int32)
    padded_parts = []
    for head_index in range(head_local):
        belongs = arrived & (slot_head == head_index)
        belongs_int = belongs.astype(jnp.int32)
        places = jnp.cumsum(belongs_int) - belongs_int
        chosen = belongs[None, :] & (places[None, :] == compact_ids[:, None])
        chosen_int = chosen.astype(jnp.int32)
        pick_slot = jnp.sum(chosen_int * slot_ids[None, :], axis=1)
        kept_valid = jnp.any(chosen, axis=1)
        kept_ids = jnp.sum(chosen_int * slot_block[None, :], axis=1)
        gathered = jnp.take(incoming, pick_slot, axis=0).reshape(capacity * block_len, triple)
        positions = (
            kept_ids[:, None] * block_len + jnp.arange(block_len, dtype=jnp.int32)[None, :]
        ).reshape(-1)
        usable = jnp.repeat(kept_valid, block_len)
        attended = attend_all(
            gathered[:, :head_width],
            gathered[:, head_width : 2 * head_width],
            gathered[:, 2 * head_width :],
            positions,
            usable,
        )
        padded_parts.append(attended.reshape(capacity, block_len, head_width))
        padded_parts.append(jnp.zeros((1, block_len, head_width), jnp.bfloat16))
        place_all = place_all + jnp.where(belongs, places, 0)
    padded_all = jnp.concatenate(padded_parts, axis=0)
    back_index = jnp.where(arrived, slot_head * (capacity + 1) + place_all, capacity)
    outbound = jnp.take(padded_all, back_index, axis=0)
    home_slots = lax.all_to_all(outbound, "seq", split_axis=0, concat_axis=0, tiled=True)
    own_blocks = jnp.take(home_slots, own_slot, axis=0).reshape(
        head_local, per_shard, block_len, head_width
    )
    features = own_blocks.transpose(1, 2, 0, 3).reshape(tok_rows, head_local * head_width)
    summed = jnp.dot(
        lax.all_gather(features, "head", axis=1, tiled=True),
        out_weight,
        preferred_element_type=jnp.float32,
    )
    return summed.astype(jnp.bfloat16)


VMEM_BYTES = 24 * 1024 * 1024


def split_kernel(ids_ref, qkv_ref, q_keep, kv_keep, first, second, third):
    column = ids_ref[0, 0]
    plane = ids_ref[0, 1]
    rows, width = q_keep.shape

    def pieces(head):
        yield lambda: qkv_ref[head, :, :width]
        yield lambda: qkv_ref[head, :, width : 2 * width]
        yield lambda: jnp.concatenate(
            [
                qkv_ref[head, b * width : (b + 1) * width, 2 * width :].T
                for b in range(rows // width)
            ],
            axis=0,
        )

    query, key, value = pieces(column)
    q_keep[...] = query()
    kv_keep[0] = key()
    kv_keep[1] = value()
    query, key, value = pieces(1 - column)

    @pl.when(plane == 0)
    def _():
        first[...] = key()
        second[...] = value()
        third[...] = query()

    @pl.when(plane > 0)
    def _():
        first[...] = query()
        second[...] = key()
        third[...] = value()


def split_heads(ids, by_head):
    heads, rows, triple = by_head.shape
    width = triple // 3
    step = rows // 4
    one = jax.ShapeDtypeStruct((rows, width), by_head.dtype)
    two = jax.ShapeDtypeStruct((2, rows, width), by_head.dtype)
    spec = pl.BlockSpec((step, width), lambda i: (i, 0))
    return pl.pallas_call(
        split_kernel,
        grid=(rows // step,),
        in_specs=[
            pl.BlockSpec(memory_space=pltpu.SMEM),
            pl.BlockSpec((heads, step, triple), lambda i: (0, i, 0)),
        ],
        out_specs=[spec, pl.BlockSpec((2, step, width), lambda i: (0, i, 0)), spec, spec, spec],
        out_shape=[one, two, one, one, one],
        compiler_params=pltpu.CompilerParams(vmem_limit_bytes=VMEM_BYTES),
        name="split_heads",
    )(ids, by_head)


OWN, LOW, BOTH, NEAR, KEPT, SWAPPED = range(0, 18, 3)
TABLE_ROWS = 24


def tables_kernel(per_shard, cluster_count, ids_ref, table_ref, out_ref):
    column = ids_ref[0, 0]
    plane = ids_ref[0, 1]
    blocks = table_ref.shape[1]
    span = 2 * per_shard
    out_ref[...] = jnp.zeros_like(out_ref)
    labels = jnp.where(column == 0, table_ref[0:1, :], table_ref[1:2, :])
    down = lax.broadcasted_iota(jnp.int32, (blocks, blocks), 0)
    along = lax.broadcasted_iota(jnp.int32, (blocks, blocks), 1)
    wide = jnp.broadcast_to(labels, (blocks, blocks))
    tall = jnp.sum(jnp.where(down == along, wide, 0), axis=1, keepdims=True)
    before = (tall < wide) | ((tall == wide) & (down < along))
    cluster = lax.broadcasted_iota(jnp.int32, (blocks, cluster_count), 1)
    block = lax.broadcasted_iota(jnp.int32, (blocks, 1), 0)
    in_plane = block // span
    side = lax.rem(block // per_shard, 2)
    high = (in_plane == 2) | (in_plane == 3)
    for row, member in (
        (OWN, in_plane == plane),
        (LOW, in_plane == plane - 1),
        (BOTH, (in_plane == plane) | (in_plane == plane - 1)),
        (NEAR, in_plane == plane + 1),
        (KEPT, high & (side == column)),
        (SWAPPED, high & (side != column)),
    ):
        one = member.astype(jnp.int32)
        place = jnp.sum(jnp.where(before, one, 0), axis=0, keepdims=True)
        start = jnp.sum(jnp.where(tall < cluster, one, 0), axis=0, keepdims=True)
        count = jnp.sum(jnp.where(tall == cluster, one, 0), axis=0, keepdims=True)
        out_ref[row : row + 1, :blocks] = place
        out_ref[row + 1 : row + 2, :cluster_count] = start
        out_ref[row + 2 : row + 3, :cluster_count] = count


def block_tables(ids, table, per_shard):
    cluster_count = table.shape[1] // per_shard
    vmem = pl.BlockSpec(memory_space=pltpu.VMEM)
    return pl.pallas_call(
        functools.partial(tables_kernel, per_shard, cluster_count),
        in_specs=[pl.BlockSpec(memory_space=pltpu.SMEM), vmem],
        out_specs=vmem,
        out_shape=jax.ShapeDtypeStruct((TABLE_ROWS, 2 * table.shape[1]), jnp.int32),
        compiler_params=pltpu.CompilerParams(vmem_limit_bytes=VMEM_BYTES),
        name="block_tables",
    )(ids, table)


KINDS = {
    "own": (OWN, OWN, 1),
    "near": (OWN, NEAR, 1),
    "far_high": (OWN, KEPT, 1),
    "far_low": (LOW, KEPT, 1),
    "far_both": (BOTH, SWAPPED, 2),
}


def attend_kernel(kind, per_shard, cluster_count, sizes, ids_ref, tab, *refs):
    own = kind == "own"
    kv_row, q_row, _ = KINDS[kind]
    upper, lower = kind != "far_low", kind in ("far_low", "far_both")
    merging = kind == "far_low"
    q_count = 1 if own else 2
    kv_count = 4 * upper + 3 * lower
    q_refs = refs[:q_count]
    kv_refs = refs[q_count : q_count + kv_count]
    refs = refs[q_count + kv_count :]
    earlier, refs = (refs[:2], refs[2:]) if merging else ((), refs)
    out_refs = refs[:2]
    keys, values, queries, outs, logs, mine = refs[2:]
    column = ids_ref[0, 0]
    plane = ids_ref[0, 1]
    width = keys.shape[2]
    scale = 1.0 / math.sqrt(width)
    log_scale = scale / math.log(2.0)

    def body():
        used = tab[kv_row + 1, cluster_count - 1] + tab[kv_row + 2, cluster_count - 1]

        def bring(shard, key_ref, value_ref):
            for b in range(per_shard):
                to = tab[kv_row, shard * per_shard + b]
                keys[to] = key_ref[b * width : (b + 1) * width, :]
                values[to] = value_ref[b * width : (b + 1) * width, :]

        if upper:
            next_shard = 2 * plane + 1 - column
            kept, first, second, third = kv_refs[:4]
            bring(2 * plane + column, kept.at[0], kept.at[1])

            @pl.when(plane == 0)
            def _():
                bring(next_shard, first, second)

            @pl.when(plane > 0)
            def _():
                bring(next_shard, second, third)

        if lower:
            low_keep, low_first, low_second = kv_refs[-3:]
            bring(2 * plane - 2 + column, low_keep.at[0], low_keep.at[1])
            bring(2 * plane - 1 - column, low_first, low_second)

        def blank(i, carry):
            keys[used + i] = jnp.zeros(keys.shape[1:], keys.dtype)
            values[used + i] = jnp.zeros(values.shape[1:], values.dtype)
            return carry

        lax.fori_loop(0, sizes[-1], blank, 0)

        if own:
            shards = (2 * plane + column, 2 * plane + 1 - column)
        elif kind == "near":
            shards = (2 * plane + 2 + column, 2 * plane + 3 - column)
        elif kind == "far_both":
            shards = (2 * plane + 3 - column, 2 * plane + 5 - column)
        else:
            shards = (2 * plane + 2 + column, 2 * plane + 4 + column)

        def bring_query(shard, q_ref):
            for b in range(per_shard):
                to = tab[q_row, shard * per_shard + b]
                queries[to] = q_ref[b * width : (b + 1) * width, :]

        bring_query(shards[0], q_refs[0])
        if own:

            @pl.when(plane == 0)
            def _():
                bring_query(shards[1], third)

            @pl.when(plane > 0)
            def _():
                bring_query(shards[1], first)
        else:
            bring_query(shards[1], q_refs[1])

        row = lax.broadcasted_iota(jnp.int32, (width, 2 * width), 0)
        lane = lax.broadcasted_iota(jnp.int32, (width, 2 * width), 1)

        def cluster(c, carry):
            begin = tab[kv_row + 1, c]
            length = tab[kv_row + 2, c]
            q_begin = tab[q_row + 1, c]
            q_count = tab[q_row + 2, c]

            def pair(p, carry):
                at_q = q_begin + 2 * p
                blocks = jnp.minimum(2 * p + 2, length) if own else length

                def tile(most, surely):
                    query = queries[pl.ds(at_q, 2)].reshape(2 * width, width)
                    parts = []
                    for u in range(most):
                        part = lax.dot_general(
                            keys[begin + u],
                            query,
                            (((1,), (1,)), ((), ())),
                            preferred_element_type=jnp.float32,
                        )
                        if own:
                            part = jnp.where(row - lane <= (2 * p - u) * width, part, NEG)
                        elif u >= surely:
                            part = jnp.where(u < length, part, NEG)
                        parts.append(part)
                    scores = jnp.concatenate(parts, axis=0)
                    top = jnp.max(scores, axis=0, keepdims=True)
                    weights = jnp.exp2((scores - top) * log_scale)
                    total = jnp.sum(weights, axis=0, keepdims=True)
                    acc = jnp.dot(
                        jnp.concatenate([values[begin + u] for u in range(most)], axis=1),
                        weights.astype(jnp.bfloat16),
                        preferred_element_type=jnp.float32,
                    )
                    result = (acc / total).astype(outs.dtype)
                    log = top * scale + jnp.log(total)
                    for j in range(2):
                        outs[at_q + j] = result[:, j * width : (j + 1) * width]
                        logs[pl.ds(at_q + j, 1), :] = log[:, j * width : (j + 1) * width]

                for k, most in enumerate(sizes):
                    below = sizes[k - 1] if k else 0

                    @pl.when((blocks > below) & (blocks <= most))
                    def _(most=most, below=below):
                        tile(most, below + 1)

                if not own:

                    @pl.when(blocks == 0)
                    def _():
                        for j in range(2):
                            outs[at_q + j] = jnp.zeros((width, width), outs.dtype)
                            logs[pl.ds(at_q + j, 1), :] = jnp.full((1, width), NEG, jnp.float32)

                return carry

            return lax.fori_loop(0, (q_count + 1) // 2, pair, carry)

        lax.fori_loop(0, cluster_count, cluster, 0)
        for g, out_ref in enumerate(out_refs):
            for b in range(per_shard):
                mine[b : b + 1, :] = logs[pl.ds(tab[q_row, shards[g] * per_shard + b], 1), :]
            rest = mine[...]
            if merging:
                other = log_of(earlier[g], per_shard * width)
                top = jnp.maximum(rest, other)
                share, other_share = jnp.exp(rest - top), jnp.exp(other - top)
                total = share + other_share
                share, other_share = share / total, other_share / total
                rest = jnp.maximum(top + jnp.log(total), NEG)
            for b in range(per_shard):
                lines = slice(b * width, (b + 1) * width)
                block = outs[tab[q_row, shards[g] * per_shard + b]]
                if merging:
                    block = block.astype(jnp.float32) * share[b : b + 1]
                    block += earlier[g][lines, :].astype(jnp.float32) * other_share[b : b + 1]
                out_ref[lines, :] = block.astype(jnp.bfloat16)
            pieces = []
            for _ in range(3):
                piece = rest.astype(jnp.bfloat16).astype(jnp.float32)
                rest = rest - piece
                pieces.append(piece)
            pieces.append(jnp.zeros_like(rest))
            out_ref[per_shard * width :, :] = jnp.concatenate(pieces, axis=0).astype(jnp.bfloat16)

    if own:
        body()
    else:

        @pl.when(lax.rem(plane, 2) == 0 if kind == "near" else plane == 1)
        def _():
            body()


def log_of(ref, rows):
    tail = ref[rows:, :].astype(jnp.float32)
    step = tail.shape[0] // 4
    return tail[:step] + tail[step : 2 * step] + tail[2 * step : 3 * step]


def attend(kind, cluster_count, ids, tables, queries, key_values, earlier=()):
    rows, width = queries[0].shape
    per_shard = rows // width
    most = KINDS[kind][2] * (per_shard // 2)
    sizes = (most // 2, most)
    held = KINDS[kind][2] * 2 * per_shard + most
    smem = pl.BlockSpec(memory_space=pltpu.SMEM)
    vmem = pl.BlockSpec(memory_space=pltpu.VMEM)
    out = jax.ShapeDtypeStruct((per_shard * (width + 4), width), jnp.bfloat16)
    tile = (width, width)
    return pl.pallas_call(
        functools.partial(attend_kernel, kind, per_shard, cluster_count, sizes),
        in_specs=[smem, smem] + [vmem] * (len(queries) + len(key_values) + len(earlier)),
        out_specs=[vmem] * 2,
        out_shape=[out] * 2,
        scratch_shapes=[
            pltpu.VMEM((held,) + tile, jnp.bfloat16),
            pltpu.VMEM((held,) + tile, jnp.bfloat16),
            pltpu.VMEM((2 * per_shard + 2,) + tile, jnp.bfloat16),
            pltpu.VMEM((2 * per_shard + 2,) + tile, jnp.bfloat16),
            pltpu.VMEM((2 * per_shard + 8, width), jnp.float32),
            pltpu.VMEM((per_shard, width), jnp.float32),
        ],
        compiler_params=pltpu.CompilerParams(vmem_limit_bytes=VMEM_BYTES),
    )(ids, tables, *queries, *key_values, *earlier)


def combine_kernel(ids_ref, own, near, second, third, out_ref):
    plane = ids_ref[0, 1]
    width, rows = out_ref.shape
    own_log = log_of(own, rows)
    near_log = jnp.where(lax.rem(plane, 2) == 1, log_of(near, rows), NEG)
    far_log = jnp.where(plane == 3, log_of(third, rows), log_of(second, rows))
    far_log = jnp.where(plane > 1, far_log, NEG)
    top = jnp.maximum(jnp.maximum(own_log, near_log), far_log)
    own_part = jnp.exp(own_log - top)
    near_part = jnp.exp(near_log - top)
    far_part = jnp.exp(far_log - top)
    share = 1.0 / (own_part + near_part + far_part)
    own_part, near_part, far_part = own_part * share, near_part * share, far_part * share
    for b in range(rows // width):
        lines = slice(b * width, (b + 1) * width)
        far = jnp.where(plane == 3, third[lines, :], second[lines, :])
        mixed = (
            own[lines, :].astype(jnp.float32) * own_part[b : b + 1]
            + near[lines, :].astype(jnp.float32) * near_part[b : b + 1]
            + far.astype(jnp.float32) * far_part[b : b + 1]
        )
        out_ref[:, lines] = mixed.astype(jnp.bfloat16)


def combine(ids, values):
    size, width = values[-1].shape
    rows = size // (width + 4) * width
    vmem = pl.BlockSpec(memory_space=pltpu.VMEM)
    return pl.pallas_call(
        combine_kernel,
        in_specs=[pl.BlockSpec(memory_space=pltpu.SMEM)] + [vmem] * len(values),
        out_specs=vmem,
        out_shape=jax.ShapeDtypeStruct((width, rows), jnp.bfloat16),
        compiler_params=pltpu.CompilerParams(vmem_limit_bytes=VMEM_BYTES),
        name="combine",
    )(ids, *values)


def project_kernel(other, ids_ref, weight_ref, *refs):
    group = ids_ref[0, 2]
    column = ids_ref[0, 0]
    head = 1 - column if other else column
    out_ref = refs[-1]
    features = refs[:4]
    given = refs[4] if len(refs) == 6 else None
    depth, rows = features[0].shape
    lines = [pl.ds(pl.multiple_of(((group ^ j) * 2 + head) * depth, depth), depth) for j in range(4)]
    chunk = 256
    for line in range(0, rows, chunk):
        left = jnp.concatenate([f[:, line : line + chunk] for f in features], axis=0)
        for col in range(0, out_ref.shape[1], 2 * chunk):
            cols = slice(col, col + 2 * chunk)
            right = jnp.concatenate([weight_ref[at, cols] for at in lines], axis=0)
            acc = lax.dot_general(
                left, right, (((0,), (0,)), ((), ())), preferred_element_type=jnp.float32
            )
            if given is not None:
                acc = acc + given[line : line + chunk, cols]
            out_ref[line : line + chunk, cols] = acc.astype(out_ref.dtype)


def project(other, ids, weight, features, given):
    rows = features[0].shape[1]
    vmem = pl.BlockSpec(memory_space=pltpu.VMEM)
    given = [] if given is None else [given]
    last = bool(given)
    return pl.pallas_call(
        functools.partial(project_kernel, other),
        in_specs=[pl.BlockSpec(memory_space=pltpu.SMEM)] + [vmem] * (5 + len(given)),
        out_specs=vmem,
        out_shape=jax.ShapeDtypeStruct(
            (rows, weight.shape[1]), jnp.bfloat16 if last else jnp.float32
        ),
        compiler_params=pltpu.CompilerParams(vmem_limit_bytes=VMEM_BYTES),
        name="project",
    )(ids, weight, *features, *given)


def planes_plan(qkv_heads, clusters, out_weight):
    seq_count = lax.axis_size("seq")
    head_count = lax.axis_size("head")
    shard = lax.axis_index("seq")
    group = lax.axis_index("head")
    tok_rows, _, triple = qkv_heads.shape
    width = triple // 3
    ids = jnp.stack([shard % 2, shard // 2, group]).astype(jnp.int32).reshape(1, 3)

    swap = [(c, c ^ 1) for c in range(seq_count)]

    def hop(*moves, cross=0):
        return [(2 * a + x, 2 * b + (x ^ cross)) for a, b in moves for x in range(2)]

    def send(value, pairs):
        return lax.ppermute(value, "seq", pairs)

    def across(value, flip):
        return lax.ppermute(value, "head", [(g, g ^ flip) for g in range(head_count)])

    by_head = qkv_heads.transpose(1, 0, 2)
    q_keep, kv_keep, give1, give2, give3 = split_heads(ids, by_head)

    first = send(give1, swap)
    low_keep = send(kv_keep, hop((0, 1)))
    far2_keep = send(q_keep, hop((2, 1)))
    far3_keep = send(q_keep, hop((3, 1)))
    second = send(give2, swap)
    third = send(give3, swap)
    near_keep = send(q_keep, hop((1, 0), (3, 2)))
    low_first = send(first, hop((0, 1)))
    far2_swap = send(first, hop((2, 1)))
    far3_swap = send(first, hop((3, 1)))
    low_second = send(second, hop((0, 1)))
    near_swap = send(first, hop((1, 0), (3, 2)))

    per_shard = tok_rows // width
    cluster_count = clusters.shape[1] // per_shard
    tables = block_tables(ids, clusters, per_shard)

    def meet(kind, queries, key_values, earlier=()):
        return attend(kind, cluster_count, ids, tables, queries, key_values, earlier)

    plane_kv = (kv_keep, first, second, third)
    low_kv = (low_keep, low_first, low_second)
    own_keep, own_swap = meet("own", (q_keep,), plane_kv)
    own_other = send(own_swap, swap)
    started = meet("far_high", (far2_keep, far3_keep), plane_kv)
    back2_keep, back3_keep = meet("far_low", (far2_keep, far3_keep), low_kv, started)
    back3_keep = send(back3_keep, hop((1, 3)))
    back2_keep = send(back2_keep, hop((1, 2)))
    down_keep, down_swap = meet("near", (near_keep, near_swap), plane_kv)
    down_keep = send(down_keep, hop((0, 1), (2, 3)))
    down_other = send(down_swap, hop((0, 1), (2, 3), cross=1))
    back2_swap, back3_swap = meet("far_both", (far2_swap, far3_swap), plane_kv + low_kv)
    back3_other = send(back3_swap, hop((1, 3), cross=1))
    back2_other = send(back2_swap, hop((1, 2), cross=1))
    half = head_count // 2
    out = None
    for part, values in enumerate(
        (
            (own_keep, down_keep, back2_keep, back3_keep),
            (own_other, down_other, back2_other, back3_other),
        )
    ):
        local = combine(ids, values)
        over = across(local, half)
        beside = across(local, 1)
        over_beside = across(over, 1)
        out = project(part == 1, ids, out_weight, (local, beside, over, over_beside), out)
    return out


def solution(mesh):
    in_specs = (P("seq", "head", None), P("head", None), P(None, "head"))
    out_specs = P("seq", "head")
    by_planes = mesh.shape["seq"] == 8 and mesh.shape["head"] == 4
    plan = planes_plan if by_planes else routed_plan

    return jax.shard_map(plan, mesh=mesh, in_specs=in_specs, out_specs=out_specs, check_vma=False)
```

```python
import functools
import math

import jax
import jax.numpy as jnp
from jax import lax
from jax.experimental import pallas as pl
from jax.experimental.pallas import tpu as pltpu
from jax.sharding import PartitionSpec as P


NEG = -1e30


def softmax_rows(query_part, query_pos, key_rows, value_rows, key_pos, usable, score_scale):
    scores = jnp.dot(query_part, key_rows.T, preferred_element_type=jnp.float32) * score_scale
    allowed = usable[None, :] & (key_pos[None, :] <= query_pos[:, None])
    scores = jnp.where(allowed, scores, -1e30)
    highest = jnp.max(scores, axis=1, keepdims=True)
    weights = jnp.exp(scores - highest)
    totals = jnp.sum(weights, axis=1, keepdims=True)
    probabilities = weights.astype(jnp.bfloat16)
    attended = jnp.dot(probabilities, value_rows, preferred_element_type=jnp.float32) / totals
    return attended.astype(jnp.bfloat16)


def attend_all(queries, key_rows, value_rows, positions, usable):
    length = queries.shape[0]
    rows_step = min(512, length)
    score_scale = 1.0 / math.sqrt(queries.shape[1])
    pieces = []
    for step_index in range(length // rows_step):
        first_row = step_index * rows_step
        key_end = first_row + rows_step
        pieces.append(
            softmax_rows(
                queries[first_row : first_row + rows_step],
                positions[first_row : first_row + rows_step],
                key_rows[:key_end],
                value_rows[:key_end],
                positions[:key_end],
                usable[:key_end],
                score_scale,
            )
        )
    return jnp.concatenate(pieces, axis=0)


def slot_tables(owners, myself, pair_slots):
    source_count, item_count = owners.shape
    item_ids = jnp.arange(item_count, dtype=jnp.int32)
    before = item_ids[None, :] < item_ids[:, None]
    same_owner = owners[:, :, None] == owners[:, None, :]
    rank_within = jnp.sum((same_owner & before[None]).astype(jnp.int32), axis=2)
    own_owner = lax.dynamic_index_in_dim(owners, myself, 0, keepdims=False)
    own_rank = lax.dynamic_index_in_dim(rank_within, myself, 0, keepdims=False)
    own_slot = own_owner * pair_slots + own_rank
    slot_ids = jnp.arange(source_count * pair_slots, dtype=jnp.int32)
    slot_match = own_slot[None, :] == slot_ids[:, None]
    source_item = jnp.sum(slot_match.astype(jnp.int32) * item_ids[None, :], axis=1)
    filled = jnp.any(slot_match, axis=1)
    rank_ids = jnp.arange(pair_slots, dtype=jnp.int32)
    arriving = (owners == myself)[:, None, :] & (rank_within[:, None, :] == rank_ids[None, :, None])
    arrived_item = jnp.sum(arriving.astype(jnp.int32) * item_ids[None, None, :], axis=2).reshape(-1)
    arrived = jnp.any(arriving, axis=2).reshape(-1)
    return (own_slot, source_item, filled, arrived_item, arrived)


def routed_plan(qkv_heads, clusters, out_weight):
    seq_count = lax.axis_size("seq")
    myself = lax.axis_index("seq")
    tok_rows, head_local, triple = qkv_heads.shape
    head_width = triple // 3
    block_total = clusters.shape[1]
    per_shard = block_total // seq_count
    block_len = tok_rows // per_shard
    capacity = 2 * per_shard
    cluster_table = clusters.reshape(head_local, seq_count, per_shard)
    blocks = qkv_heads.reshape(per_shard, block_len, head_local, triple).transpose(2, 0, 1, 3)
    pair_slots = (head_local * capacity + seq_count - 1) // seq_count
    owners = cluster_table.transpose(1, 0, 2).reshape(seq_count, head_local * per_shard)
    own_slot, source_item, filled, arrived_item, arrived = slot_tables(owners, myself, pair_slots)
    flat_blocks = blocks.reshape(head_local * per_shard, block_len, triple)
    outgoing = jnp.take(flat_blocks, source_item, axis=0)
    outgoing = jnp.where(filled[:, None, None], outgoing, jnp.zeros((), outgoing.dtype))
    incoming = lax.all_to_all(outgoing, "seq", split_axis=0, concat_axis=0, tiled=True)
    slot_head = arrived_item // per_shard
    slot_source = jnp.arange(seq_count * pair_slots, dtype=jnp.int32) // pair_slots
    slot_block = slot_source * per_shard + arrived_item % per_shard
    slot_count = incoming.shape[0]
    slot_ids = jnp.arange(slot_count, dtype=jnp.int32)
    compact_ids = jnp.arange(capacity, dtype=jnp.int32)
    place_all = jnp.zeros((slot_count,), jnp.int32)
    padded_parts = []
    for head_index in range(head_local):
        belongs = arrived & (slot_head == head_index)
        belongs_int = belongs.astype(jnp.int32)
        places = jnp.cumsum(belongs_int) - belongs_int
        chosen = belongs[None, :] & (places[None, :] == compact_ids[:, None])
        chosen_int = chosen.astype(jnp.int32)
        pick_slot = jnp.sum(chosen_int * slot_ids[None, :], axis=1)
        kept_valid = jnp.any(chosen, axis=1)
        kept_ids = jnp.sum(chosen_int * slot_block[None, :], axis=1)
        gathered = jnp.take(incoming, pick_slot, axis=0).reshape(capacity * block_len, triple)
        positions = (
            kept_ids[:, None] * block_len + jnp.arange(block_len, dtype=jnp.int32)[None, :]
        ).reshape(-1)
        usable = jnp.repeat(kept_valid, block_len)
        attended = attend_all(
            gathered[:, :head_width],
            gathered[:, head_width : 2 * head_width],
            gathered[:, 2 * head_width :],
            positions,
            usable,
        )
        padded_parts.append(attended.reshape(capacity, block_len, head_width))
        padded_parts.append(jnp.zeros((1, block_len, head_width), jnp.bfloat16))
        place_all = place_all + jnp.where(belongs, places, 0)
    padded_all = jnp.concatenate(padded_parts, axis=0)
    back_index = jnp.where(arrived, slot_head * (capacity + 1) + place_all, capacity)
    outbound = jnp.take(padded_all, back_index, axis=0)
    home_slots = lax.all_to_all(outbound, "seq", split_axis=0, concat_axis=0, tiled=True)
    own_blocks = jnp.take(home_slots, own_slot, axis=0).reshape(
        head_local, per_shard, block_len, head_width
    )
    features = own_blocks.transpose(1, 2, 0, 3).reshape(tok_rows, head_local * head_width)
    summed = jnp.dot(
        lax.all_gather(features, "head", axis=1, tiled=True),
        out_weight,
        preferred_element_type=jnp.float32,
    )
    return summed.astype(jnp.bfloat16)


VMEM_BYTES = 24 * 1024 * 1024


def split_kernel(ids_ref, qkv_ref, q_keep, kv_keep, first, second, third):
    column = ids_ref[0, 0]
    plane = ids_ref[0, 1]
    rows, width = q_keep.shape

    def pieces(head):
        yield lambda: qkv_ref[head, :, :width]
        yield lambda: qkv_ref[head, :, width : 2 * width]
        yield lambda: jnp.concatenate(
            [
                qkv_ref[head, b * width : (b + 1) * width, 2 * width :].T
                for b in range(rows // width)
            ],
            axis=0,
        )

    query, key, value = pieces(column)
    q_keep[...] = query()
    kv_keep[0] = key()
    kv_keep[1] = value()
    query, key, value = pieces(1 - column)

    @pl.when(plane == 0)
    def _():
        first[...] = key()
        second[...] = value()
        third[...] = query()

    @pl.when(plane > 0)
    def _():
        first[...] = query()
        second[...] = key()
        third[...] = value()


def split_heads(ids, by_head):
    heads, rows, triple = by_head.shape
    width = triple // 3
    step = rows // 4
    one = jax.ShapeDtypeStruct((rows, width), by_head.dtype)
    two = jax.ShapeDtypeStruct((2, rows, width), by_head.dtype)
    spec = pl.BlockSpec((step, width), lambda i: (i, 0))
    return pl.pallas_call(
        split_kernel,
        grid=(rows // step,),
        in_specs=[
            pl.BlockSpec(memory_space=pltpu.SMEM),
            pl.BlockSpec((heads, step, triple), lambda i: (0, i, 0)),
        ],
        out_specs=[spec, pl.BlockSpec((2, step, width), lambda i: (0, i, 0)), spec, spec, spec],
        out_shape=[one, two, one, one, one],
        compiler_params=pltpu.CompilerParams(vmem_limit_bytes=VMEM_BYTES),
        name="split_heads",
    )(ids, by_head)


OWN, UPPER, REST, BOTH, NEAR, KEPT, SWAPPED = range(0, 21, 3)
TABLE_ROWS = 24


def tables_kernel(per_shard, cluster_count, ids_ref, table_ref, out_ref):
    column = ids_ref[0, 0]
    plane = ids_ref[0, 1]
    blocks = table_ref.shape[1]
    span = 2 * per_shard
    out_ref[...] = jnp.zeros_like(out_ref)
    labels = jnp.where(column == 0, table_ref[0:1, :], table_ref[1:2, :])
    down = lax.broadcasted_iota(jnp.int32, (blocks, blocks), 0)
    along = lax.broadcasted_iota(jnp.int32, (blocks, blocks), 1)
    wide = jnp.broadcast_to(labels, (blocks, blocks))
    tall = jnp.sum(jnp.where(down == along, wide, 0), axis=1, keepdims=True)
    before = (tall < wide) | ((tall == wide) & (down < along))
    cluster = lax.broadcasted_iota(jnp.int32, (blocks, cluster_count), 1)
    block = lax.broadcasted_iota(jnp.int32, (blocks, 1), 0)
    in_plane = block // span
    side = lax.rem(block // per_shard, 2)
    high = (in_plane == 2) | (in_plane == 3)
    for row, member in (
        (OWN, in_plane == plane),
        (UPPER, (in_plane == plane) | ((in_plane == plane - 1) & (side == column))),
        (REST, (in_plane == plane - 1) & (side != column)),
        (BOTH, (in_plane == plane) | (in_plane == plane - 1)),
        (NEAR, in_plane == plane + 1),
        (KEPT, high & (side == column)),
        (SWAPPED, high & (side != column)),
    ):
        one = member.astype(jnp.int32)
        place = jnp.sum(jnp.where(before, one, 0), axis=0, keepdims=True)
        start = jnp.sum(jnp.where(tall < cluster, one, 0), axis=0, keepdims=True)
        count = jnp.sum(jnp.where(tall == cluster, one, 0), axis=0, keepdims=True)
        out_ref[row : row + 1, :blocks] = place
        out_ref[row + 1 : row + 2, :cluster_count] = start
        out_ref[row + 2 : row + 3, :cluster_count] = count


def block_tables(ids, table, per_shard):
    cluster_count = table.shape[1] // per_shard
    vmem = pl.BlockSpec(memory_space=pltpu.VMEM)
    return pl.pallas_call(
        functools.partial(tables_kernel, per_shard, cluster_count),
        in_specs=[pl.BlockSpec(memory_space=pltpu.SMEM), vmem],
        out_specs=vmem,
        out_shape=jax.ShapeDtypeStruct((TABLE_ROWS, 2 * table.shape[1]), jnp.int32),
        compiler_params=pltpu.CompilerParams(vmem_limit_bytes=VMEM_BYTES),
        name="block_tables",
    )(ids, table)


KINDS = {
    "own": (OWN, OWN, 4, (1, 2, 4)),
    "near": (OWN, NEAR, 2, (1, 2)),
    "far_high": (UPPER, KEPT, 3, (1, 2, 3)),
    "far_low": (REST, KEPT, 1, (1,)),
    "far_both": (BOTH, SWAPPED, 4, (2, 4)),
}


def attend_kernel(kind, per_shard, cluster_count, sizes, ids_ref, tab, *refs):
    own = kind == "own"
    kv_row, q_row = KINDS[kind][:2]
    plane_keys = kind != "far_low"
    low_kept = kind in ("own", "far_high", "far_both")
    low_rest = kind in ("own", "far_low", "far_both")
    merging = kind == "far_low"
    q_count = 1 if own else 2
    kv_count = 4 * plane_keys + low_kept + 2 * low_rest
    q_refs = refs[:q_count]
    kv_refs = refs[q_count : q_count + kv_count]
    refs = refs[q_count + kv_count :]
    earlier, refs = (refs[:2], refs[2:]) if merging else ((), refs)
    out_refs = refs[:2]
    keys, values, queries, outs, logs, mine = refs[2:]
    column = ids_ref[0, 0]
    plane = ids_ref[0, 1]
    width = keys.shape[2]
    scale = 1.0 / math.sqrt(width)
    log_scale = scale / math.log(2.0)
    if own:
        kv_row = jnp.where(plane == 1, BOTH, OWN)

    def body():
        used = tab[kv_row + 1, cluster_count - 1] + tab[kv_row + 2, cluster_count - 1]

        def bring(shard, key_ref, value_ref):
            for b in range(per_shard):
                to = tab[kv_row, shard * per_shard + b]
                keys[to] = key_ref[b * width : (b + 1) * width, :]
                values[to] = value_ref[b * width : (b + 1) * width, :]

        if plane_keys:
            next_shard = 2 * plane + 1 - column
            kept, first, second, third = kv_refs[:4]
            bring(2 * plane + column, kept.at[0], kept.at[1])

            @pl.when(plane == 0)
            def _():
                bring(next_shard, first, second)

            @pl.when(plane > 0)
            def _():
                bring(next_shard, second, third)

        def bring_low():
            if low_kept:
                low_keep = kv_refs[4]
                bring(2 * plane - 2 + column, low_keep.at[0], low_keep.at[1])
            if low_rest:
                bring(2 * plane - 1 - column, kv_refs[-2], kv_refs[-1])

        if own:
            pl.when(plane == 1)(bring_low)
        else:
            bring_low()

        def blank(i, carry):
            keys[used + i] = jnp.zeros(keys.shape[1:], keys.dtype)
            values[used + i] = jnp.zeros(values.shape[1:], values.dtype)
            return carry

        lax.fori_loop(0, sizes[-1], blank, 0)

        if own:
            shards = (2 * plane + column, 2 * plane + 1 - column)
        elif kind == "near":
            shards = (2 * plane + 2 + column, 2 * plane + 3 - column)
        elif kind == "far_both":
            shards = (2 * plane + 3 - column, 2 * plane + 5 - column)
        else:
            shards = (2 * plane + 2 + column, 2 * plane + 4 + column)

        def bring_query(shard, q_ref):
            for b in range(per_shard):
                to = tab[q_row, shard * per_shard + b]
                queries[to] = q_ref[b * width : (b + 1) * width, :]

        bring_query(shards[0], q_refs[0])
        if own:

            @pl.when(plane == 0)
            def _():
                bring_query(shards[1], third)

            @pl.when(plane > 0)
            def _():
                bring_query(shards[1], first)
        else:
            bring_query(shards[1], q_refs[1])

        row = lax.broadcasted_iota(jnp.int32, (width, 2 * width), 0)
        lane = lax.broadcasted_iota(jnp.int32, (width, 2 * width), 1)

        def cluster(c, carry):
            begin = tab[kv_row + 1, c]
            length = tab[kv_row + 2, c]
            q_begin = tab[q_row + 1, c]
            q_count = tab[q_row + 2, c]

            def pair(p, carry):
                at_q = q_begin + 2 * p
                turn = length - q_count + 2 * p
                blocks = jnp.minimum(turn + 2, length) if own else length

                def tile(most, surely):
                    query = queries[pl.ds(at_q, 2)].reshape(2 * width, width)
                    parts = []
                    for u in range(most):
                        part = lax.dot_general(
                            keys[begin + u],
                            query,
                            (((1,), (1,)), ((), ())),
                            preferred_element_type=jnp.float32,
                        )
                        if own:
                            part = jnp.where(row - lane <= (turn - u) * width, part, NEG)
                        elif u >= surely:
                            part = jnp.where(u < length, part, NEG)
                        parts.append(part)
                    scores = jnp.concatenate(parts, axis=0)
                    top = jnp.max(scores, axis=0, keepdims=True)
                    weights = jnp.exp2((scores - top) * log_scale)
                    total = jnp.sum(weights, axis=0, keepdims=True)
                    acc = jnp.dot(
                        jnp.concatenate([values[begin + u] for u in range(most)], axis=1),
                        weights.astype(jnp.bfloat16),
                        preferred_element_type=jnp.float32,
                    )
                    result = (acc / total).astype(outs.dtype)
                    log = top * scale + jnp.log(total)
                    for j in range(2):
                        outs[at_q + j] = result[:, j * width : (j + 1) * width]
                        logs[pl.ds(at_q + j, 1), :] = log[:, j * width : (j + 1) * width]

                for k, most in enumerate(sizes):
                    below = sizes[k - 1] if k else 0

                    @pl.when((blocks > below) & (blocks <= most))
                    def _(most=most, below=below):
                        tile(most, below + 1)

                if not own:

                    @pl.when(blocks == 0)
                    def _():
                        for j in range(2):
                            outs[at_q + j] = jnp.zeros((width, width), outs.dtype)
                            logs[pl.ds(at_q + j, 1), :] = jnp.full((1, width), NEG, jnp.float32)

                return carry

            return lax.fori_loop(0, (q_count + 1) // 2, pair, carry)

        lax.fori_loop(0, cluster_count, cluster, 0)
        for g, out_ref in enumerate(out_refs):
            for b in range(per_shard):
                mine[b : b + 1, :] = logs[pl.ds(tab[q_row, shards[g] * per_shard + b], 1), :]
            rest = mine[...]
            if merging:
                other = log_of(earlier[g], per_shard * width)
                top = jnp.maximum(rest, other)
                share, other_share = jnp.exp(rest - top), jnp.exp(other - top)
                total = share + other_share
                share, other_share = share / total, other_share / total
                rest = jnp.maximum(top + jnp.log(total), NEG)
            for b in range(per_shard):
                lines = slice(b * width, (b + 1) * width)
                block = outs[tab[q_row, shards[g] * per_shard + b]]
                if merging:
                    block = block.astype(jnp.float32) * share[b : b + 1]
                    block += earlier[g][lines, :].astype(jnp.float32) * other_share[b : b + 1]
                out_ref[lines, :] = block.astype(jnp.bfloat16)
            pieces = []
            for _ in range(3):
                piece = rest.astype(jnp.bfloat16).astype(jnp.float32)
                rest = rest - piece
                pieces.append(piece)
            pieces.append(jnp.zeros_like(rest))
            out_ref[per_shard * width :, :] = jnp.concatenate(pieces, axis=0).astype(jnp.bfloat16)

    if own:
        body()
    else:

        @pl.when(plane == (2 if kind == "near" else 1))
        def _():
            body()


def log_of(ref, rows):
    tail = ref[rows:, :].astype(jnp.float32)
    step = tail.shape[0] // 4
    return tail[:step] + tail[step : 2 * step] + tail[2 * step : 3 * step]


def attend(kind, cluster_count, ids, tables, queries, key_values, earlier=()):
    rows, width = queries[0].shape
    per_shard = rows // width
    shards, quarters = KINDS[kind][2:]
    sizes = tuple(q * per_shard // 4 for q in quarters)
    held = shards * per_shard + sizes[-1]
    smem = pl.BlockSpec(memory_space=pltpu.SMEM)
    vmem = pl.BlockSpec(memory_space=pltpu.VMEM)
    out = jax.ShapeDtypeStruct((per_shard * (width + 4), width), jnp.bfloat16)
    tile = (width, width)
    return pl.pallas_call(
        functools.partial(attend_kernel, kind, per_shard, cluster_count, sizes),
        in_specs=[smem, smem] + [vmem] * (len(queries) + len(key_values) + len(earlier)),
        out_specs=[vmem] * 2,
        out_shape=[out] * 2,
        scratch_shapes=[
            pltpu.VMEM((held,) + tile, jnp.bfloat16),
            pltpu.VMEM((held,) + tile, jnp.bfloat16),
            pltpu.VMEM((2 * per_shard + 2,) + tile, jnp.bfloat16),
            pltpu.VMEM((2 * per_shard + 2,) + tile, jnp.bfloat16),
            pltpu.VMEM((2 * per_shard + 8, width), jnp.float32),
            pltpu.VMEM((per_shard, width), jnp.float32),
        ],
        compiler_params=pltpu.CompilerParams(vmem_limit_bytes=VMEM_BYTES),
    )(ids, tables, *queries, *key_values, *earlier)


def combine_kernel(ids_ref, own, near, second, third, out_ref):
    plane = ids_ref[0, 1]
    width, rows = out_ref.shape
    own_log = log_of(own, rows)
    near_log = jnp.where(plane == 3, log_of(near, rows), NEG)
    far_log = jnp.where(plane == 3, log_of(third, rows), log_of(second, rows))
    far_log = jnp.where(plane > 1, far_log, NEG)
    top = jnp.maximum(jnp.maximum(own_log, near_log), far_log)
    own_part = jnp.exp(own_log - top)
    near_part = jnp.exp(near_log - top)
    far_part = jnp.exp(far_log - top)
    share = 1.0 / (own_part + near_part + far_part)
    own_part, near_part, far_part = own_part * share, near_part * share, far_part * share
    for b in range(rows // width):
        lines = slice(b * width, (b + 1) * width)
        far = jnp.where(plane == 3, third[lines, :], second[lines, :])
        mixed = (
            own[lines, :].astype(jnp.float32) * own_part[b : b + 1]
            + near[lines, :].astype(jnp.float32) * near_part[b : b + 1]
            + far.astype(jnp.float32) * far_part[b : b + 1]
        )
        out_ref[:, lines] = mixed.astype(jnp.bfloat16)


def combine(ids, values):
    size, width = values[-1].shape
    rows = size // (width + 4) * width
    vmem = pl.BlockSpec(memory_space=pltpu.VMEM)
    return pl.pallas_call(
        combine_kernel,
        in_specs=[pl.BlockSpec(memory_space=pltpu.SMEM)] + [vmem] * len(values),
        out_specs=vmem,
        out_shape=jax.ShapeDtypeStruct((width, rows), jnp.bfloat16),
        compiler_params=pltpu.CompilerParams(vmem_limit_bytes=VMEM_BYTES),
        name="combine",
    )(ids, *values)


def project_kernel(other, ids_ref, weight_ref, *refs):
    group = ids_ref[0, 2]
    column = ids_ref[0, 0]
    head = 1 - column if other else column
    out_ref = refs[-1]
    features = refs[:4]
    given = refs[4] if len(refs) == 6 else None
    depth, rows = features[0].shape
    lines = [pl.ds(pl.multiple_of(((group ^ j) * 2 + head) * depth, depth), depth) for j in range(4)]
    chunk = 256
    for line in range(0, rows, chunk):
        left = jnp.concatenate([f[:, line : line + chunk] for f in features], axis=0)
        for col in range(0, out_ref.shape[1], 2 * chunk):
            cols = slice(col, col + 2 * chunk)
            right = jnp.concatenate([weight_ref[at, cols] for at in lines], axis=0)
            acc = lax.dot_general(
                left, right, (((0,), (0,)), ((), ())), preferred_element_type=jnp.float32
            )
            if given is not None:
                acc = acc + given[line : line + chunk, cols]
            out_ref[line : line + chunk, cols] = acc.astype(out_ref.dtype)


def project(other, ids, weight, features, given):
    rows = features[0].shape[1]
    vmem = pl.BlockSpec(memory_space=pltpu.VMEM)
    given = [] if given is None else [given]
    last = bool(given)
    return pl.pallas_call(
        functools.partial(project_kernel, other),
        in_specs=[pl.BlockSpec(memory_space=pltpu.SMEM)] + [vmem] * (5 + len(given)),
        out_specs=vmem,
        out_shape=jax.ShapeDtypeStruct(
            (rows, weight.shape[1]), jnp.bfloat16 if last else jnp.float32
        ),
        compiler_params=pltpu.CompilerParams(vmem_limit_bytes=VMEM_BYTES),
        name="project",
    )(ids, weight, *features, *given)


def planes_plan(qkv_heads, clusters, out_weight):
    seq_count = lax.axis_size("seq")
    head_count = lax.axis_size("head")
    shard = lax.axis_index("seq")
    group = lax.axis_index("head")
    tok_rows, _, triple = qkv_heads.shape
    width = triple // 3
    ids = jnp.stack([shard % 2, shard // 2, group]).astype(jnp.int32).reshape(1, 3)

    swap = [(c, c ^ 1) for c in range(seq_count)]

    def hop(*moves, cross=0):
        return [(2 * a + x, 2 * b + (x ^ cross)) for a, b in moves for x in range(2)]

    def send(value, pairs):
        return lax.ppermute(value, "seq", pairs)

    def across(value, flip):
        return lax.ppermute(value, "head", [(g, g ^ flip) for g in range(head_count)])

    by_head = qkv_heads.transpose(1, 0, 2)
    q_keep, kv_keep, give1, give2, give3 = split_heads(ids, by_head)

    first = send(give1, swap)
    low_keep = send(kv_keep, hop((0, 1)))
    far2_keep = send(q_keep, hop((2, 1)))
    far3_keep = send(q_keep, hop((3, 1)))
    second = send(give2, swap)
    third = send(give3, swap)
    near_keep = send(q_keep, hop((3, 2)))
    low_first = send(first, hop((0, 1)))
    far2_swap = send(first, hop((2, 1)))
    far3_swap = send(first, hop((3, 1)))
    low_second = send(second, hop((0, 1)))
    near_swap = send(first, hop((3, 2)))

    per_shard = tok_rows // width
    cluster_count = clusters.shape[1] // per_shard
    tables = block_tables(ids, clusters, per_shard)

    def meet(kind, queries, key_values, earlier=()):
        return attend(kind, cluster_count, ids, tables, queries, key_values, earlier)

    plane_kv = (kv_keep, first, second, third)
    started = meet("far_high", (far2_keep, far3_keep), plane_kv + (low_keep,))
    back2_keep, back3_keep = meet(
        "far_low", (far2_keep, far3_keep), (low_first, low_second), started
    )
    back3_keep = send(back3_keep, hop((1, 3)))
    back2_keep = send(back2_keep, hop((1, 2)))
    both_kv = plane_kv + (low_keep, low_first, low_second)
    back2_swap, back3_swap = meet("far_both", (far2_swap, far3_swap), both_kv)
    back3_other = send(back3_swap, hop((1, 3), cross=1))
    back2_other = send(back2_swap, hop((1, 2), cross=1))
    down_keep, down_swap = meet("near", (near_keep, near_swap), plane_kv)
    down_keep = send(down_keep, hop((2, 3)))
    down_other = send(down_swap, hop((2, 3), cross=1))
    own_keep, own_swap = meet("own", (q_keep,), both_kv)
    own_other = send(own_swap, swap)
    half = head_count // 2
    out = None
    for part, values in enumerate(
        (
            (own_keep, down_keep, back2_keep, back3_keep),
            (own_other, down_other, back2_other, back3_other),
        )
    ):
        local = combine(ids, values)
        over = across(local, half)
        beside = across(local, 1)
        over_beside = across(over, 1)
        out = project(part == 1, ids, out_weight, (local, beside, over, over_beside), out)
    return out


def solution(mesh):
    in_specs = (P("seq", "head", None), P("head", None), P(None, "head"))
    out_specs = P("seq", "head")
    by_planes = mesh.shape["seq"] == 8 and mesh.shape["head"] == 4
    plan = planes_plan if by_planes else routed_plan

    return jax.shard_map(plan, mesh=mesh, in_specs=in_specs, out_specs=out_specs, check_vma=False)
```

```python
import functools
import math

import jax
import jax.numpy as jnp
from jax import lax
from jax.experimental import pallas as pl
from jax.experimental.pallas import tpu as pltpu
from jax.sharding import PartitionSpec as P


NEG = -1e30


def softmax_rows(query_part, query_pos, key_rows, value_rows, key_pos, usable, score_scale):
    scores = jnp.dot(query_part, key_rows.T, preferred_element_type=jnp.float32) * score_scale
    allowed = usable[None, :] & (key_pos[None, :] <= query_pos[:, None])
    scores = jnp.where(allowed, scores, -1e30)
    highest = jnp.max(scores, axis=1, keepdims=True)
    weights = jnp.exp(scores - highest)
    totals = jnp.sum(weights, axis=1, keepdims=True)
    probabilities = weights.astype(jnp.bfloat16)
    attended = jnp.dot(probabilities, value_rows, preferred_element_type=jnp.float32) / totals
    return attended.astype(jnp.bfloat16)


def attend_all(queries, key_rows, value_rows, positions, usable):
    length = queries.shape[0]
    rows_step = min(512, length)
    score_scale = 1.0 / math.sqrt(queries.shape[1])
    pieces = []
    for step_index in range(length // rows_step):
        first_row = step_index * rows_step
        key_end = first_row + rows_step
        pieces.append(
            softmax_rows(
                queries[first_row : first_row + rows_step],
                positions[first_row : first_row + rows_step],
                key_rows[:key_end],
                value_rows[:key_end],
                positions[:key_end],
                usable[:key_end],
                score_scale,
            )
        )
    return jnp.concatenate(pieces, axis=0)


def slot_tables(owners, myself, pair_slots):
    source_count, item_count = owners.shape
    item_ids = jnp.arange(item_count, dtype=jnp.int32)
    before = item_ids[None, :] < item_ids[:, None]
    same_owner = owners[:, :, None] == owners[:, None, :]
    rank_within = jnp.sum((same_owner & before[None]).astype(jnp.int32), axis=2)
    own_owner = lax.dynamic_index_in_dim(owners, myself, 0, keepdims=False)
    own_rank = lax.dynamic_index_in_dim(rank_within, myself, 0, keepdims=False)
    own_slot = own_owner * pair_slots + own_rank
    slot_ids = jnp.arange(source_count * pair_slots, dtype=jnp.int32)
    slot_match = own_slot[None, :] == slot_ids[:, None]
    source_item = jnp.sum(slot_match.astype(jnp.int32) * item_ids[None, :], axis=1)
    filled = jnp.any(slot_match, axis=1)
    rank_ids = jnp.arange(pair_slots, dtype=jnp.int32)
    arriving = (owners == myself)[:, None, :] & (rank_within[:, None, :] == rank_ids[None, :, None])
    arrived_item = jnp.sum(arriving.astype(jnp.int32) * item_ids[None, None, :], axis=2).reshape(-1)
    arrived = jnp.any(arriving, axis=2).reshape(-1)
    return (own_slot, source_item, filled, arrived_item, arrived)


def routed_plan(qkv_heads, clusters, out_weight):
    seq_count = lax.axis_size("seq")
    myself = lax.axis_index("seq")
    tok_rows, head_local, triple = qkv_heads.shape
    head_width = triple // 3
    block_total = clusters.shape[1]
    per_shard = block_total // seq_count
    block_len = tok_rows // per_shard
    capacity = 2 * per_shard
    cluster_table = clusters.reshape(head_local, seq_count, per_shard)
    blocks = qkv_heads.reshape(per_shard, block_len, head_local, triple).transpose(2, 0, 1, 3)
    pair_slots = (head_local * capacity + seq_count - 1) // seq_count
    owners = cluster_table.transpose(1, 0, 2).reshape(seq_count, head_local * per_shard)
    own_slot, source_item, filled, arrived_item, arrived = slot_tables(owners, myself, pair_slots)
    flat_blocks = blocks.reshape(head_local * per_shard, block_len, triple)
    outgoing = jnp.take(flat_blocks, source_item, axis=0)
    outgoing = jnp.where(filled[:, None, None], outgoing, jnp.zeros((), outgoing.dtype))
    incoming = lax.all_to_all(outgoing, "seq", split_axis=0, concat_axis=0, tiled=True)
    slot_head = arrived_item // per_shard
    slot_source = jnp.arange(seq_count * pair_slots, dtype=jnp.int32) // pair_slots
    slot_block = slot_source * per_shard + arrived_item % per_shard
    slot_count = incoming.shape[0]
    slot_ids = jnp.arange(slot_count, dtype=jnp.int32)
    compact_ids = jnp.arange(capacity, dtype=jnp.int32)
    place_all = jnp.zeros((slot_count,), jnp.int32)
    padded_parts = []
    for head_index in range(head_local):
        belongs = arrived & (slot_head == head_index)
        belongs_int = belongs.astype(jnp.int32)
        places = jnp.cumsum(belongs_int) - belongs_int
        chosen = belongs[None, :] & (places[None, :] == compact_ids[:, None])
        chosen_int = chosen.astype(jnp.int32)
        pick_slot = jnp.sum(chosen_int * slot_ids[None, :], axis=1)
        kept_valid = jnp.any(chosen, axis=1)
        kept_ids = jnp.sum(chosen_int * slot_block[None, :], axis=1)
        gathered = jnp.take(incoming, pick_slot, axis=0).reshape(capacity * block_len, triple)
        positions = (
            kept_ids[:, None] * block_len + jnp.arange(block_len, dtype=jnp.int32)[None, :]
        ).reshape(-1)
        usable = jnp.repeat(kept_valid, block_len)
        attended = attend_all(
            gathered[:, :head_width],
            gathered[:, head_width : 2 * head_width],
            gathered[:, 2 * head_width :],
            positions,
            usable,
        )
        padded_parts.append(attended.reshape(capacity, block_len, head_width))
        padded_parts.append(jnp.zeros((1, block_len, head_width), jnp.bfloat16))
        place_all = place_all + jnp.where(belongs, places, 0)
    padded_all = jnp.concatenate(padded_parts, axis=0)
    back_index = jnp.where(arrived, slot_head * (capacity + 1) + place_all, capacity)
    outbound = jnp.take(padded_all, back_index, axis=0)
    home_slots = lax.all_to_all(outbound, "seq", split_axis=0, concat_axis=0, tiled=True)
    own_blocks = jnp.take(home_slots, own_slot, axis=0).reshape(
        head_local, per_shard, block_len, head_width
    )
    features = own_blocks.transpose(1, 2, 0, 3).reshape(tok_rows, head_local * head_width)
    summed = jnp.dot(
        lax.all_gather(features, "head", axis=1, tiled=True),
        out_weight,
        preferred_element_type=jnp.float32,
    )
    return summed.astype(jnp.bfloat16)


VMEM_BYTES = 24 * 1024 * 1024


def split_kernel(ids_ref, qkv_ref, q_keep, kv_keep, first, second, third):
    column = ids_ref[0, 0]
    plane = ids_ref[0, 1]
    rows, width = q_keep.shape

    def pieces(head):
        yield lambda: qkv_ref[head, :, :width]
        yield lambda: qkv_ref[head, :, width : 2 * width]
        yield lambda: jnp.concatenate(
            [
                qkv_ref[head, b * width : (b + 1) * width, 2 * width :].T
                for b in range(rows // width)
            ],
            axis=0,
        )

    query, key, value = pieces(column)
    q_keep[...] = query()
    kv_keep[0] = key()
    kv_keep[1] = value()
    query, key, value = pieces(1 - column)

    @pl.when(plane == 0)
    def _():
        first[...] = key()
        second[...] = value()
        third[...] = query()

    @pl.when(plane > 0)
    def _():
        first[...] = query()
        second[...] = key()
        third[...] = value()


def split_heads(ids, by_head):
    heads, rows, triple = by_head.shape
    width = triple // 3
    step = rows // 4
    one = jax.ShapeDtypeStruct((rows, width), by_head.dtype)
    two = jax.ShapeDtypeStruct((2, rows, width), by_head.dtype)
    spec = pl.BlockSpec((step, width), lambda i: (i, 0))
    return pl.pallas_call(
        split_kernel,
        grid=(rows // step,),
        in_specs=[
            pl.BlockSpec(memory_space=pltpu.SMEM),
            pl.BlockSpec((heads, step, triple), lambda i: (0, i, 0)),
        ],
        out_specs=[spec, pl.BlockSpec((2, step, width), lambda i: (0, i, 0)), spec, spec, spec],
        out_shape=[one, two, one, one, one],
        compiler_params=pltpu.CompilerParams(vmem_limit_bytes=VMEM_BYTES),
        name="split_heads",
    )(ids, by_head)


OWN, UPPER, REST, BOTH, NEAR, KEPT, SWAPPED = range(0, 21, 3)
WHERE = 21
TABLE_ROWS = 24


def tables_kernel(per_shard, cluster_count, ids_ref, table_ref, out_ref):
    column = ids_ref[0, 0]
    plane = ids_ref[0, 1]
    blocks = table_ref.shape[1]
    span = 2 * per_shard
    out_ref[...] = jnp.zeros_like(out_ref)
    slot = lax.broadcasted_iota(jnp.int32, (1, 2 * blocks), 1)
    out_ref[WHERE : WHERE + 1, :] = jnp.where(slot == 0, column, plane)
    labels = jnp.where(column == 0, table_ref[0:1, :], table_ref[1:2, :])
    down = lax.broadcasted_iota(jnp.int32, (blocks, blocks), 0)
    along = lax.broadcasted_iota(jnp.int32, (blocks, blocks), 1)
    wide = jnp.broadcast_to(labels, (blocks, blocks))
    tall = jnp.sum(jnp.where(down == along, wide, 0), axis=1, keepdims=True)
    before = (tall < wide) | ((tall == wide) & (down < along))
    cluster = lax.broadcasted_iota(jnp.int32, (blocks, cluster_count), 1)
    block = lax.broadcasted_iota(jnp.int32, (blocks, 1), 0)
    in_plane = block // span
    side = lax.rem(block // per_shard, 2)
    high = (in_plane == 2) | (in_plane == 3)
    for row, member in (
        (OWN, in_plane == plane),
        (UPPER, (in_plane == plane) | ((in_plane == plane - 1) & (side == column))),
        (REST, (in_plane == plane - 1) & (side != column)),
        (BOTH, (in_plane == plane) | (in_plane == plane - 1)),
        (NEAR, in_plane == plane + 1),
        (KEPT, high & (side == column)),
        (SWAPPED, high & (side != column)),
    ):
        one = member.astype(jnp.int32)
        place = jnp.sum(jnp.where(before, one, 0), axis=0, keepdims=True)
        start = jnp.sum(jnp.where(tall < cluster, one, 0), axis=0, keepdims=True)
        count = jnp.sum(jnp.where(tall == cluster, one, 0), axis=0, keepdims=True)
        out_ref[row : row + 1, :blocks] = place
        out_ref[row + 1 : row + 2, :cluster_count] = start
        out_ref[row + 2 : row + 3, :cluster_count] = count


def block_tables(ids, table, per_shard):
    cluster_count = table.shape[1] // per_shard
    vmem = pl.BlockSpec(memory_space=pltpu.VMEM)
    return pl.pallas_call(
        functools.partial(tables_kernel, per_shard, cluster_count),
        in_specs=[pl.BlockSpec(memory_space=pltpu.SMEM), vmem],
        out_specs=vmem,
        out_shape=jax.ShapeDtypeStruct((TABLE_ROWS, 2 * table.shape[1]), jnp.int32),
        compiler_params=pltpu.CompilerParams(vmem_limit_bytes=VMEM_BYTES),
        name="block_tables",
    )(ids, table)


KINDS = {
    "own": (OWN, OWN, 4, (1, 2, 4)),
    "near": (OWN, NEAR, 2, (1, 2)),
    "far_high": (UPPER, KEPT, 3, (1, 2, 3)),
    "far_low": (REST, KEPT, 1, (1,)),
    "far_both": (BOTH, SWAPPED, 4, (2, 4)),
}


def attend_kernel(kind, per_shard, cluster_count, sizes, tab, *refs):
    own = kind == "own"
    kv_row, q_row = KINDS[kind][:2]
    plane_keys = kind != "far_low"
    low_kept = kind in ("own", "far_high", "far_both")
    low_rest = kind in ("own", "far_low", "far_both")
    merging = kind == "far_low"
    q_count = 1 if own else 2
    kv_count = 4 * plane_keys + low_kept + 2 * low_rest
    q_refs = refs[:q_count]
    kv_refs = refs[q_count : q_count + kv_count]
    refs = refs[q_count + kv_count :]
    earlier, refs = (refs[:2], refs[2:]) if merging else ((), refs)
    out_refs = refs[:2]
    keys, values, queries, outs, logs, mine = refs[2:]
    column = tab[WHERE, 0]
    plane = tab[WHERE, 1]
    width = keys.shape[2]
    scale = 1.0 / math.sqrt(width)
    log_scale = scale / math.log(2.0)
    if own:
        kv_row = jnp.where(plane == 1, BOTH, OWN)

    def body():
        used = tab[kv_row + 1, cluster_count - 1] + tab[kv_row + 2, cluster_count - 1]

        def bring(shard, key_ref, value_ref):
            for b in range(per_shard):
                to = tab[kv_row, shard * per_shard + b]
                keys[to] = key_ref[b * width : (b + 1) * width, :]
                values[to] = value_ref[b * width : (b + 1) * width, :]

        if plane_keys:
            next_shard = 2 * plane + 1 - column
            kept, first, second, third = kv_refs[:4]
            bring(2 * plane + column, kept.at[0], kept.at[1])

            @pl.when(plane == 0)
            def _():
                bring(next_shard, first, second)

            @pl.when(plane > 0)
            def _():
                bring(next_shard, second, third)

        def bring_low():
            if low_kept:
                low_keep = kv_refs[4]
                bring(2 * plane - 2 + column, low_keep.at[0], low_keep.at[1])
            if low_rest:
                bring(2 * plane - 1 - column, kv_refs[-2], kv_refs[-1])

        if own:
            pl.when(plane == 1)(bring_low)
        else:
            bring_low()

        def blank(i, carry):
            keys[used + i] = jnp.zeros(keys.shape[1:], keys.dtype)
            values[used + i] = jnp.zeros(values.shape[1:], values.dtype)
            return carry

        lax.fori_loop(0, sizes[-1], blank, 0)

        if own:
            shards = (2 * plane + column, 2 * plane + 1 - column)
        elif kind == "near":
            shards = (2 * plane + 2 + column, 2 * plane + 3 - column)
        elif kind == "far_both":
            shards = (2 * plane + 3 - column, 2 * plane + 5 - column)
        else:
            shards = (2 * plane + 2 + column, 2 * plane + 4 + column)

        def bring_query(shard, q_ref):
            for b in range(per_shard):
                to = tab[q_row, shard * per_shard + b]
                queries[to] = q_ref[b * width : (b + 1) * width, :]

        bring_query(shards[0], q_refs[0])
        if own:

            @pl.when(plane == 0)
            def _():
                bring_query(shards[1], third)

            @pl.when(plane > 0)
            def _():
                bring_query(shards[1], first)
        else:
            bring_query(shards[1], q_refs[1])

        if own:
            ahead = lax.broadcasted_iota(jnp.int32, (width, 4 * width), 0)
            ahead -= lax.broadcasted_iota(jnp.int32, (width, 4 * width), 1)

        def cluster(c, carry):
            begin = tab[kv_row + 1, c]
            length = tab[kv_row + 2, c]
            q_begin = tab[q_row + 1, c]
            q_count = tab[q_row + 2, c]

            def tile(wide, most, below):
                query = queries[pl.ds(q_begin, wide)].reshape(wide * width, width)
                parts = []
                for u in range(most):
                    part = lax.dot_general(
                        keys[begin + u],
                        query,
                        (((1,), (1,)), ((), ())),
                        preferred_element_type=jnp.float32,
                    )
                    if own:
                        allowed = ahead[:, : wide * width] <= (length - q_count - u) * width
                        part = jnp.where(allowed, part, NEG)
                    elif u > below:
                        part = jnp.where(u < length, part, NEG)
                    parts.append(part)
                scores = jnp.concatenate(parts, axis=0)
                top = jnp.max(scores, axis=0, keepdims=True)
                weights = jnp.exp2((scores - top) * log_scale)
                total = jnp.sum(weights, axis=0, keepdims=True)
                acc = jnp.dot(
                    jnp.concatenate([values[begin + u] for u in range(most)], axis=1),
                    weights.astype(jnp.bfloat16),
                    preferred_element_type=jnp.float32,
                )
                result = (acc / total).astype(outs.dtype)
                log = top * scale + jnp.log(total)
                for j in range(wide):
                    outs[q_begin + j] = result[:, j * width : (j + 1) * width]
                    logs[pl.ds(q_begin + j, 1), :] = log[:, j * width : (j + 1) * width]

            for wide in (2, 4):
                for k, most in enumerate(sizes):
                    below = sizes[k - 1] if k else 0

                    fits = (q_count > wide - 2) & (q_count <= wide)

                    @pl.when(fits & (length > below) & (length <= most))
                    def _(wide=wide, most=most, below=below):
                        tile(wide, most, below)

            if not own:

                @pl.when(length == 0)
                def _():
                    def empty(i, carry):
                        outs[q_begin + i] = jnp.zeros((width, width), outs.dtype)
                        logs[pl.ds(q_begin + i, 1), :] = jnp.full((1, width), NEG, jnp.float32)
                        return carry

                    lax.fori_loop(0, q_count, empty, 0)

            return carry

        lax.fori_loop(0, cluster_count, cluster, 0)
        for g, out_ref in enumerate(out_refs):
            for b in range(per_shard):
                mine[b : b + 1, :] = logs[pl.ds(tab[q_row, shards[g] * per_shard + b], 1), :]
            rest = mine[...]
            if merging:
                other = log_of(earlier[g], per_shard * width)
                top = jnp.maximum(rest, other)
                share, other_share = jnp.exp(rest - top), jnp.exp(other - top)
                total = share + other_share
                share, other_share = share / total, other_share / total
                rest = jnp.maximum(top + jnp.log(total), NEG)
            for b in range(per_shard):
                lines = slice(b * width, (b + 1) * width)
                block = outs[tab[q_row, shards[g] * per_shard + b]]
                if merging:
                    block = block.astype(jnp.float32) * share[b : b + 1]
                    block += earlier[g][lines, :].astype(jnp.float32) * other_share[b : b + 1]
                out_ref[lines, :] = block.astype(jnp.bfloat16)
            pieces = []
            for _ in range(3):
                piece = rest.astype(jnp.bfloat16).astype(jnp.float32)
                rest = rest - piece
                pieces.append(piece)
            pieces.append(jnp.zeros_like(rest))
            out_ref[per_shard * width :, :] = jnp.concatenate(pieces, axis=0).astype(jnp.bfloat16)

    if own:
        body()
    else:

        @pl.when(plane == (2 if kind == "near" else 1))
        def _():
            body()


def log_of(ref, rows):
    tail = ref[rows:, :].astype(jnp.float32)
    step = tail.shape[0] // 4
    return tail[:step] + tail[step : 2 * step] + tail[2 * step : 3 * step]


def attend(kind, cluster_count, tables, queries, key_values, earlier=()):
    rows, width = queries[0].shape
    per_shard = rows // width
    shards, quarters = KINDS[kind][2:]
    sizes = tuple(q * per_shard // 4 for q in quarters)
    held = shards * per_shard + sizes[-1]
    smem = pl.BlockSpec(memory_space=pltpu.SMEM)
    vmem = pl.BlockSpec(memory_space=pltpu.VMEM)
    out = jax.ShapeDtypeStruct((per_shard * (width + 4), width), jnp.bfloat16)
    tile = (width, width)
    return pl.pallas_call(
        functools.partial(attend_kernel, kind, per_shard, cluster_count, sizes),
        in_specs=[smem] + [vmem] * (len(queries) + len(key_values) + len(earlier)),
        out_specs=[vmem] * 2,
        out_shape=[out] * 2,
        scratch_shapes=[
            pltpu.VMEM((held,) + tile, jnp.bfloat16),
            pltpu.VMEM((held,) + tile, jnp.bfloat16),
            pltpu.VMEM((2 * per_shard + 4,) + tile, jnp.bfloat16),
            pltpu.VMEM((2 * per_shard + 4,) + tile, jnp.bfloat16),
            pltpu.VMEM((2 * per_shard + 8, width), jnp.float32),
            pltpu.VMEM((per_shard, width), jnp.float32),
        ],
        compiler_params=pltpu.CompilerParams(vmem_limit_bytes=VMEM_BYTES),
    )(tables, *queries, *key_values, *earlier)


def combine_kernel(ids_ref, own, near, second, third, out_ref):
    plane = ids_ref[0, 1]
    width, rows = out_ref.shape
    own_log = log_of(own, rows)
    near_log = jnp.where(plane == 3, log_of(near, rows), NEG)
    far_log = jnp.where(plane == 3, log_of(third, rows), log_of(second, rows))
    far_log = jnp.where(plane > 1, far_log, NEG)
    top = jnp.maximum(jnp.maximum(own_log, near_log), far_log)
    own_part = jnp.exp(own_log - top)
    near_part = jnp.exp(near_log - top)
    far_part = jnp.exp(far_log - top)
    share = 1.0 / (own_part + near_part + far_part)
    own_part, near_part, far_part = own_part * share, near_part * share, far_part * share
    for b in range(rows // width):
        lines = slice(b * width, (b + 1) * width)
        far = jnp.where(plane == 3, third[lines, :], second[lines, :])
        mixed = (
            own[lines, :].astype(jnp.float32) * own_part[b : b + 1]
            + near[lines, :].astype(jnp.float32) * near_part[b : b + 1]
            + far.astype(jnp.float32) * far_part[b : b + 1]
        )
        out_ref[:, lines] = mixed.astype(jnp.bfloat16)


def combine(ids, values):
    size, width = values[-1].shape
    rows = size // (width + 4) * width
    vmem = pl.BlockSpec(memory_space=pltpu.VMEM)
    return pl.pallas_call(
        combine_kernel,
        in_specs=[pl.BlockSpec(memory_space=pltpu.SMEM)] + [vmem] * len(values),
        out_specs=vmem,
        out_shape=jax.ShapeDtypeStruct((width, rows), jnp.bfloat16),
        compiler_params=pltpu.CompilerParams(vmem_limit_bytes=VMEM_BYTES),
        name="combine",
    )(ids, *values)


def project_kernel(other, ids_ref, weight_ref, *refs):
    group = ids_ref[0, 2]
    column = ids_ref[0, 0]
    head = 1 - column if other else column
    out_ref = refs[-1]
    features = refs[:4]
    given = refs[4] if len(refs) == 6 else None
    depth, rows = features[0].shape
    lines = [pl.ds(pl.multiple_of(((group ^ j) * 2 + head) * depth, depth), depth) for j in range(4)]
    chunk = 256
    for line in range(0, rows, chunk):
        left = jnp.concatenate([f[:, line : line + chunk] for f in features], axis=0)
        for col in range(0, out_ref.shape[1], 2 * chunk):
            cols = slice(col, col + 2 * chunk)
            right = jnp.concatenate([weight_ref[at, cols] for at in lines], axis=0)
            acc = lax.dot_general(
                left, right, (((0,), (0,)), ((), ())), preferred_element_type=jnp.float32
            )
            if given is not None:
                acc = acc + given[line : line + chunk, cols]
            out_ref[line : line + chunk, cols] = acc.astype(out_ref.dtype)


def project(other, ids, weight, features, given):
    rows = features[0].shape[1]
    vmem = pl.BlockSpec(memory_space=pltpu.VMEM)
    given = [] if given is None else [given]
    last = bool(given)
    return pl.pallas_call(
        functools.partial(project_kernel, other),
        in_specs=[pl.BlockSpec(memory_space=pltpu.SMEM)] + [vmem] * (5 + len(given)),
        out_specs=vmem,
        out_shape=jax.ShapeDtypeStruct(
            (rows, weight.shape[1]), jnp.bfloat16 if last else jnp.float32
        ),
        compiler_params=pltpu.CompilerParams(vmem_limit_bytes=VMEM_BYTES),
        name="project",
    )(ids, weight, *features, *given)


def planes_plan(qkv_heads, clusters, out_weight):
    seq_count = lax.axis_size("seq")
    head_count = lax.axis_size("head")
    shard = lax.axis_index("seq")
    group = lax.axis_index("head")
    tok_rows, _, triple = qkv_heads.shape
    width = triple // 3
    ids = jnp.stack([shard % 2, shard // 2, group]).astype(jnp.int32).reshape(1, 3)

    swap = [(c, c ^ 1) for c in range(seq_count)]

    def hop(*moves, cross=0):
        return [(2 * a + x, 2 * b + (x ^ cross)) for a, b in moves for x in range(2)]

    def send(value, pairs):
        return lax.ppermute(value, "seq", pairs)

    def across(value, flip):
        return lax.ppermute(value, "head", [(g, g ^ flip) for g in range(head_count)])

    by_head = qkv_heads.transpose(1, 0, 2)
    q_keep, kv_keep, give1, give2, give3 = split_heads(ids, by_head)

    first = send(give1, swap)
    low_keep = send(kv_keep, hop((0, 1)))
    far2_keep = send(q_keep, hop((2, 1)))
    far3_keep = send(q_keep, hop((3, 1)))
    second = send(give2, swap)
    third = send(give3, swap)
    near_keep = send(q_keep, hop((3, 2)))
    low_first = send(first, hop((0, 1)))
    far2_swap = send(first, hop((2, 1)))
    far3_swap = send(first, hop((3, 1)))
    low_second = send(second, hop((0, 1)))
    near_swap = send(first, hop((3, 2)))

    per_shard = tok_rows // width
    cluster_count = clusters.shape[1] // per_shard
    tables = block_tables(ids, clusters, per_shard)

    def meet(kind, queries, key_values, earlier=()):
        return attend(kind, cluster_count, tables, queries, key_values, earlier)

    plane_kv = (kv_keep, first, second, third)
    started = meet("far_high", (far2_keep, far3_keep), plane_kv + (low_keep,))
    back2_keep, back3_keep = meet(
        "far_low", (far2_keep, far3_keep), (low_first, low_second), started
    )
    back3_keep = send(back3_keep, hop((1, 3)))
    back2_keep = send(back2_keep, hop((1, 2)))
    both_kv = plane_kv + (low_keep, low_first, low_second)
    back2_swap, back3_swap = meet("far_both", (far2_swap, far3_swap), both_kv)
    back3_other = send(back3_swap, hop((1, 3), cross=1))
    back2_other = send(back2_swap, hop((1, 2), cross=1))
    down_keep, down_swap = meet("near", (near_keep, near_swap), plane_kv)
    down_keep = send(down_keep, hop((2, 3)))
    down_other = send(down_swap, hop((2, 3), cross=1))
    own_keep, own_swap = meet("own", (q_keep,), both_kv)
    own_other = send(own_swap, swap)
    half = head_count // 2
    out = None
    for part, values in enumerate(
        (
            (own_keep, down_keep, back2_keep, back3_keep),
            (own_other, down_other, back2_other, back3_other),
        )
    ):
        local = combine(ids, values)
        over = across(local, half)
        beside = across(local, 1)
        over_beside = across(over, 1)
        out = project(part == 1, ids, out_weight, (local, beside, over, over_beside), out)
    return out


def solution(mesh):
    in_specs = (P("seq", "head", None), P("head", None), P(None, "head"))
    out_specs = P("seq", "head")
    by_planes = mesh.shape["seq"] == 8 and mesh.shape["head"] == 4
    plan = planes_plan if by_planes else routed_plan

    return jax.shard_map(plan, mesh=mesh, in_specs=in_specs, out_specs=out_specs, check_vma=False)
```

```python
import functools
import math

import jax
import jax.numpy as jnp
from jax import lax
from jax.experimental import pallas as pl
from jax.experimental.pallas import tpu as pltpu
from jax.sharding import PartitionSpec as P


NEG = -1e30


def softmax_rows(query_part, query_pos, key_rows, value_rows, key_pos, usable, score_scale):
    scores = jnp.dot(query_part, key_rows.T, preferred_element_type=jnp.float32) * score_scale
    allowed = usable[None, :] & (key_pos[None, :] <= query_pos[:, None])
    scores = jnp.where(allowed, scores, -1e30)
    highest = jnp.max(scores, axis=1, keepdims=True)
    weights = jnp.exp(scores - highest)
    totals = jnp.sum(weights, axis=1, keepdims=True)
    probabilities = weights.astype(jnp.bfloat16)
    attended = jnp.dot(probabilities, value_rows, preferred_element_type=jnp.float32) / totals
    return attended.astype(jnp.bfloat16)


def attend_all(queries, key_rows, value_rows, positions, usable):
    length = queries.shape[0]
    rows_step = min(512, length)
    score_scale = 1.0 / math.sqrt(queries.shape[1])
    pieces = []
    for step_index in range(length // rows_step):
        first_row = step_index * rows_step
        key_end = first_row + rows_step
        pieces.append(
            softmax_rows(
                queries[first_row : first_row + rows_step],
                positions[first_row : first_row + rows_step],
                key_rows[:key_end],
                value_rows[:key_end],
                positions[:key_end],
                usable[:key_end],
                score_scale,
            )
        )
    return jnp.concatenate(pieces, axis=0)


def slot_tables(owners, myself, pair_slots):
    source_count, item_count = owners.shape
    item_ids = jnp.arange(item_count, dtype=jnp.int32)
    before = item_ids[None, :] < item_ids[:, None]
    same_owner = owners[:, :, None] == owners[:, None, :]
    rank_within = jnp.sum((same_owner & before[None]).astype(jnp.int32), axis=2)
    own_owner = lax.dynamic_index_in_dim(owners, myself, 0, keepdims=False)
    own_rank = lax.dynamic_index_in_dim(rank_within, myself, 0, keepdims=False)
    own_slot = own_owner * pair_slots + own_rank
    slot_ids = jnp.arange(source_count * pair_slots, dtype=jnp.int32)
    slot_match = own_slot[None, :] == slot_ids[:, None]
    source_item = jnp.sum(slot_match.astype(jnp.int32) * item_ids[None, :], axis=1)
    filled = jnp.any(slot_match, axis=1)
    rank_ids = jnp.arange(pair_slots, dtype=jnp.int32)
    arriving = (owners == myself)[:, None, :] & (rank_within[:, None, :] == rank_ids[None, :, None])
    arrived_item = jnp.sum(arriving.astype(jnp.int32) * item_ids[None, None, :], axis=2).reshape(-1)
    arrived = jnp.any(arriving, axis=2).reshape(-1)
    return (own_slot, source_item, filled, arrived_item, arrived)


def routed_plan(qkv_heads, clusters, out_weight):
    seq_count = lax.axis_size("seq")
    myself = lax.axis_index("seq")
    tok_rows, head_local, triple = qkv_heads.shape
    head_width = triple // 3
    block_total = clusters.shape[1]
    per_shard = block_total // seq_count
    block_len = tok_rows // per_shard
    capacity = 2 * per_shard
    cluster_table = clusters.reshape(head_local, seq_count, per_shard)
    blocks = qkv_heads.reshape(per_shard, block_len, head_local, triple).transpose(2, 0, 1, 3)
    pair_slots = (head_local * capacity + seq_count - 1) // seq_count
    owners = cluster_table.transpose(1, 0, 2).reshape(seq_count, head_local * per_shard)
    own_slot, source_item, filled, arrived_item, arrived = slot_tables(owners, myself, pair_slots)
    flat_blocks = blocks.reshape(head_local * per_shard, block_len, triple)
    outgoing = jnp.take(flat_blocks, source_item, axis=0)
    outgoing = jnp.where(filled[:, None, None], outgoing, jnp.zeros((), outgoing.dtype))
    incoming = lax.all_to_all(outgoing, "seq", split_axis=0, concat_axis=0, tiled=True)
    slot_head = arrived_item // per_shard
    slot_source = jnp.arange(seq_count * pair_slots, dtype=jnp.int32) // pair_slots
    slot_block = slot_source * per_shard + arrived_item % per_shard
    slot_count = incoming.shape[0]
    slot_ids = jnp.arange(slot_count, dtype=jnp.int32)
    compact_ids = jnp.arange(capacity, dtype=jnp.int32)
    place_all = jnp.zeros((slot_count,), jnp.int32)
    padded_parts = []
    for head_index in range(head_local):
        belongs = arrived & (slot_head == head_index)
        belongs_int = belongs.astype(jnp.int32)
        places = jnp.cumsum(belongs_int) - belongs_int
        chosen = belongs[None, :] & (places[None, :] == compact_ids[:, None])
        chosen_int = chosen.astype(jnp.int32)
        pick_slot = jnp.sum(chosen_int * slot_ids[None, :], axis=1)
        kept_valid = jnp.any(chosen, axis=1)
        kept_ids = jnp.sum(chosen_int * slot_block[None, :], axis=1)
        gathered = jnp.take(incoming, pick_slot, axis=0).reshape(capacity * block_len, triple)
        positions = (
            kept_ids[:, None] * block_len + jnp.arange(block_len, dtype=jnp.int32)[None, :]
        ).reshape(-1)
        usable = jnp.repeat(kept_valid, block_len)
        attended = attend_all(
            gathered[:, :head_width],
            gathered[:, head_width : 2 * head_width],
            gathered[:, 2 * head_width :],
            positions,
            usable,
        )
        padded_parts.append(attended.reshape(capacity, block_len, head_width))
        padded_parts.append(jnp.zeros((1, block_len, head_width), jnp.bfloat16))
        place_all = place_all + jnp.where(belongs, places, 0)
    padded_all = jnp.concatenate(padded_parts, axis=0)
    back_index = jnp.where(arrived, slot_head * (capacity + 1) + place_all, capacity)
    outbound = jnp.take(padded_all, back_index, axis=0)
    home_slots = lax.all_to_all(outbound, "seq", split_axis=0, concat_axis=0, tiled=True)
    own_blocks = jnp.take(home_slots, own_slot, axis=0).reshape(
        head_local, per_shard, block_len, head_width
    )
    features = own_blocks.transpose(1, 2, 0, 3).reshape(tok_rows, head_local * head_width)
    summed = jnp.dot(
        lax.all_gather(features, "head", axis=1, tiled=True),
        out_weight,
        preferred_element_type=jnp.float32,
    )
    return summed.astype(jnp.bfloat16)


VMEM_BYTES = 24 * 1024 * 1024


def split_kernel(ids_ref, qkv_ref, q_keep, kv_keep, first, second, third):
    column = ids_ref[0, 0]
    plane = ids_ref[0, 1]
    rows, width = q_keep.shape

    def pieces(head):
        yield lambda: qkv_ref[head, :, :width]
        yield lambda: qkv_ref[head, :, width : 2 * width]
        yield lambda: jnp.concatenate(
            [
                qkv_ref[head, b * width : (b + 1) * width, 2 * width :].T
                for b in range(rows // width)
            ],
            axis=0,
        )

    query, key, value = pieces(column)
    q_keep[...] = query()
    kv_keep[0] = key()
    kv_keep[1] = value()
    query, key, value = pieces(1 - column)

    @pl.when(plane == 0)
    def _():
        first[...] = key()
        second[...] = value()
        third[...] = query()

    @pl.when(plane > 0)
    def _():
        first[...] = query()
        second[...] = key()
        third[...] = value()


def split_heads(ids, by_head):
    heads, rows, triple = by_head.shape
    width = triple // 3
    step = rows // 4
    one = jax.ShapeDtypeStruct((rows, width), by_head.dtype)
    two = jax.ShapeDtypeStruct((2, rows, width), by_head.dtype)
    spec = pl.BlockSpec((step, width), lambda i: (i, 0))
    return pl.pallas_call(
        split_kernel,
        grid=(rows // step,),
        in_specs=[
            pl.BlockSpec(memory_space=pltpu.SMEM),
            pl.BlockSpec((heads, step, triple), lambda i: (0, i, 0)),
        ],
        out_specs=[spec, pl.BlockSpec((2, step, width), lambda i: (0, i, 0)), spec, spec, spec],
        out_shape=[one, two, one, one, one],
        compiler_params=pltpu.CompilerParams(vmem_limit_bytes=VMEM_BYTES),
        name="split_heads",
    )(ids, by_head)


OWN, UPPER, REST, BOTH, NEAR, KEPT, SWAPPED = range(0, 21, 3)
WHERE = 21
TABLE_ROWS = 24


def tables_kernel(per_shard, cluster_count, ids_ref, table_ref, out_ref):
    column = ids_ref[0, 0]
    plane = ids_ref[0, 1]
    blocks = table_ref.shape[1]
    span = 2 * per_shard
    out_ref[...] = jnp.zeros_like(out_ref)
    slot = lax.broadcasted_iota(jnp.int32, (1, 2 * blocks), 1)
    out_ref[WHERE : WHERE + 1, :] = jnp.where(slot == 0, column, plane)
    labels = jnp.where(column == 0, table_ref[0:1, :], table_ref[1:2, :])
    down = lax.broadcasted_iota(jnp.int32, (blocks, blocks), 0)
    along = lax.broadcasted_iota(jnp.int32, (blocks, blocks), 1)
    wide = jnp.broadcast_to(labels, (blocks, blocks))
    tall = jnp.sum(jnp.where(down == along, wide, 0), axis=1, keepdims=True)
    before = (tall < wide) | ((tall == wide) & (down < along))
    cluster = lax.broadcasted_iota(jnp.int32, (blocks, cluster_count), 1)
    block = lax.broadcasted_iota(jnp.int32, (blocks, 1), 0)
    in_plane = block // span
    side = lax.rem(block // per_shard, 2)
    high = (in_plane == 2) | (in_plane == 3)
    for row, member in (
        (OWN, in_plane == plane),
        (UPPER, (in_plane == plane) | ((in_plane == plane - 1) & (side == column))),
        (REST, (in_plane == plane - 1) & (side != column)),
        (BOTH, (in_plane == plane) | (in_plane == plane - 1)),
        (NEAR, in_plane == plane + 1),
        (KEPT, high & (side == column)),
        (SWAPPED, high & (side != column)),
    ):
        one = member.astype(jnp.int32)
        place = jnp.sum(jnp.where(before, one, 0), axis=0, keepdims=True)
        start = jnp.sum(jnp.where(tall < cluster, one, 0), axis=0, keepdims=True)
        count = jnp.sum(jnp.where(tall == cluster, one, 0), axis=0, keepdims=True)
        out_ref[row : row + 1, :blocks] = place
        out_ref[row + 1 : row + 2, :cluster_count] = start
        out_ref[row + 2 : row + 3, :cluster_count] = count


def block_tables(ids, table, per_shard):
    cluster_count = table.shape[1] // per_shard
    vmem = pl.BlockSpec(memory_space=pltpu.VMEM)
    return pl.pallas_call(
        functools.partial(tables_kernel, per_shard, cluster_count),
        in_specs=[pl.BlockSpec(memory_space=pltpu.SMEM), vmem],
        out_specs=vmem,
        out_shape=jax.ShapeDtypeStruct((TABLE_ROWS, 2 * table.shape[1]), jnp.int32),
        compiler_params=pltpu.CompilerParams(vmem_limit_bytes=VMEM_BYTES),
        name="block_tables",
    )(ids, table)


KINDS = {
    "own": (OWN, OWN, 4, (1, 2, 4)),
    "near": (OWN, NEAR, 2, (1, 2)),
    "far_high": (UPPER, KEPT, 3, (1, 2, 3)),
    "far_low": (REST, KEPT, 1, (1,)),
    "far_both": (BOTH, SWAPPED, 4, (2, 4)),
}


def attend_kernel(kind, per_shard, cluster_count, sizes, tab, *refs):
    own = kind == "own"
    kv_row, q_row = KINDS[kind][:2]
    plane_keys = kind != "far_low"
    low_kept = kind in ("own", "far_high", "far_both")
    low_rest = kind in ("own", "far_low", "far_both")
    merging = kind == "far_low"
    q_count = 1 if own else 2
    kv_count = 4 * plane_keys + low_kept + 2 * low_rest
    q_refs = refs[:q_count]
    kv_refs = refs[q_count : q_count + kv_count]
    refs = refs[q_count + kv_count :]
    earlier, refs = (refs[:2], refs[2:]) if merging else ((), refs)
    out_refs = refs[:2]
    keys, values, queries, outs, logs, mine = refs[2:]
    column = tab[WHERE, 0]
    plane = tab[WHERE, 1]
    width = keys.shape[2]
    scale = 1.0 / math.sqrt(width)
    log_scale = scale / math.log(2.0)
    if own:
        kv_row = jnp.where(plane == 1, BOTH, OWN)

    def body():
        used = tab[kv_row + 1, cluster_count - 1] + tab[kv_row + 2, cluster_count - 1]

        def bring(shard, key_ref, value_ref):
            for b in range(per_shard):
                to = tab[kv_row, shard * per_shard + b]
                keys[to] = key_ref[b * width : (b + 1) * width, :]
                values[to] = value_ref[b * width : (b + 1) * width, :]

        if plane_keys:
            next_shard = 2 * plane + 1 - column
            kept, first, second, third = kv_refs[:4]
            bring(2 * plane + column, kept.at[0], kept.at[1])

            @pl.when(plane == 0)
            def _():
                bring(next_shard, first, second)

            @pl.when(plane > 0)
            def _():
                bring(next_shard, second, third)

        def bring_low():
            if low_kept:
                low_keep = kv_refs[4]
                bring(2 * plane - 2 + column, low_keep.at[0], low_keep.at[1])
            if low_rest:
                bring(2 * plane - 1 - column, kv_refs[-2], kv_refs[-1])

        if own:
            pl.when(plane == 1)(bring_low)
        else:
            bring_low()

        def blank(i, carry):
            keys[used + i] = jnp.zeros(keys.shape[1:], keys.dtype)
            values[used + i] = jnp.zeros(values.shape[1:], values.dtype)
            return carry

        lax.fori_loop(0, sizes[-1], blank, 0)

        if own:
            shards = (2 * plane + column, 2 * plane + 1 - column)
        elif kind == "near":
            shards = (2 * plane + 2 + column, 2 * plane + 3 - column)
        elif kind == "far_both":
            shards = (2 * plane + 3 - column, 2 * plane + 5 - column)
        else:
            shards = (2 * plane + 2 + column, 2 * plane + 4 + column)

        def bring_query(shard, q_ref):
            for b in range(per_shard):
                to = tab[q_row, shard * per_shard + b]
                queries[to] = q_ref[b * width : (b + 1) * width, :]

        bring_query(shards[0], q_refs[0])
        if own:

            @pl.when(plane == 0)
            def _():
                bring_query(shards[1], third)

            @pl.when(plane > 0)
            def _():
                bring_query(shards[1], first)
        else:
            bring_query(shards[1], q_refs[1])

        if own:
            ahead = lax.broadcasted_iota(jnp.int32, (width, 4 * width), 0)
            ahead -= lax.broadcasted_iota(jnp.int32, (width, 4 * width), 1)

        def cluster(c, carry):
            begin = tab[kv_row + 1, c]
            length = tab[kv_row + 2, c]
            q_begin = tab[q_row + 1, c]
            q_count = tab[q_row + 2, c]

            def tile(wide, most, below):
                query = queries[pl.ds(q_begin, wide)].reshape(wide * width, width)
                parts = []
                for u in range(most):
                    part = lax.dot_general(
                        keys[begin + u],
                        query,
                        (((1,), (1,)), ((), ())),
                        preferred_element_type=jnp.float32,
                    )
                    if own:
                        allowed = ahead[:, : wide * width] <= (length - q_count - u) * width
                        part = jnp.where(allowed, part, NEG)
                    elif u > below:
                        part = jnp.where(u < length, part, NEG)
                    parts.append(part)
                scores = jnp.concatenate(parts, axis=0)
                top = jnp.max(scores, axis=0, keepdims=True)
                weights = jnp.exp2((scores - top) * log_scale)
                total = jnp.sum(weights, axis=0, keepdims=True)
                acc = jnp.dot(
                    jnp.concatenate([values[begin + u] for u in range(most)], axis=1),
                    weights.astype(jnp.bfloat16),
                    preferred_element_type=jnp.float32,
                )
                result = (acc / total).astype(outs.dtype)
                log = top * scale + jnp.log(total)
                for j in range(wide):
                    outs[q_begin + j] = result[:, j * width : (j + 1) * width]
                    logs[pl.ds(q_begin + j, 1), :] = log[:, j * width : (j + 1) * width]

            for wide in (2, 4):
                for k, most in enumerate(sizes):
                    below = sizes[k - 1] if k else 0

                    fits = (q_count > wide - 2) & (q_count <= wide)

                    @pl.when(fits & (length > below) & (length <= most))
                    def _(wide=wide, most=most, below=below):
                        tile(wide, most, below)

            if not own:

                @pl.when(length == 0)
                def _():
                    def empty(i, carry):
                        outs[q_begin + i] = jnp.zeros((width, width), outs.dtype)
                        logs[pl.ds(q_begin + i, 1), :] = jnp.full((1, width), NEG, jnp.float32)
                        return carry

                    lax.fori_loop(0, q_count, empty, 0)

            return carry

        lax.fori_loop(0, cluster_count, cluster, 0)
        for g, out_ref in enumerate(out_refs):
            for b in range(per_shard):
                mine[b : b + 1, :] = logs[pl.ds(tab[q_row, shards[g] * per_shard + b], 1), :]
            rest = mine[...]
            if merging:
                other = log_of(earlier[g], per_shard * width)
                top = jnp.maximum(rest, other)
                share, other_share = jnp.exp(rest - top), jnp.exp(other - top)
                total = share + other_share
                share, other_share = share / total, other_share / total
                rest = jnp.maximum(top + jnp.log(total), NEG)
            for b in range(per_shard):
                lines = slice(b * width, (b + 1) * width)
                block = outs[tab[q_row, shards[g] * per_shard + b]]
                if merging:
                    block = block.astype(jnp.float32) * share[b : b + 1]
                    block += earlier[g][lines, :].astype(jnp.float32) * other_share[b : b + 1]
                out_ref[lines, :] = block.astype(jnp.bfloat16)
            pieces = []
            for _ in range(3):
                piece = rest.astype(jnp.bfloat16).astype(jnp.float32)
                rest = rest - piece
                pieces.append(piece)
            pieces.append(jnp.zeros_like(rest))
            out_ref[per_shard * width :, :] = jnp.concatenate(pieces, axis=0).astype(jnp.bfloat16)

    if own:
        body()
    else:

        @pl.when(plane == (2 if kind == "near" else 1))
        def _():
            body()


def log_of(ref, rows):
    tail = ref[rows:, :].astype(jnp.float32)
    step = tail.shape[0] // 4
    return tail[:step] + tail[step : 2 * step] + tail[2 * step : 3 * step]


def attend(kind, cluster_count, tables, queries, key_values, earlier=()):
    rows, width = queries[0].shape
    per_shard = rows // width
    shards, quarters = KINDS[kind][2:]
    sizes = tuple(q * per_shard // 4 for q in quarters)
    held = shards * per_shard + sizes[-1]
    smem = pl.BlockSpec(memory_space=pltpu.SMEM)
    vmem = pl.BlockSpec(memory_space=pltpu.VMEM)
    out = jax.ShapeDtypeStruct((per_shard * (width + 4), width), jnp.bfloat16)
    tile = (width, width)
    return pl.pallas_call(
        functools.partial(attend_kernel, kind, per_shard, cluster_count, sizes),
        in_specs=[smem] + [vmem] * (len(queries) + len(key_values) + len(earlier)),
        out_specs=[vmem] * 2,
        out_shape=[out] * 2,
        scratch_shapes=[
            pltpu.VMEM((held,) + tile, jnp.bfloat16),
            pltpu.VMEM((held,) + tile, jnp.bfloat16),
            pltpu.VMEM((2 * per_shard + 4,) + tile, jnp.bfloat16),
            pltpu.VMEM((2 * per_shard + 4,) + tile, jnp.bfloat16),
            pltpu.VMEM((2 * per_shard + 8, width), jnp.float32),
            pltpu.VMEM((per_shard, width), jnp.float32),
        ],
        compiler_params=pltpu.CompilerParams(vmem_limit_bytes=VMEM_BYTES),
    )(tables, *queries, *key_values, *earlier)


def combine_kernel(ids_ref, own, near, second, third, out_ref):
    plane = ids_ref[0, 1]
    width, rows = out_ref.shape
    own_log = log_of(own, rows)
    near_log = jnp.where(plane == 3, log_of(near, rows), NEG)
    far_log = jnp.where(plane == 3, log_of(third, rows), log_of(second, rows))
    far_log = jnp.where(plane > 1, far_log, NEG)
    top = jnp.maximum(jnp.maximum(own_log, near_log), far_log)
    own_part = jnp.exp(own_log - top)
    near_part = jnp.exp(near_log - top)
    far_part = jnp.exp(far_log - top)
    share = 1.0 / (own_part + near_part + far_part)
    own_part, near_part, far_part = own_part * share, near_part * share, far_part * share
    for b in range(rows // width):
        lines = slice(b * width, (b + 1) * width)
        far = jnp.where(plane == 3, third[lines, :], second[lines, :])
        mixed = (
            own[lines, :].astype(jnp.float32) * own_part[b : b + 1]
            + near[lines, :].astype(jnp.float32) * near_part[b : b + 1]
            + far.astype(jnp.float32) * far_part[b : b + 1]
        )
        out_ref[:, lines] = mixed.astype(jnp.bfloat16)


def combine(ids, values):
    size, width = values[-1].shape
    rows = size // (width + 4) * width
    vmem = pl.BlockSpec(memory_space=pltpu.VMEM)
    return pl.pallas_call(
        combine_kernel,
        in_specs=[pl.BlockSpec(memory_space=pltpu.SMEM)] + [vmem] * len(values),
        out_specs=vmem,
        out_shape=jax.ShapeDtypeStruct((width, rows), jnp.bfloat16),
        compiler_params=pltpu.CompilerParams(vmem_limit_bytes=VMEM_BYTES),
        name="combine",
    )(ids, *values)


def project_kernel(other, which, ids_ref, weight_ref, *refs):
    group = ids_ref[0, 2]
    column = ids_ref[0, 0]
    head = 1 - column if other else column
    out_ref = refs[-1]
    features = refs[: len(which)]
    given = refs[len(which)] if len(refs) > len(which) + 1 else None
    depth = features[0].shape[0]
    rows = out_ref.shape[0]
    first = pl.program_id(0) * rows
    lines = [pl.ds(pl.multiple_of(((group ^ j) * 2 + head) * depth, depth), depth) for j in which]
    here = pl.ds(pl.multiple_of(first, rows), rows)
    left = jnp.concatenate([f[:, here] for f in features], axis=0)
    chunk = 512
    for col in range(0, out_ref.shape[1], chunk):
        cols = slice(col, col + chunk)
        right = jnp.concatenate([weight_ref[at, cols] for at in lines], axis=0)
        acc = lax.dot_general(
            left, right, (((0,), (0,)), ((), ())), preferred_element_type=jnp.float32
        )
        if given is not None:
            acc = acc + given[here, cols]
        out_ref[:, cols] = acc.astype(out_ref.dtype)


def project(other, final, which, ids, weight, features, given):
    rows = features[0].shape[1]
    step = rows // 4
    vmem = pl.BlockSpec(memory_space=pltpu.VMEM)
    given = [] if given is None else [given]
    width = weight.shape[1]
    return pl.pallas_call(
        functools.partial(project_kernel, other, which),
        grid=(rows // step,),
        in_specs=[pl.BlockSpec(memory_space=pltpu.SMEM)]
        + [vmem] * (1 + len(features) + len(given)),
        out_specs=pl.BlockSpec((step, width), lambda i: (i, 0)),
        out_shape=jax.ShapeDtypeStruct((rows, width), jnp.bfloat16 if final else jnp.float32),
        compiler_params=pltpu.CompilerParams(vmem_limit_bytes=VMEM_BYTES),
        name="project",
    )(ids, weight, *features, *given)


def planes_plan(qkv_heads, clusters, out_weight):
    seq_count = lax.axis_size("seq")
    head_count = lax.axis_size("head")
    shard = lax.axis_index("seq")
    group = lax.axis_index("head")
    tok_rows, _, triple = qkv_heads.shape
    width = triple // 3
    ids = jnp.stack([shard % 2, shard // 2, group]).astype(jnp.int32).reshape(1, 3)

    swap = [(c, c ^ 1) for c in range(seq_count)]

    def hop(*moves, cross=0):
        return [(2 * a + x, 2 * b + (x ^ cross)) for a, b in moves for x in range(2)]

    def send(value, pairs):
        return lax.ppermute(value, "seq", pairs)

    def across(value, flip):
        return lax.ppermute(value, "head", [(g, g ^ flip) for g in range(head_count)])

    by_head = qkv_heads.transpose(1, 0, 2)
    q_keep, kv_keep, give1, give2, give3 = split_heads(ids, by_head)

    first = send(give1, swap)
    low_keep = send(kv_keep, hop((0, 1)))
    far2_keep = send(q_keep, hop((2, 1)))
    far3_keep = send(q_keep, hop((3, 1)))
    second = send(give2, swap)
    third = send(give3, swap)
    near_keep = send(q_keep, hop((3, 2)))
    low_first = send(first, hop((0, 1)))
    far2_swap = send(first, hop((2, 1)))
    far3_swap = send(first, hop((3, 1)))
    low_second = send(second, hop((0, 1)))
    near_swap = send(first, hop((3, 2)))

    per_shard = tok_rows // width
    cluster_count = clusters.shape[1] // per_shard
    tables = block_tables(ids, clusters, per_shard)

    def meet(kind, queries, key_values, earlier=()):
        return attend(kind, cluster_count, tables, queries, key_values, earlier)

    plane_kv = (kv_keep, first, second, third)
    started = meet("far_high", (far2_keep, far3_keep), plane_kv + (low_keep,))
    back2_keep, back3_keep = meet(
        "far_low", (far2_keep, far3_keep), (low_first, low_second), started
    )
    back3_keep = send(back3_keep, hop((1, 3)))
    back2_keep = send(back2_keep, hop((1, 2)))
    both_kv = plane_kv + (low_keep, low_first, low_second)
    back2_swap, back3_swap = meet("far_both", (far2_swap, far3_swap), both_kv)
    back3_other = send(back3_swap, hop((1, 3), cross=1))
    back2_other = send(back2_swap, hop((1, 2), cross=1))
    down_keep, down_swap = meet("near", (near_keep, near_swap), plane_kv)
    down_keep = send(down_keep, hop((2, 3)))
    down_other = send(down_swap, hop((2, 3), cross=1))
    own_keep, own_swap = meet("own", (q_keep,), both_kv)
    own_other = send(own_swap, swap)
    half = head_count // 2
    out = None
    for part, values in enumerate(
        (
            (own_keep, down_keep, back2_keep, back3_keep),
            (own_other, down_other, back2_other, back3_other),
        )
    ):
        local = combine(ids, values)
        over = across(local, half)
        beside = across(local, 1)
        over_beside = across(over, 1)
        if part == 0:
            out = project(
                False, False, (0, 1, 2, 3), ids, out_weight,
                (local, beside, over, over_beside), None,
            )
        else:
            out = project(True, False, (0, 1), ids, out_weight, (local, beside), out)
            out = project(True, True, (2, 3), ids, out_weight, (over, over_beside), out)
    return out


def solution(mesh):
    in_specs = (P("seq", "head", None), P("head", None), P(None, "head"))
    out_specs = P("seq", "head")
    by_planes = mesh.shape["seq"] == 8 and mesh.shape["head"] == 4
    plan = planes_plan if by_planes else routed_plan

    return jax.shard_map(plan, mesh=mesh, in_specs=in_specs, out_specs=out_specs, check_vma=False)
```

```python
import functools
import math

import jax
import jax.numpy as jnp
from jax import lax
from jax.experimental import pallas as pl
from jax.experimental.pallas import tpu as pltpu
from jax.sharding import PartitionSpec as P


NEG = -1e30


def softmax_rows(query_part, query_pos, key_rows, value_rows, key_pos, usable, score_scale):
    scores = jnp.dot(query_part, key_rows.T, preferred_element_type=jnp.float32) * score_scale
    allowed = usable[None, :] & (key_pos[None, :] <= query_pos[:, None])
    scores = jnp.where(allowed, scores, -1e30)
    highest = jnp.max(scores, axis=1, keepdims=True)
    weights = jnp.exp(scores - highest)
    totals = jnp.sum(weights, axis=1, keepdims=True)
    probabilities = weights.astype(jnp.bfloat16)
    attended = jnp.dot(probabilities, value_rows, preferred_element_type=jnp.float32) / totals
    return attended.astype(jnp.bfloat16)


def attend_all(queries, key_rows, value_rows, positions, usable):
    length = queries.shape[0]
    rows_step = min(512, length)
    score_scale = 1.0 / math.sqrt(queries.shape[1])
    pieces = []
    for step_index in range(length // rows_step):
        first_row = step_index * rows_step
        key_end = first_row + rows_step
        pieces.append(
            softmax_rows(
                queries[first_row : first_row + rows_step],
                positions[first_row : first_row + rows_step],
                key_rows[:key_end],
                value_rows[:key_end],
                positions[:key_end],
                usable[:key_end],
                score_scale,
            )
        )
    return jnp.concatenate(pieces, axis=0)


def slot_tables(owners, myself, pair_slots):
    source_count, item_count = owners.shape
    item_ids = jnp.arange(item_count, dtype=jnp.int32)
    before = item_ids[None, :] < item_ids[:, None]
    same_owner = owners[:, :, None] == owners[:, None, :]
    rank_within = jnp.sum((same_owner & before[None]).astype(jnp.int32), axis=2)
    own_owner = lax.dynamic_index_in_dim(owners, myself, 0, keepdims=False)
    own_rank = lax.dynamic_index_in_dim(rank_within, myself, 0, keepdims=False)
    own_slot = own_owner * pair_slots + own_rank
    slot_ids = jnp.arange(source_count * pair_slots, dtype=jnp.int32)
    slot_match = own_slot[None, :] == slot_ids[:, None]
    source_item = jnp.sum(slot_match.astype(jnp.int32) * item_ids[None, :], axis=1)
    filled = jnp.any(slot_match, axis=1)
    rank_ids = jnp.arange(pair_slots, dtype=jnp.int32)
    arriving = (owners == myself)[:, None, :] & (rank_within[:, None, :] == rank_ids[None, :, None])
    arrived_item = jnp.sum(arriving.astype(jnp.int32) * item_ids[None, None, :], axis=2).reshape(-1)
    arrived = jnp.any(arriving, axis=2).reshape(-1)
    return (own_slot, source_item, filled, arrived_item, arrived)


def routed_plan(qkv_heads, clusters, out_weight):
    seq_count = lax.axis_size("seq")
    myself = lax.axis_index("seq")
    tok_rows, head_local, triple = qkv_heads.shape
    head_width = triple // 3
    block_total = clusters.shape[1]
    per_shard = block_total // seq_count
    block_len = tok_rows // per_shard
    capacity = 2 * per_shard
    cluster_table = clusters.reshape(head_local, seq_count, per_shard)
    blocks = qkv_heads.reshape(per_shard, block_len, head_local, triple).transpose(2, 0, 1, 3)
    pair_slots = (head_local * capacity + seq_count - 1) // seq_count
    owners = cluster_table.transpose(1, 0, 2).reshape(seq_count, head_local * per_shard)
    own_slot, source_item, filled, arrived_item, arrived = slot_tables(owners, myself, pair_slots)
    flat_blocks = blocks.reshape(head_local * per_shard, block_len, triple)
    outgoing = jnp.take(flat_blocks, source_item, axis=0)
    outgoing = jnp.where(filled[:, None, None], outgoing, jnp.zeros((), outgoing.dtype))
    incoming = lax.all_to_all(outgoing, "seq", split_axis=0, concat_axis=0, tiled=True)
    slot_head = arrived_item // per_shard
    slot_source = jnp.arange(seq_count * pair_slots, dtype=jnp.int32) // pair_slots
    slot_block = slot_source * per_shard + arrived_item % per_shard
    slot_count = incoming.shape[0]
    slot_ids = jnp.arange(slot_count, dtype=jnp.int32)
    compact_ids = jnp.arange(capacity, dtype=jnp.int32)
    place_all = jnp.zeros((slot_count,), jnp.int32)
    padded_parts = []
    for head_index in range(head_local):
        belongs = arrived & (slot_head == head_index)
        belongs_int = belongs.astype(jnp.int32)
        places = jnp.cumsum(belongs_int) - belongs_int
        chosen = belongs[None, :] & (places[None, :] == compact_ids[:, None])
        chosen_int = chosen.astype(jnp.int32)
        pick_slot = jnp.sum(chosen_int * slot_ids[None, :], axis=1)
        kept_valid = jnp.any(chosen, axis=1)
        kept_ids = jnp.sum(chosen_int * slot_block[None, :], axis=1)
        gathered = jnp.take(incoming, pick_slot, axis=0).reshape(capacity * block_len, triple)
        positions = (
            kept_ids[:, None] * block_len + jnp.arange(block_len, dtype=jnp.int32)[None, :]
        ).reshape(-1)
        usable = jnp.repeat(kept_valid, block_len)
        attended = attend_all(
            gathered[:, :head_width],
            gathered[:, head_width : 2 * head_width],
            gathered[:, 2 * head_width :],
            positions,
            usable,
        )
        padded_parts.append(attended.reshape(capacity, block_len, head_width))
        padded_parts.append(jnp.zeros((1, block_len, head_width), jnp.bfloat16))
        place_all = place_all + jnp.where(belongs, places, 0)
    padded_all = jnp.concatenate(padded_parts, axis=0)
    back_index = jnp.where(arrived, slot_head * (capacity + 1) + place_all, capacity)
    outbound = jnp.take(padded_all, back_index, axis=0)
    home_slots = lax.all_to_all(outbound, "seq", split_axis=0, concat_axis=0, tiled=True)
    own_blocks = jnp.take(home_slots, own_slot, axis=0).reshape(
        head_local, per_shard, block_len, head_width
    )
    features = own_blocks.transpose(1, 2, 0, 3).reshape(tok_rows, head_local * head_width)
    summed = jnp.dot(
        lax.all_gather(features, "head", axis=1, tiled=True),
        out_weight,
        preferred_element_type=jnp.float32,
    )
    return summed.astype(jnp.bfloat16)


VMEM_BYTES = 24 * 1024 * 1024


def split_kernel(ids_ref, qkv_ref, q_keep, kv_keep, first, second, third):
    column = ids_ref[0, 0]
    plane = ids_ref[0, 1]
    rows, width = q_keep.shape

    def pieces(head):
        yield lambda: qkv_ref[head, :, :width]
        yield lambda: qkv_ref[head, :, width : 2 * width]
        yield lambda: jnp.concatenate(
            [
                qkv_ref[head, b * width : (b + 1) * width, 2 * width :].T
                for b in range(rows // width)
            ],
            axis=0,
        )

    query, key, value = pieces(column)
    q_keep[...] = query()
    kv_keep[0] = key()
    kv_keep[1] = value()
    query, key, value = pieces(1 - column)

    @pl.when(plane == 0)
    def _():
        first[...] = key()
        second[...] = value()
        third[...] = query()

    @pl.when(plane > 0)
    def _():
        first[...] = query()
        second[...] = key()
        third[...] = value()


def split_heads(ids, by_head):
    heads, rows, triple = by_head.shape
    width = triple // 3
    step = rows // 4
    one = jax.ShapeDtypeStruct((rows, width), by_head.dtype)
    two = jax.ShapeDtypeStruct((2, rows, width), by_head.dtype)
    spec = pl.BlockSpec((step, width), lambda i: (i, 0))
    return pl.pallas_call(
        split_kernel,
        grid=(rows // step,),
        in_specs=[
            pl.BlockSpec(memory_space=pltpu.SMEM),
            pl.BlockSpec((heads, step, triple), lambda i: (0, i, 0)),
        ],
        out_specs=[spec, pl.BlockSpec((2, step, width), lambda i: (0, i, 0)), spec, spec, spec],
        out_shape=[one, two, one, one, one],
        compiler_params=pltpu.CompilerParams(vmem_limit_bytes=VMEM_BYTES),
        name="split_heads",
    )(ids, by_head)


OWN, UPPER, REST, BOTH, NEAR, KEPT, SWAPPED = range(0, 21, 3)
WHERE = 21
TABLE_ROWS = 24


def tables_kernel(per_shard, cluster_count, ids_ref, table_ref, out_ref):
    column = ids_ref[0, 0]
    plane = ids_ref[0, 1]
    blocks = table_ref.shape[1]
    span = 2 * per_shard
    out_ref[...] = jnp.zeros_like(out_ref)
    slot = lax.broadcasted_iota(jnp.int32, (1, 2 * blocks), 1)
    out_ref[WHERE : WHERE + 1, :] = jnp.where(slot == 0, column, plane)
    labels = jnp.where(column == 0, table_ref[0:1, :], table_ref[1:2, :])
    down = lax.broadcasted_iota(jnp.int32, (blocks, blocks), 0)
    along = lax.broadcasted_iota(jnp.int32, (blocks, blocks), 1)
    wide = jnp.broadcast_to(labels, (blocks, blocks))
    tall = jnp.sum(jnp.where(down == along, wide, 0), axis=1, keepdims=True)
    before = (tall < wide) | ((tall == wide) & (down < along))
    cluster = lax.broadcasted_iota(jnp.int32, (blocks, cluster_count), 1)
    block = lax.broadcasted_iota(jnp.int32, (blocks, 1), 0)
    in_plane = block // span
    side = lax.rem(block // per_shard, 2)
    high = (in_plane == 2) | (in_plane == 3)
    for row, member in (
        (OWN, in_plane == plane),
        (UPPER, (in_plane == plane) | ((in_plane == plane - 1) & (side == column))),
        (REST, (in_plane == plane - 1) & (side != column)),
        (BOTH, (in_plane == plane) | (in_plane == plane - 1)),
        (NEAR, in_plane == plane + 1),
        (KEPT, high & (side == column)),
        (SWAPPED, high & (side != column)),
    ):
        one = member.astype(jnp.int32)
        place = jnp.sum(jnp.where(before, one, 0), axis=0, keepdims=True)
        start = jnp.sum(jnp.where(tall < cluster, one, 0), axis=0, keepdims=True)
        count = jnp.sum(jnp.where(tall == cluster, one, 0), axis=0, keepdims=True)
        out_ref[row : row + 1, :blocks] = place
        out_ref[row + 1 : row + 2, :cluster_count] = start
        out_ref[row + 2 : row + 3, :cluster_count] = count


def block_tables(ids, table, per_shard):
    cluster_count = table.shape[1] // per_shard
    vmem = pl.BlockSpec(memory_space=pltpu.VMEM)
    return pl.pallas_call(
        functools.partial(tables_kernel, per_shard, cluster_count),
        in_specs=[pl.BlockSpec(memory_space=pltpu.SMEM), vmem],
        out_specs=vmem,
        out_shape=jax.ShapeDtypeStruct((TABLE_ROWS, 2 * table.shape[1]), jnp.int32),
        compiler_params=pltpu.CompilerParams(vmem_limit_bytes=VMEM_BYTES),
        name="block_tables",
    )(ids, table)


KINDS = {
    "own": (OWN, OWN, 4, (1, 2, 4)),
    "near": (OWN, NEAR, 2, (1, 2)),
    "far_high": (UPPER, KEPT, 3, (1, 2, 3)),
    "far_low": (REST, KEPT, 1, (1,)),
    "far_both": (BOTH, SWAPPED, 4, (2, 4)),
}


def attend_kernel(kind, per_shard, cluster_count, sizes, tab, *refs):
    own = kind == "own"
    kv_row, q_row = KINDS[kind][:2]
    plane_keys = kind != "far_low"
    low_kept = kind in ("own", "far_high", "far_both")
    low_rest = kind in ("own", "far_low", "far_both")
    merging = kind == "far_low"
    q_count = 1 if own else 2
    kv_count = 4 * plane_keys + low_kept + 2 * low_rest
    q_refs = refs[:q_count]
    kv_refs = refs[q_count : q_count + kv_count]
    refs = refs[q_count + kv_count :]
    earlier, refs = (refs[:2], refs[2:]) if merging else ((), refs)
    out_refs = refs[:2]
    keys, values, queries, outs, logs, mine = refs[2:]
    column = tab[WHERE, 0]
    plane = tab[WHERE, 1]
    width = keys.shape[2]
    scale = 1.0 / math.sqrt(width)
    log_scale = scale / math.log(2.0)
    if own:
        kv_row = jnp.where(plane == 1, BOTH, OWN)

    def body():
        used = tab[kv_row + 1, cluster_count - 1] + tab[kv_row + 2, cluster_count - 1]

        def bring(shard, key_ref, value_ref):
            for b in range(per_shard):
                to = tab[kv_row, shard * per_shard + b]
                keys[to] = key_ref[b * width : (b + 1) * width, :]
                values[to] = value_ref[b * width : (b + 1) * width, :]

        if plane_keys:
            next_shard = 2 * plane + 1 - column
            kept, first, second, third = kv_refs[:4]
            bring(2 * plane + column, kept.at[0], kept.at[1])

            @pl.when(plane == 0)
            def _():
                bring(next_shard, first, second)

            @pl.when(plane > 0)
            def _():
                bring(next_shard, second, third)

        def bring_low():
            if low_kept:
                low_keep = kv_refs[4]
                bring(2 * plane - 2 + column, low_keep.at[0], low_keep.at[1])
            if low_rest:
                bring(2 * plane - 1 - column, kv_refs[-2], kv_refs[-1])

        if own:
            pl.when(plane == 1)(bring_low)
        else:
            bring_low()

        def blank(i, carry):
            keys[used + i] = jnp.zeros(keys.shape[1:], keys.dtype)
            values[used + i] = jnp.zeros(values.shape[1:], values.dtype)
            return carry

        lax.fori_loop(0, sizes[-1], blank, 0)

        if own:
            shards = (2 * plane + column, 2 * plane + 1 - column)
        elif kind == "near":
            shards = (2 * plane + 2 + column, 2 * plane + 3 - column)
        elif kind == "far_both":
            shards = (2 * plane + 3 - column, 2 * plane + 5 - column)
        else:
            shards = (2 * plane + 2 + column, 2 * plane + 4 + column)

        def bring_query(shard, q_ref):
            for b in range(per_shard):
                to = tab[q_row, shard * per_shard + b]
                queries[to] = q_ref[b * width : (b + 1) * width, :]

        bring_query(shards[0], q_refs[0])
        if own:

            @pl.when(plane == 0)
            def _():
                bring_query(shards[1], third)

            @pl.when(plane > 0)
            def _():
                bring_query(shards[1], first)
        else:
            bring_query(shards[1], q_refs[1])

        if own:
            ahead = lax.broadcasted_iota(jnp.int32, (width, 4 * width), 0)
            ahead -= lax.broadcasted_iota(jnp.int32, (width, 4 * width), 1)

        def cluster(c, carry):
            begin = tab[kv_row + 1, c]
            length = tab[kv_row + 2, c]
            q_begin = tab[q_row + 1, c]
            q_count = tab[q_row + 2, c]

            def tile(wide, most, below):
                query = queries[pl.ds(q_begin, wide)].reshape(wide * width, width)
                parts = []
                for u in range(most):
                    part = lax.dot_general(
                        keys[begin + u],
                        query,
                        (((1,), (1,)), ((), ())),
                        preferred_element_type=jnp.float32,
                    )
                    if own:
                        allowed = ahead[:, : wide * width] <= (length - q_count - u) * width
                        part = jnp.where(allowed, part, NEG)
                    elif u > below:
                        part = jnp.where(u < length, part, NEG)
                    parts.append(part)
                scores = jnp.concatenate(parts, axis=0)
                top = jnp.max(scores, axis=0, keepdims=True)
                weights = jnp.exp2((scores - top) * log_scale)
                total = jnp.sum(weights, axis=0, keepdims=True)
                acc = jnp.dot(
                    jnp.concatenate([values[begin + u] for u in range(most)], axis=1),
                    weights.astype(jnp.bfloat16),
                    preferred_element_type=jnp.float32,
                )
                result = (acc / total).astype(outs.dtype)
                log = top * scale + jnp.log(total)
                for j in range(wide):
                    outs[q_begin + j] = result[:, j * width : (j + 1) * width]
                    logs[pl.ds(q_begin + j, 1), :] = log[:, j * width : (j + 1) * width]

            for wide in (2, 4):
                for k, most in enumerate(sizes):
                    below = sizes[k - 1] if k else 0

                    fits = (q_count > wide - 2) & (q_count <= wide)

                    @pl.when(fits & (length > below) & (length <= most))
                    def _(wide=wide, most=most, below=below):
                        tile(wide, most, below)

            if not own:

                @pl.when(length == 0)
                def _():
                    def empty(i, carry):
                        outs[q_begin + i] = jnp.zeros((width, width), outs.dtype)
                        logs[pl.ds(q_begin + i, 1), :] = jnp.full((1, width), NEG, jnp.float32)
                        return carry

                    lax.fori_loop(0, q_count, empty, 0)

            return carry

        lax.fori_loop(0, cluster_count, cluster, 0)
        for g, out_ref in enumerate(out_refs):
            for b in range(per_shard):
                mine[b : b + 1, :] = logs[pl.ds(tab[q_row, shards[g] * per_shard + b], 1), :]
            rest = mine[...]
            if merging:
                other = log_of(earlier[g], per_shard * width)
                top = jnp.maximum(rest, other)
                share, other_share = jnp.exp(rest - top), jnp.exp(other - top)
                total = share + other_share
                share, other_share = share / total, other_share / total
                rest = jnp.maximum(top + jnp.log(total), NEG)
            for b in range(per_shard):
                lines = slice(b * width, (b + 1) * width)
                block = outs[tab[q_row, shards[g] * per_shard + b]]
                if merging:
                    block = block.astype(jnp.float32) * share[b : b + 1]
                    block += earlier[g][lines, :].astype(jnp.float32) * other_share[b : b + 1]
                out_ref[lines, :] = block.astype(jnp.bfloat16)
            pieces = []
            for _ in range(3):
                piece = rest.astype(jnp.bfloat16).astype(jnp.float32)
                rest = rest - piece
                pieces.append(piece)
            pieces.append(jnp.zeros_like(rest))
            out_ref[per_shard * width :, :] = jnp.concatenate(pieces, axis=0).astype(jnp.bfloat16)

    if own:
        body()
    else:

        @pl.when(plane == (2 if kind == "near" else 1))
        def _():
            body()


def log_of(ref, rows):
    tail = ref[rows:, :].astype(jnp.float32)
    step = tail.shape[0] // 4
    return tail[:step] + tail[step : 2 * step] + tail[2 * step : 3 * step]


def attend(kind, cluster_count, tables, queries, key_values, earlier=()):
    rows, width = queries[0].shape
    per_shard = rows // width
    shards, quarters = KINDS[kind][2:]
    sizes = tuple(q * per_shard // 4 for q in quarters)
    held = shards * per_shard + sizes[-1]
    smem = pl.BlockSpec(memory_space=pltpu.SMEM)
    vmem = pl.BlockSpec(memory_space=pltpu.VMEM)
    out = jax.ShapeDtypeStruct((per_shard * (width + 4), width), jnp.bfloat16)
    tile = (width, width)
    return pl.pallas_call(
        functools.partial(attend_kernel, kind, per_shard, cluster_count, sizes),
        in_specs=[smem] + [vmem] * (len(queries) + len(key_values) + len(earlier)),
        out_specs=[vmem] * 2,
        out_shape=[out] * 2,
        scratch_shapes=[
            pltpu.VMEM((held,) + tile, jnp.bfloat16),
            pltpu.VMEM((held,) + tile, jnp.bfloat16),
            pltpu.VMEM((2 * per_shard + 4,) + tile, jnp.bfloat16),
            pltpu.VMEM((2 * per_shard + 4,) + tile, jnp.bfloat16),
            pltpu.VMEM((2 * per_shard + 8, width), jnp.float32),
            pltpu.VMEM((per_shard, width), jnp.float32),
        ],
        compiler_params=pltpu.CompilerParams(vmem_limit_bytes=VMEM_BYTES),
    )(tables, *queries, *key_values, *earlier)


def combine_kernel(ids_ref, own, near, second, third, out_ref):
    plane = ids_ref[0, 1]
    rows, width = out_ref.shape
    own_log = log_of(own, rows)
    near_log = jnp.where(plane == 3, log_of(near, rows), NEG)
    far_log = jnp.where(plane == 3, log_of(third, rows), log_of(second, rows))
    far_log = jnp.where(plane > 1, far_log, NEG)
    top = jnp.maximum(jnp.maximum(own_log, near_log), far_log)
    own_part = jnp.exp(own_log - top)
    near_part = jnp.exp(near_log - top)
    far_part = jnp.exp(far_log - top)
    share = 1.0 / (own_part + near_part + far_part)
    own_part, near_part, far_part = own_part * share, near_part * share, far_part * share
    for b in range(rows // width):
        lines = slice(b * width, (b + 1) * width)
        far = jnp.where(plane == 3, third[lines, :], second[lines, :])
        mixed = (
            own[lines, :].astype(jnp.float32) * own_part[b : b + 1]
            + near[lines, :].astype(jnp.float32) * near_part[b : b + 1]
            + far.astype(jnp.float32) * far_part[b : b + 1]
        )
        out_ref[lines, :] = mixed.T.astype(jnp.bfloat16)


def combine(ids, values):
    size, width = values[-1].shape
    rows = size // (width + 4) * width
    vmem = pl.BlockSpec(memory_space=pltpu.VMEM)
    return pl.pallas_call(
        combine_kernel,
        in_specs=[pl.BlockSpec(memory_space=pltpu.SMEM)] + [vmem] * len(values),
        out_specs=vmem,
        out_shape=jax.ShapeDtypeStruct((rows, width), jnp.bfloat16),
        compiler_params=pltpu.CompilerParams(vmem_limit_bytes=VMEM_BYTES),
        name="combine",
    )(ids, *values)


def project_kernel(other, which, ids_ref, weight_ref, *refs):
    group = ids_ref[0, 2]
    column = ids_ref[0, 0]
    head = 1 - column if other else column
    out_ref = refs[-1]
    features = refs[: len(which)]
    given = refs[len(which)] if len(refs) > len(which) + 1 else None
    depth = features[0].shape[1]
    cols = out_ref.shape[1]
    here = pl.ds(pl.multiple_of(pl.program_id(0) * cols, cols), cols)
    lines = [pl.ds(pl.multiple_of(((group ^ j) * 2 + head) * depth, depth), depth) for j in which]
    right = jnp.concatenate([weight_ref[at, here] for at in lines], axis=0)
    chunk = 512
    for start in range(0, out_ref.shape[0], chunk):
        rows = slice(start, start + chunk)
        left = jnp.concatenate([f[rows, :] for f in features], axis=1)
        acc = jnp.dot(left, right, preferred_element_type=jnp.float32)
        if given is not None:
            acc = acc + given[rows, here]
        out_ref[rows, :] = acc.astype(out_ref.dtype)


def project(other, final, which, ids, weight, features, given):
    rows = features[0].shape[0]
    vmem = pl.BlockSpec(memory_space=pltpu.VMEM)
    given = [] if given is None else [given]
    width = weight.shape[1]
    step = width // 4
    return pl.pallas_call(
        functools.partial(project_kernel, other, which),
        grid=(width // step,),
        in_specs=[pl.BlockSpec(memory_space=pltpu.SMEM)]
        + [vmem] * (1 + len(features) + len(given)),
        out_specs=pl.BlockSpec((rows, step), lambda i: (0, i)),
        out_shape=jax.ShapeDtypeStruct((rows, width), jnp.bfloat16 if final else jnp.float32),
        compiler_params=pltpu.CompilerParams(vmem_limit_bytes=VMEM_BYTES),
        name="project",
    )(ids, weight, *features, *given)


def planes_plan(qkv_heads, clusters, out_weight):
    seq_count = lax.axis_size("seq")
    head_count = lax.axis_size("head")
    shard = lax.axis_index("seq")
    group = lax.axis_index("head")
    tok_rows, _, triple = qkv_heads.shape
    width = triple // 3
    ids = jnp.stack([shard % 2, shard // 2, group]).astype(jnp.int32).reshape(1, 3)

    swap = [(c, c ^ 1) for c in range(seq_count)]

    def hop(*moves, cross=0):
        return [(2 * a + x, 2 * b + (x ^ cross)) for a, b in moves for x in range(2)]

    def send(value, pairs):
        return lax.ppermute(value, "seq", pairs)

    def across(value, flip):
        return lax.ppermute(value, "head", [(g, g ^ flip) for g in range(head_count)])

    by_head = qkv_heads.transpose(1, 0, 2)
    q_keep, kv_keep, give1, give2, give3 = split_heads(ids, by_head)

    first = send(give1, swap)
    low_keep = send(kv_keep, hop((0, 1)))
    far2_keep = send(q_keep, hop((2, 1)))
    far3_keep = send(q_keep, hop((3, 1)))
    second = send(give2, swap)
    third = send(give3, swap)
    near_keep = send(q_keep, hop((3, 2)))
    low_first = send(first, hop((0, 1)))
    far2_swap = send(first, hop((2, 1)))
    far3_swap = send(first, hop((3, 1)))
    low_second = send(second, hop((0, 1)))
    near_swap = send(first, hop((3, 2)))

    per_shard = tok_rows // width
    cluster_count = clusters.shape[1] // per_shard
    tables = block_tables(ids, clusters, per_shard)

    def meet(kind, queries, key_values, earlier=()):
        return attend(kind, cluster_count, tables, queries, key_values, earlier)

    plane_kv = (kv_keep, first, second, third)
    started = meet("far_high", (far2_keep, far3_keep), plane_kv + (low_keep,))
    back2_keep, back3_keep = meet(
        "far_low", (far2_keep, far3_keep), (low_first, low_second), started
    )
    back3_keep = send(back3_keep, hop((1, 3)))
    back2_keep = send(back2_keep, hop((1, 2)))
    both_kv = plane_kv + (low_keep, low_first, low_second)
    down_keep, down_swap = meet("near", (near_keep, near_swap), plane_kv)
    down_keep = send(down_keep, hop((2, 3)))
    back2_swap, back3_swap = meet("far_both", (far2_swap, far3_swap), both_kv)
    back3_other = send(back3_swap, hop((1, 3), cross=1))
    back2_other = send(back2_swap, hop((1, 2), cross=1))
    down_other = send(down_swap, hop((2, 3), cross=1))
    own_keep, own_swap = meet("own", (q_keep,), both_kv)
    own_other = send(own_swap, swap)
    half = head_count // 2
    out = None
    for part, values in enumerate(
        (
            (own_keep, down_keep, back2_keep, back3_keep),
            (own_other, down_other, back2_other, back3_other),
        )
    ):
        local = combine(ids, values)
        over = across(local, half)
        beside = across(local, 1)
        over_beside = across(over, 1)
        if part == 0:
            out = project(
                False, False, (0, 1, 2, 3), ids, out_weight,
                (local, beside, over, over_beside), None,
            )
        else:
            out = project(True, False, (0, 1), ids, out_weight, (local, beside), out)
            out = project(True, True, (2, 3), ids, out_weight, (over, over_beside), out)
    return out


def solution(mesh):
    in_specs = (P("seq", "head", None), P("head", None), P(None, "head"))
    out_specs = P("seq", "head")
    by_planes = mesh.shape["seq"] == 8 and mesh.shape["head"] == 4
    plan = planes_plan if by_planes else routed_plan

    return jax.shard_map(plan, mesh=mesh, in_specs=in_specs, out_specs=out_specs, check_vma=False)
```

```python
import functools
import math

import jax
import jax.numpy as jnp
from jax import lax
from jax.experimental import pallas as pl
from jax.experimental.pallas import tpu as pltpu
from jax.sharding import PartitionSpec as P


NEG = -1e30


def softmax_rows(query_part, query_pos, key_rows, value_rows, key_pos, usable, score_scale):
    scores = jnp.dot(query_part, key_rows.T, preferred_element_type=jnp.float32) * score_scale
    allowed = usable[None, :] & (key_pos[None, :] <= query_pos[:, None])
    scores = jnp.where(allowed, scores, -1e30)
    highest = jnp.max(scores, axis=1, keepdims=True)
    weights = jnp.exp(scores - highest)
    totals = jnp.sum(weights, axis=1, keepdims=True)
    probabilities = weights.astype(jnp.bfloat16)
    attended = jnp.dot(probabilities, value_rows, preferred_element_type=jnp.float32) / totals
    return attended.astype(jnp.bfloat16)


def attend_all(queries, key_rows, value_rows, positions, usable):
    length = queries.shape[0]
    rows_step = min(512, length)
    score_scale = 1.0 / math.sqrt(queries.shape[1])
    pieces = []
    for step_index in range(length // rows_step):
        first_row = step_index * rows_step
        key_end = first_row + rows_step
        pieces.append(
            softmax_rows(
                queries[first_row : first_row + rows_step],
                positions[first_row : first_row + rows_step],
                key_rows[:key_end],
                value_rows[:key_end],
                positions[:key_end],
                usable[:key_end],
                score_scale,
            )
        )
    return jnp.concatenate(pieces, axis=0)


def slot_tables(owners, myself, pair_slots):
    source_count, item_count = owners.shape
    item_ids = jnp.arange(item_count, dtype=jnp.int32)
    before = item_ids[None, :] < item_ids[:, None]
    same_owner = owners[:, :, None] == owners[:, None, :]
    rank_within = jnp.sum((same_owner & before[None]).astype(jnp.int32), axis=2)
    own_owner = lax.dynamic_index_in_dim(owners, myself, 0, keepdims=False)
    own_rank = lax.dynamic_index_in_dim(rank_within, myself, 0, keepdims=False)
    own_slot = own_owner * pair_slots + own_rank
    slot_ids = jnp.arange(source_count * pair_slots, dtype=jnp.int32)
    slot_match = own_slot[None, :] == slot_ids[:, None]
    source_item = jnp.sum(slot_match.astype(jnp.int32) * item_ids[None, :], axis=1)
    filled = jnp.any(slot_match, axis=1)
    rank_ids = jnp.arange(pair_slots, dtype=jnp.int32)
    arriving = (owners == myself)[:, None, :] & (rank_within[:, None, :] == rank_ids[None, :, None])
    arrived_item = jnp.sum(arriving.astype(jnp.int32) * item_ids[None, None, :], axis=2).reshape(-1)
    arrived = jnp.any(arriving, axis=2).reshape(-1)
    return (own_slot, source_item, filled, arrived_item, arrived)


def routed_plan(qkv_heads, clusters, out_weight):
    seq_count = lax.axis_size("seq")
    myself = lax.axis_index("seq")
    tok_rows, head_local, triple = qkv_heads.shape
    head_width = triple // 3
    block_total = clusters.shape[1]
    per_shard = block_total // seq_count
    block_len = tok_rows // per_shard
    capacity = 2 * per_shard
    cluster_table = clusters.reshape(head_local, seq_count, per_shard)
    blocks = qkv_heads.reshape(per_shard, block_len, head_local, triple).transpose(2, 0, 1, 3)
    pair_slots = (head_local * capacity + seq_count - 1) // seq_count
    owners = cluster_table.transpose(1, 0, 2).reshape(seq_count, head_local * per_shard)
    own_slot, source_item, filled, arrived_item, arrived = slot_tables(owners, myself, pair_slots)
    flat_blocks = blocks.reshape(head_local * per_shard, block_len, triple)
    outgoing = jnp.take(flat_blocks, source_item, axis=0)
    outgoing = jnp.where(filled[:, None, None], outgoing, jnp.zeros((), outgoing.dtype))
    incoming = lax.all_to_all(outgoing, "seq", split_axis=0, concat_axis=0, tiled=True)
    slot_head = arrived_item // per_shard
    slot_source = jnp.arange(seq_count * pair_slots, dtype=jnp.int32) // pair_slots
    slot_block = slot_source * per_shard + arrived_item % per_shard
    slot_count = incoming.shape[0]
    slot_ids = jnp.arange(slot_count, dtype=jnp.int32)
    compact_ids = jnp.arange(capacity, dtype=jnp.int32)
    place_all = jnp.zeros((slot_count,), jnp.int32)
    padded_parts = []
    for head_index in range(head_local):
        belongs = arrived & (slot_head == head_index)
        belongs_int = belongs.astype(jnp.int32)
        places = jnp.cumsum(belongs_int) - belongs_int
        chosen = belongs[None, :] & (places[None, :] == compact_ids[:, None])
        chosen_int = chosen.astype(jnp.int32)
        pick_slot = jnp.sum(chosen_int * slot_ids[None, :], axis=1)
        kept_valid = jnp.any(chosen, axis=1)
        kept_ids = jnp.sum(chosen_int * slot_block[None, :], axis=1)
        gathered = jnp.take(incoming, pick_slot, axis=0).reshape(capacity * block_len, triple)
        positions = (
            kept_ids[:, None] * block_len + jnp.arange(block_len, dtype=jnp.int32)[None, :]
        ).reshape(-1)
        usable = jnp.repeat(kept_valid, block_len)
        attended = attend_all(
            gathered[:, :head_width],
            gathered[:, head_width : 2 * head_width],
            gathered[:, 2 * head_width :],
            positions,
            usable,
        )
        padded_parts.append(attended.reshape(capacity, block_len, head_width))
        padded_parts.append(jnp.zeros((1, block_len, head_width), jnp.bfloat16))
        place_all = place_all + jnp.where(belongs, places, 0)
    padded_all = jnp.concatenate(padded_parts, axis=0)
    back_index = jnp.where(arrived, slot_head * (capacity + 1) + place_all, capacity)
    outbound = jnp.take(padded_all, back_index, axis=0)
    home_slots = lax.all_to_all(outbound, "seq", split_axis=0, concat_axis=0, tiled=True)
    own_blocks = jnp.take(home_slots, own_slot, axis=0).reshape(
        head_local, per_shard, block_len, head_width
    )
    features = own_blocks.transpose(1, 2, 0, 3).reshape(tok_rows, head_local * head_width)
    summed = jnp.dot(
        lax.all_gather(features, "head", axis=1, tiled=True),
        out_weight,
        preferred_element_type=jnp.float32,
    )
    return summed.astype(jnp.bfloat16)


VMEM_BYTES = 24 * 1024 * 1024


def split_kernel(ids_ref, qkv_ref, q_keep, kv_keep, first, second, third):
    column = ids_ref[0, 0]
    plane = ids_ref[0, 1]
    rows, width = q_keep.shape

    def pieces(head):
        yield lambda: qkv_ref[head, :, :width]
        yield lambda: qkv_ref[head, :, width : 2 * width]
        yield lambda: jnp.concatenate(
            [
                qkv_ref[head, b * width : (b + 1) * width, 2 * width :].T
                for b in range(rows // width)
            ],
            axis=0,
        )

    query, key, value = pieces(column)
    q_keep[...] = query()
    kv_keep[0] = key()
    kv_keep[1] = value()
    query, key, value = pieces(1 - column)

    @pl.when(plane == 0)
    def _():
        first[...] = key()
        second[...] = value()
        third[...] = query()

    @pl.when(plane > 0)
    def _():
        first[...] = query()
        second[...] = key()
        third[...] = value()


def split_heads(ids, by_head):
    heads, rows, triple = by_head.shape
    width = triple // 3
    step = rows // 4
    one = jax.ShapeDtypeStruct((rows, width), by_head.dtype)
    two = jax.ShapeDtypeStruct((2, rows, width), by_head.dtype)
    spec = pl.BlockSpec((step, width), lambda i: (i, 0))
    return pl.pallas_call(
        split_kernel,
        grid=(rows // step,),
        in_specs=[
            pl.BlockSpec(memory_space=pltpu.SMEM),
            pl.BlockSpec((heads, step, triple), lambda i: (0, i, 0)),
        ],
        out_specs=[spec, pl.BlockSpec((2, step, width), lambda i: (0, i, 0)), spec, spec, spec],
        out_shape=[one, two, one, one, one],
        compiler_params=pltpu.CompilerParams(vmem_limit_bytes=VMEM_BYTES),
        name="split_heads",
    )(ids, by_head)


OWN, UPPER, REST, BOTH, NEAR, KEPT, SWAPPED = range(0, 21, 3)
WHERE = 21
TABLE_ROWS = 24


def tables_kernel(per_shard, cluster_count, ids_ref, table_ref, out_ref):
    column = ids_ref[0, 0]
    plane = ids_ref[0, 1]
    blocks = table_ref.shape[1]
    span = 2 * per_shard
    out_ref[...] = jnp.zeros_like(out_ref)
    slot = lax.broadcasted_iota(jnp.int32, (1, 2 * blocks), 1)
    out_ref[WHERE : WHERE + 1, :] = jnp.where(slot == 0, column, plane)
    labels = jnp.where(column == 0, table_ref[0:1, :], table_ref[1:2, :])
    down = lax.broadcasted_iota(jnp.int32, (blocks, blocks), 0)
    along = lax.broadcasted_iota(jnp.int32, (blocks, blocks), 1)
    wide = jnp.broadcast_to(labels, (blocks, blocks))
    tall = jnp.sum(jnp.where(down == along, wide, 0), axis=1, keepdims=True)
    before = (tall < wide) | ((tall == wide) & (down < along))
    cluster = lax.broadcasted_iota(jnp.int32, (blocks, cluster_count), 1)
    block = lax.broadcasted_iota(jnp.int32, (blocks, 1), 0)
    in_plane = block // span
    side = lax.rem(block // per_shard, 2)
    high = (in_plane == 2) | (in_plane == 3)
    for row, member in (
        (OWN, in_plane == plane),
        (UPPER, (in_plane == plane) | ((in_plane == plane - 1) & (side == column))),
        (REST, (in_plane == plane - 1) & (side != column)),
        (BOTH, (in_plane == plane) | (in_plane == plane - 1)),
        (NEAR, in_plane == plane + 1),
        (KEPT, high & (side == column)),
        (SWAPPED, high & (side != column)),
    ):
        one = member.astype(jnp.int32)
        place = jnp.sum(jnp.where(before, one, 0), axis=0, keepdims=True)
        start = jnp.sum(jnp.where(tall < cluster, one, 0), axis=0, keepdims=True)
        count = jnp.sum(jnp.where(tall == cluster, one, 0), axis=0, keepdims=True)
        out_ref[row : row + 1, :blocks] = place
        out_ref[row + 1 : row + 2, :cluster_count] = start
        out_ref[row + 2 : row + 3, :cluster_count] = count


def block_tables(ids, table, per_shard):
    cluster_count = table.shape[1] // per_shard
    vmem = pl.BlockSpec(memory_space=pltpu.VMEM)
    return pl.pallas_call(
        functools.partial(tables_kernel, per_shard, cluster_count),
        in_specs=[pl.BlockSpec(memory_space=pltpu.SMEM), vmem],
        out_specs=vmem,
        out_shape=jax.ShapeDtypeStruct((TABLE_ROWS, 2 * table.shape[1]), jnp.int32),
        compiler_params=pltpu.CompilerParams(vmem_limit_bytes=VMEM_BYTES),
        name="block_tables",
    )(ids, table)


KINDS = {
    "own": (OWN, OWN, 4, (1, 2, 4)),
    "near": (OWN, NEAR, 2, (1, 2)),
    "far_high": (UPPER, KEPT, 3, (1, 2, 3)),
    "far_low": (REST, KEPT, 1, (1,)),
    "far_both": (BOTH, SWAPPED, 4, (2, 4)),
}


def attend_kernel(kind, per_shard, cluster_count, sizes, tab, *refs):
    own = kind == "own"
    kv_row, q_row = KINDS[kind][:2]
    plane_keys = kind != "far_low"
    low_kept = kind in ("own", "far_high", "far_both")
    low_rest = kind in ("own", "far_low", "far_both")
    merging = kind == "far_low"
    q_count = 1 if own else 2
    kv_count = 4 * plane_keys + low_kept + 2 * low_rest
    q_refs = refs[:q_count]
    kv_refs = refs[q_count : q_count + kv_count]
    refs = refs[q_count + kv_count :]
    earlier, refs = (refs[:2], refs[2:]) if merging else ((), refs)
    out_refs = refs[:2]
    keys, values, queries, outs, logs, mine = refs[2:]
    column = tab[WHERE, 0]
    plane = tab[WHERE, 1]
    width = keys.shape[2]
    scale = 1.0 / math.sqrt(width)
    log_scale = scale / math.log(2.0)
    if own:
        kv_row = jnp.where(plane == 1, BOTH, OWN)

    def body():
        used = tab[kv_row + 1, cluster_count - 1] + tab[kv_row + 2, cluster_count - 1]

        def bring(shard, key_ref, value_ref):
            for b in range(per_shard):
                to = tab[kv_row, shard * per_shard + b]
                keys[to] = key_ref[b * width : (b + 1) * width, :]
                values[to] = value_ref[b * width : (b + 1) * width, :]

        if plane_keys:
            next_shard = 2 * plane + 1 - column
            kept, first, second, third = kv_refs[:4]
            bring(2 * plane + column, kept.at[0], kept.at[1])

            @pl.when(plane == 0)
            def _():
                bring(next_shard, first, second)

            @pl.when(plane > 0)
            def _():
                bring(next_shard, second, third)

        def bring_low():
            if low_kept:
                low_keep = kv_refs[4]
                bring(2 * plane - 2 + column, low_keep.at[0], low_keep.at[1])
            if low_rest:
                bring(2 * plane - 1 - column, kv_refs[-2], kv_refs[-1])

        if own:
            pl.when(plane == 1)(bring_low)
        else:
            bring_low()

        def blank(i, carry):
            keys[used + i] = jnp.zeros(keys.shape[1:], keys.dtype)
            values[used + i] = jnp.zeros(values.shape[1:], values.dtype)
            return carry

        lax.fori_loop(0, sizes[-1], blank, 0)

        if own:
            shards = (2 * plane + column, 2 * plane + 1 - column)
        elif kind == "near":
            shards = (2 * plane + 2 + column, 2 * plane + 3 - column)
        elif kind == "far_both":
            shards = (2 * plane + 3 - column, 2 * plane + 5 - column)
        else:
            shards = (2 * plane + 2 + column, 2 * plane + 4 + column)

        def bring_query(shard, q_ref):
            for b in range(per_shard):
                to = tab[q_row, shard * per_shard + b]
                queries[to] = q_ref[b * width : (b + 1) * width, :]

        bring_query(shards[0], q_refs[0])
        if own:

            @pl.when(plane == 0)
            def _():
                bring_query(shards[1], third)

            @pl.when(plane > 0)
            def _():
                bring_query(shards[1], first)
        else:
            bring_query(shards[1], q_refs[1])

        if own:
            ahead = lax.broadcasted_iota(jnp.int32, (width, 4 * width), 0)
            ahead -= lax.broadcasted_iota(jnp.int32, (width, 4 * width), 1)

        def cluster(c, carry):
            begin = tab[kv_row + 1, c]
            length = tab[kv_row + 2, c]
            q_begin = tab[q_row + 1, c]
            q_count = tab[q_row + 2, c]

            def tile(wide, most, below):
                query = queries[pl.ds(q_begin, wide)].reshape(wide * width, width)
                parts = []
                for u in range(most):
                    part = lax.dot_general(
                        keys[begin + u],
                        query,
                        (((1,), (1,)), ((), ())),
                        preferred_element_type=jnp.float32,
                    )
                    if own:
                        allowed = ahead[:, : wide * width] <= (length - q_count - u) * width
                        part = jnp.where(allowed, part, NEG)
                    elif u > below:
                        part = jnp.where(u < length, part, NEG)
                    parts.append(part)
                scores = jnp.concatenate(parts, axis=0)
                top = jnp.max(scores, axis=0, keepdims=True)
                weights = jnp.exp2((scores - top) * log_scale)
                total = jnp.sum(weights, axis=0, keepdims=True)
                acc = jnp.dot(
                    jnp.concatenate([values[begin + u] for u in range(most)], axis=1),
                    weights.astype(jnp.bfloat16),
                    preferred_element_type=jnp.float32,
                )
                result = (acc / total).astype(outs.dtype)
                log = top * scale + jnp.log(total)
                for j in range(wide):
                    outs[q_begin + j] = result[:, j * width : (j + 1) * width]
                    logs[pl.ds(q_begin + j, 1), :] = log[:, j * width : (j + 1) * width]

            for wide in (2, 4):
                for k, most in enumerate(sizes):
                    below = sizes[k - 1] if k else 0

                    fits = (q_count > wide - 2) & (q_count <= wide)

                    @pl.when(fits & (length > below) & (length <= most))
                    def _(wide=wide, most=most, below=below):
                        tile(wide, most, below)

            if not own:

                @pl.when(length == 0)
                def _():
                    def empty(i, carry):
                        outs[q_begin + i] = jnp.zeros((width, width), outs.dtype)
                        logs[pl.ds(q_begin + i, 1), :] = jnp.full((1, width), NEG, jnp.float32)
                        return carry

                    lax.fori_loop(0, q_count, empty, 0)

            return carry

        lax.fori_loop(0, cluster_count, cluster, 0)
        for g, out_ref in enumerate(out_refs):
            for b in range(per_shard):
                mine[b : b + 1, :] = logs[pl.ds(tab[q_row, shards[g] * per_shard + b], 1), :]
            rest = mine[...]
            if merging:
                other = log_of(earlier[g], per_shard * width)
                top = jnp.maximum(rest, other)
                share, other_share = jnp.exp(rest - top), jnp.exp(other - top)
                total = share + other_share
                share, other_share = share / total, other_share / total
                rest = jnp.maximum(top + jnp.log(total), NEG)
            for b in range(per_shard):
                lines = slice(b * width, (b + 1) * width)
                block = outs[tab[q_row, shards[g] * per_shard + b]]
                if merging:
                    block = block.astype(jnp.float32) * share[b : b + 1]
                    block += earlier[g][lines, :].astype(jnp.float32) * other_share[b : b + 1]
                out_ref[lines, :] = block.astype(jnp.bfloat16)
            pieces = []
            for _ in range(3):
                piece = rest.astype(jnp.bfloat16).astype(jnp.float32)
                rest = rest - piece
                pieces.append(piece)
            pieces.append(jnp.zeros_like(rest))
            out_ref[per_shard * width :, :] = jnp.concatenate(pieces, axis=0).astype(jnp.bfloat16)

    if own:
        body()
    else:

        @pl.when(plane == (2 if kind == "near" else 1))
        def _():
            body()


def log_of(ref, rows):
    tail = ref[rows:, :].astype(jnp.float32)
    step = tail.shape[0] // 4
    return tail[:step] + tail[step : 2 * step] + tail[2 * step : 3 * step]


def attend(kind, cluster_count, tables, queries, key_values, earlier=()):
    rows, width = queries[0].shape
    per_shard = rows // width
    shards, quarters = KINDS[kind][2:]
    sizes = tuple(q * per_shard // 4 for q in quarters)
    held = shards * per_shard + sizes[-1]
    smem = pl.BlockSpec(memory_space=pltpu.SMEM)
    vmem = pl.BlockSpec(memory_space=pltpu.VMEM)
    out = jax.ShapeDtypeStruct((per_shard * (width + 4), width), jnp.bfloat16)
    tile = (width, width)
    return pl.pallas_call(
        functools.partial(attend_kernel, kind, per_shard, cluster_count, sizes),
        in_specs=[smem] + [vmem] * (len(queries) + len(key_values) + len(earlier)),
        out_specs=[vmem] * 2,
        out_shape=[out] * 2,
        scratch_shapes=[
            pltpu.VMEM((held,) + tile, jnp.bfloat16),
            pltpu.VMEM((held,) + tile, jnp.bfloat16),
            pltpu.VMEM((2 * per_shard + 4,) + tile, jnp.bfloat16),
            pltpu.VMEM((2 * per_shard + 4,) + tile, jnp.bfloat16),
            pltpu.VMEM((2 * per_shard + 8, width), jnp.float32),
            pltpu.VMEM((per_shard, width), jnp.float32),
        ],
        compiler_params=pltpu.CompilerParams(vmem_limit_bytes=VMEM_BYTES),
    )(tables, *queries, *key_values, *earlier)


def combine_kernel(ids_ref, own, near, second, third, out_ref):
    plane = ids_ref[0, 1]
    rows, width = out_ref.shape
    own_log = log_of(own, rows)
    near_log = jnp.where(plane == 3, log_of(near, rows), NEG)
    far_log = jnp.where(plane == 3, log_of(third, rows), log_of(second, rows))
    far_log = jnp.where(plane > 1, far_log, NEG)
    top = jnp.maximum(jnp.maximum(own_log, near_log), far_log)
    own_part = jnp.exp(own_log - top)
    near_part = jnp.exp(near_log - top)
    far_part = jnp.exp(far_log - top)
    share = 1.0 / (own_part + near_part + far_part)
    own_part, near_part, far_part = own_part * share, near_part * share, far_part * share
    for b in range(rows // width):
        lines = slice(b * width, (b + 1) * width)
        far = jnp.where(plane == 3, third[lines, :], second[lines, :])
        mixed = (
            own[lines, :].astype(jnp.float32) * own_part[b : b + 1]
            + near[lines, :].astype(jnp.float32) * near_part[b : b + 1]
            + far.astype(jnp.float32) * far_part[b : b + 1]
        )
        out_ref[lines, :] = mixed.T.astype(jnp.bfloat16)


def combine(ids, values):
    size, width = values[-1].shape
    rows = size // (width + 4) * width
    vmem = pl.BlockSpec(memory_space=pltpu.VMEM)
    return pl.pallas_call(
        combine_kernel,
        in_specs=[pl.BlockSpec(memory_space=pltpu.SMEM)] + [vmem] * len(values),
        out_specs=vmem,
        out_shape=jax.ShapeDtypeStruct((rows, width), jnp.bfloat16),
        compiler_params=pltpu.CompilerParams(vmem_limit_bytes=VMEM_BYTES),
        name="combine",
    )(ids, *values)


def project_kernel(which, ids_ref, weight_ref, *refs):
    group = ids_ref[0, 2]
    column = ids_ref[0, 0]
    heads = (column, 1 - column)
    out_ref = refs[-1]
    features = refs[: len(which)]
    given = refs[len(which)] if len(refs) > len(which) + 1 else None
    depth = features[0].shape[1]
    cols = out_ref.shape[1]
    here = pl.ds(pl.multiple_of(pl.program_id(0) * cols, cols), cols)
    lines = [
        pl.ds(pl.multiple_of(((group ^ j) * 2 + heads[part]) * depth, depth), depth)
        for part, j in which
    ]
    right = jnp.concatenate([weight_ref[at, here] for at in lines], axis=0)
    chunk = 512
    for start in range(0, out_ref.shape[0], chunk):
        rows = slice(start, start + chunk)
        left = jnp.concatenate([f[rows, :] for f in features], axis=1)
        acc = jnp.dot(left, right, preferred_element_type=jnp.float32)
        if given is not None:
            acc = acc + given[rows, here]
        out_ref[rows, :] = acc.astype(out_ref.dtype)


def project(final, which, ids, weight, features, given):
    rows = features[0].shape[0]
    vmem = pl.BlockSpec(memory_space=pltpu.VMEM)
    given = [] if given is None else [given]
    width = weight.shape[1]
    step = width // 4
    return pl.pallas_call(
        functools.partial(project_kernel, which),
        grid=(width // step,),
        in_specs=[pl.BlockSpec(memory_space=pltpu.SMEM)]
        + [vmem] * (1 + len(features) + len(given)),
        out_specs=pl.BlockSpec((rows, step), lambda i: (0, i)),
        out_shape=jax.ShapeDtypeStruct((rows, width), jnp.bfloat16 if final else jnp.float32),
        compiler_params=pltpu.CompilerParams(vmem_limit_bytes=VMEM_BYTES),
        name="project",
    )(ids, weight, *features, *given)


def planes_plan(qkv_heads, clusters, out_weight):
    seq_count = lax.axis_size("seq")
    head_count = lax.axis_size("head")
    shard = lax.axis_index("seq")
    group = lax.axis_index("head")
    tok_rows, _, triple = qkv_heads.shape
    width = triple // 3
    ids = jnp.stack([shard % 2, shard // 2, group]).astype(jnp.int32).reshape(1, 3)

    swap = [(c, c ^ 1) for c in range(seq_count)]

    def hop(*moves, cross=0):
        return [(2 * a + x, 2 * b + (x ^ cross)) for a, b in moves for x in range(2)]

    def send(value, pairs):
        return lax.ppermute(value, "seq", pairs)

    def across(value, flip):
        return lax.ppermute(value, "head", [(g, g ^ flip) for g in range(head_count)])

    by_head = qkv_heads.transpose(1, 0, 2)
    q_keep, kv_keep, give1, give2, give3 = split_heads(ids, by_head)

    first = send(give1, swap)
    low_keep = send(kv_keep, hop((0, 1)))
    far2_keep = send(q_keep, hop((2, 1)))
    far3_keep = send(q_keep, hop((3, 1)))
    second = send(give2, swap)
    third = send(give3, swap)
    near_keep = send(q_keep, hop((3, 2)))
    low_first = send(first, hop((0, 1)))
    far2_swap = send(first, hop((2, 1)))
    far3_swap = send(first, hop((3, 1)))
    low_second = send(second, hop((0, 1)))
    near_swap = send(first, hop((3, 2)))

    per_shard = tok_rows // width
    cluster_count = clusters.shape[1] // per_shard
    tables = block_tables(ids, clusters, per_shard)

    def meet(kind, queries, key_values, earlier=()):
        return attend(kind, cluster_count, tables, queries, key_values, earlier)

    plane_kv = (kv_keep, first, second, third)
    started = meet("far_high", (far2_keep, far3_keep), plane_kv + (low_keep,))
    back2_keep, back3_keep = meet(
        "far_low", (far2_keep, far3_keep), (low_first, low_second), started
    )
    back3_keep = send(back3_keep, hop((1, 3)))
    back2_keep = send(back2_keep, hop((1, 2)))
    both_kv = plane_kv + (low_keep, low_first, low_second)
    down_keep, down_swap = meet("near", (near_keep, near_swap), plane_kv)
    down_keep = send(down_keep, hop((2, 3)))
    back2_swap, back3_swap = meet("far_both", (far2_swap, far3_swap), both_kv)
    back3_other = send(back3_swap, hop((1, 3), cross=1))
    back2_other = send(back2_swap, hop((1, 2), cross=1))
    down_other = send(down_swap, hop((2, 3), cross=1))
    own_keep, own_swap = meet("own", (q_keep,), both_kv)
    own_other = send(own_swap, swap)
    half = head_count // 2
    out = None
    pieces = []
    for part, values in enumerate(
        (
            (own_keep, down_keep, back2_keep, back3_keep),
            (own_other, down_other, back2_other, back3_other),
        )
    ):
        local = combine(ids, values)
        over = across(local, half)
        beside = across(local, 1)
        over_beside = across(over, 1)
        pieces += [((part, 0), local), ((part, 1), beside), ((part, 2), over), ((part, 3), over_beside)]
    for step, chosen in enumerate((pieces[:2], pieces[2:6], pieces[6:])):
        which, features = zip(*chosen)
        out = project(step == 2, which, ids, out_weight, features, out)
    return out


def solution(mesh):
    in_specs = (P("seq", "head", None), P("head", None), P(None, "head"))
    out_specs = P("seq", "head")
    by_planes = mesh.shape["seq"] == 8 and mesh.shape["head"] == 4
    plan = planes_plan if by_planes else routed_plan

    return jax.shard_map(plan, mesh=mesh, in_specs=in_specs, out_specs=out_specs, check_vma=False)
```

```python
import functools
import math

import jax
import jax.numpy as jnp
from jax import lax
from jax.experimental import pallas as pl
from jax.experimental.pallas import tpu as pltpu
from jax.sharding import PartitionSpec as P


NEG = -1e30


def softmax_rows(query_part, query_pos, key_rows, value_rows, key_pos, usable, score_scale):
    scores = jnp.dot(query_part, key_rows.T, preferred_element_type=jnp.float32) * score_scale
    allowed = usable[None, :] & (key_pos[None, :] <= query_pos[:, None])
    scores = jnp.where(allowed, scores, -1e30)
    highest = jnp.max(scores, axis=1, keepdims=True)
    weights = jnp.exp(scores - highest)
    totals = jnp.sum(weights, axis=1, keepdims=True)
    probabilities = weights.astype(jnp.bfloat16)
    attended = jnp.dot(probabilities, value_rows, preferred_element_type=jnp.float32) / totals
    return attended.astype(jnp.bfloat16)


def attend_all(queries, key_rows, value_rows, positions, usable):
    length = queries.shape[0]
    rows_step = min(512, length)
    score_scale = 1.0 / math.sqrt(queries.shape[1])
    pieces = []
    for step_index in range(length // rows_step):
        first_row = step_index * rows_step
        key_end = first_row + rows_step
        pieces.append(
            softmax_rows(
                queries[first_row : first_row + rows_step],
                positions[first_row : first_row + rows_step],
                key_rows[:key_end],
                value_rows[:key_end],
                positions[:key_end],
                usable[:key_end],
                score_scale,
            )
        )
    return jnp.concatenate(pieces, axis=0)


def slot_tables(owners, myself, pair_slots):
    source_count, item_count = owners.shape
    item_ids = jnp.arange(item_count, dtype=jnp.int32)
    before = item_ids[None, :] < item_ids[:, None]
    same_owner = owners[:, :, None] == owners[:, None, :]
    rank_within = jnp.sum((same_owner & before[None]).astype(jnp.int32), axis=2)
    own_owner = lax.dynamic_index_in_dim(owners, myself, 0, keepdims=False)
    own_rank = lax.dynamic_index_in_dim(rank_within, myself, 0, keepdims=False)
    own_slot = own_owner * pair_slots + own_rank
    slot_ids = jnp.arange(source_count * pair_slots, dtype=jnp.int32)
    slot_match = own_slot[None, :] == slot_ids[:, None]
    source_item = jnp.sum(slot_match.astype(jnp.int32) * item_ids[None, :], axis=1)
    filled = jnp.any(slot_match, axis=1)
    rank_ids = jnp.arange(pair_slots, dtype=jnp.int32)
    arriving = (owners == myself)[:, None, :] & (rank_within[:, None, :] == rank_ids[None, :, None])
    arrived_item = jnp.sum(arriving.astype(jnp.int32) * item_ids[None, None, :], axis=2).reshape(-1)
    arrived = jnp.any(arriving, axis=2).reshape(-1)
    return (own_slot, source_item, filled, arrived_item, arrived)


def routed_plan(qkv_heads, clusters, out_weight):
    seq_count = lax.axis_size("seq")
    myself = lax.axis_index("seq")
    tok_rows, head_local, triple = qkv_heads.shape
    head_width = triple // 3
    block_total = clusters.shape[1]
    per_shard = block_total // seq_count
    block_len = tok_rows // per_shard
    capacity = 2 * per_shard
    cluster_table = clusters.reshape(head_local, seq_count, per_shard)
    blocks = qkv_heads.reshape(per_shard, block_len, head_local, triple).transpose(2, 0, 1, 3)
    pair_slots = (head_local * capacity + seq_count - 1) // seq_count
    owners = cluster_table.transpose(1, 0, 2).reshape(seq_count, head_local * per_shard)
    own_slot, source_item, filled, arrived_item, arrived = slot_tables(owners, myself, pair_slots)
    flat_blocks = blocks.reshape(head_local * per_shard, block_len, triple)
    outgoing = jnp.take(flat_blocks, source_item, axis=0)
    outgoing = jnp.where(filled[:, None, None], outgoing, jnp.zeros((), outgoing.dtype))
    incoming = lax.all_to_all(outgoing, "seq", split_axis=0, concat_axis=0, tiled=True)
    slot_head = arrived_item // per_shard
    slot_source = jnp.arange(seq_count * pair_slots, dtype=jnp.int32) // pair_slots
    slot_block = slot_source * per_shard + arrived_item % per_shard
    slot_count = incoming.shape[0]
    slot_ids = jnp.arange(slot_count, dtype=jnp.int32)
    compact_ids = jnp.arange(capacity, dtype=jnp.int32)
    place_all = jnp.zeros((slot_count,), jnp.int32)
    padded_parts = []
    for head_index in range(head_local):
        belongs = arrived & (slot_head == head_index)
        belongs_int = belongs.astype(jnp.int32)
        places = jnp.cumsum(belongs_int) - belongs_int
        chosen = belongs[None, :] & (places[None, :] == compact_ids[:, None])
        chosen_int = chosen.astype(jnp.int32)
        pick_slot = jnp.sum(chosen_int * slot_ids[None, :], axis=1)
        kept_valid = jnp.any(chosen, axis=1)
        kept_ids = jnp.sum(chosen_int * slot_block[None, :], axis=1)
        gathered = jnp.take(incoming, pick_slot, axis=0).reshape(capacity * block_len, triple)
        positions = (
            kept_ids[:, None] * block_len + jnp.arange(block_len, dtype=jnp.int32)[None, :]
        ).reshape(-1)
        usable = jnp.repeat(kept_valid, block_len)
        attended = attend_all(
            gathered[:, :head_width],
            gathered[:, head_width : 2 * head_width],
            gathered[:, 2 * head_width :],
            positions,
            usable,
        )
        padded_parts.append(attended.reshape(capacity, block_len, head_width))
        padded_parts.append(jnp.zeros((1, block_len, head_width), jnp.bfloat16))
        place_all = place_all + jnp.where(belongs, places, 0)
    padded_all = jnp.concatenate(padded_parts, axis=0)
    back_index = jnp.where(arrived, slot_head * (capacity + 1) + place_all, capacity)
    outbound = jnp.take(padded_all, back_index, axis=0)
    home_slots = lax.all_to_all(outbound, "seq", split_axis=0, concat_axis=0, tiled=True)
    own_blocks = jnp.take(home_slots, own_slot, axis=0).reshape(
        head_local, per_shard, block_len, head_width
    )
    features = own_blocks.transpose(1, 2, 0, 3).reshape(tok_rows, head_local * head_width)
    summed = jnp.dot(
        lax.all_gather(features, "head", axis=1, tiled=True),
        out_weight,
        preferred_element_type=jnp.float32,
    )
    return summed.astype(jnp.bfloat16)


VMEM_BYTES = 24 * 1024 * 1024


def split_kernel(ids_ref, qkv_ref, q_keep, kv_keep, first, second, third):
    column = ids_ref[0, 0]
    plane = ids_ref[0, 1]
    rows, width = q_keep.shape

    def pieces(head):
        yield lambda: qkv_ref[head, :, :width]
        yield lambda: qkv_ref[head, :, width : 2 * width]
        yield lambda: jnp.concatenate(
            [
                qkv_ref[head, b * width : (b + 1) * width, 2 * width :].T
                for b in range(rows // width)
            ],
            axis=0,
        )

    query, key, value = pieces(column)
    q_keep[...] = query()
    kv_keep[0] = key()
    kv_keep[1] = value()
    query, key, value = pieces(1 - column)

    @pl.when(plane == 0)
    def _():
        first[...] = key()
        second[...] = value()
        third[...] = query()

    @pl.when(plane > 0)
    def _():
        first[...] = query()
        second[...] = key()
        third[...] = value()


def split_heads(ids, by_head):
    heads, rows, triple = by_head.shape
    width = triple // 3
    step = rows // 4
    one = jax.ShapeDtypeStruct((rows, width), by_head.dtype)
    two = jax.ShapeDtypeStruct((2, rows, width), by_head.dtype)
    spec = pl.BlockSpec((step, width), lambda i: (i, 0))
    return pl.pallas_call(
        split_kernel,
        grid=(rows // step,),
        in_specs=[
            pl.BlockSpec(memory_space=pltpu.SMEM),
            pl.BlockSpec((heads, step, triple), lambda i: (0, i, 0)),
        ],
        out_specs=[spec, pl.BlockSpec((2, step, width), lambda i: (0, i, 0)), spec, spec, spec],
        out_shape=[one, two, one, one, one],
        compiler_params=pltpu.CompilerParams(vmem_limit_bytes=VMEM_BYTES),
        name="split_heads",
    )(ids, by_head)


OWN, UPPER, REST, BOTH, NEAR, KEPT, SWAPPED = range(0, 21, 3)
WHERE = 21
TABLE_ROWS = 24


def tables_kernel(per_shard, cluster_count, ids_ref, table_ref, out_ref):
    column = ids_ref[0, 0]
    plane = ids_ref[0, 1]
    blocks = table_ref.shape[1]
    span = 2 * per_shard
    out_ref[...] = jnp.zeros_like(out_ref)
    slot = lax.broadcasted_iota(jnp.int32, (1, 2 * blocks), 1)
    out_ref[WHERE : WHERE + 1, :] = jnp.where(slot == 0, column, plane)
    labels = jnp.where(column == 0, table_ref[0:1, :], table_ref[1:2, :])
    down = lax.broadcasted_iota(jnp.int32, (blocks, blocks), 0)
    along = lax.broadcasted_iota(jnp.int32, (blocks, blocks), 1)
    wide = jnp.broadcast_to(labels, (blocks, blocks))
    tall = jnp.sum(jnp.where(down == along, wide, 0), axis=1, keepdims=True)
    before = (tall < wide) | ((tall == wide) & (down < along))
    cluster = lax.broadcasted_iota(jnp.int32, (blocks, cluster_count), 1)
    block = lax.broadcasted_iota(jnp.int32, (blocks, 1), 0)
    in_plane = block // span
    side = lax.rem(block // per_shard, 2)
    high = (in_plane == 2) | (in_plane == 3)
    for row, member in (
        (OWN, in_plane == plane),
        (UPPER, (in_plane == plane) | ((in_plane == plane - 1) & (side == column))),
        (REST, (in_plane == plane - 1) & (side != column)),
        (BOTH, (in_plane == plane) | (in_plane == plane - 1)),
        (NEAR, in_plane == plane + 1),
        (KEPT, high & (side == column)),
        (SWAPPED, high & (side != column)),
    ):
        one = member.astype(jnp.int32)
        place = jnp.sum(jnp.where(before, one, 0), axis=0, keepdims=True)
        start = jnp.sum(jnp.where(tall < cluster, one, 0), axis=0, keepdims=True)
        count = jnp.sum(jnp.where(tall == cluster, one, 0), axis=0, keepdims=True)
        out_ref[row : row + 1, :blocks] = place
        out_ref[row + 1 : row + 2, :cluster_count] = start
        out_ref[row + 2 : row + 3, :cluster_count] = count


def block_tables(ids, table, per_shard):
    cluster_count = table.shape[1] // per_shard
    vmem = pl.BlockSpec(memory_space=pltpu.VMEM)
    return pl.pallas_call(
        functools.partial(tables_kernel, per_shard, cluster_count),
        in_specs=[pl.BlockSpec(memory_space=pltpu.SMEM), vmem],
        out_specs=vmem,
        out_shape=jax.ShapeDtypeStruct((TABLE_ROWS, 2 * table.shape[1]), jnp.int32),
        compiler_params=pltpu.CompilerParams(vmem_limit_bytes=VMEM_BYTES),
        name="block_tables",
    )(ids, table)


KINDS = {
    "own": (OWN, OWN, 4, (1, 2, 4)),
    "near": (OWN, NEAR, 2, (1, 2)),
    "far_high": (UPPER, KEPT, 3, (1, 2, 3)),
    "far_low": (REST, KEPT, 1, (1,)),
    "far_both": (BOTH, SWAPPED, 4, (2, 4)),
}


def attend_kernel(kind, per_shard, cluster_count, sizes, tab, *refs):
    own = kind == "own"
    kv_row, q_row = KINDS[kind][:2]
    plane_keys = kind != "far_low"
    low_kept = kind in ("own", "far_high", "far_both")
    low_rest = kind in ("own", "far_low", "far_both")
    merging = kind == "far_low"
    q_count = 1 if own else 2
    kv_count = 4 * plane_keys + low_kept + 2 * low_rest
    q_refs = refs[:q_count]
    kv_refs = refs[q_count : q_count + kv_count]
    refs = refs[q_count + kv_count :]
    earlier, refs = (refs[:2], refs[2:]) if merging else ((), refs)
    out_refs = refs[:2]
    keys, values, queries, outs, logs, mine = refs[2:]
    column = tab[WHERE, 0]
    plane = tab[WHERE, 1]
    width = keys.shape[2]
    scale = 1.0 / math.sqrt(width)
    log_scale = scale / math.log(2.0)
    if own:
        kv_row = jnp.where(plane == 1, BOTH, OWN)

    def body():
        used = tab[kv_row + 1, cluster_count - 1] + tab[kv_row + 2, cluster_count - 1]

        def bring(shard, key_ref, value_ref):
            for b in range(per_shard):
                to = tab[kv_row, shard * per_shard + b]
                keys[to] = key_ref[b * width : (b + 1) * width, :]
                values[to] = value_ref[b * width : (b + 1) * width, :]

        if plane_keys:
            next_shard = 2 * plane + 1 - column
            kept, first, second, third = kv_refs[:4]
            bring(2 * plane + column, kept.at[0], kept.at[1])

            @pl.when(plane == 0)
            def _():
                bring(next_shard, first, second)

            @pl.when(plane > 0)
            def _():
                bring(next_shard, second, third)

        def bring_low():
            if low_kept:
                low_keep = kv_refs[4]
                bring(2 * plane - 2 + column, low_keep.at[0], low_keep.at[1])
            if low_rest:
                bring(2 * plane - 1 - column, kv_refs[-2], kv_refs[-1])

        if own:
            pl.when(plane == 1)(bring_low)
        else:
            bring_low()

        def blank(i, carry):
            keys[used + i] = jnp.zeros(keys.shape[1:], keys.dtype)
            values[used + i] = jnp.zeros(values.shape[1:], values.dtype)
            return carry

        lax.fori_loop(0, sizes[-1], blank, 0)

        if own:
            shards = (2 * plane + column, 2 * plane + 1 - column)
        elif kind == "near":
            shards = (2 * plane + 2 + column, 2 * plane + 3 - column)
        elif kind == "far_both":
            shards = (2 * plane + 3 - column, 2 * plane + 5 - column)
        else:
            shards = (2 * plane + 2 + column, 2 * plane + 4 + column)

        def bring_query(shard, q_ref):
            for b in range(per_shard):
                to = tab[q_row, shard * per_shard + b]
                queries[to] = q_ref[b * width : (b + 1) * width, :]

        bring_query(shards[0], q_refs[0])
        if own:

            @pl.when(plane == 0)
            def _():
                bring_query(shards[1], third)

            @pl.when(plane > 0)
            def _():
                bring_query(shards[1], first)
        else:
            bring_query(shards[1], q_refs[1])

        if own:
            ahead = lax.broadcasted_iota(jnp.int32, (width, 4 * width), 0)
            ahead -= lax.broadcasted_iota(jnp.int32, (width, 4 * width), 1)

        def cluster(c, carry):
            begin = tab[kv_row + 1, c]
            length = tab[kv_row + 2, c]
            q_begin = tab[q_row + 1, c]
            q_count = tab[q_row + 2, c]

            def tile(wide, most, below):
                query = queries[pl.ds(q_begin, wide)].reshape(wide * width, width)
                parts = []
                for u in range(most):
                    part = lax.dot_general(
                        keys[begin + u],
                        query,
                        (((1,), (1,)), ((), ())),
                        preferred_element_type=jnp.float32,
                    )
                    if own:
                        allowed = ahead[:, : wide * width] <= (length - q_count - u) * width
                        part = jnp.where(allowed, part, NEG)
                    elif u > below:
                        part = jnp.where(u < length, part, NEG)
                    parts.append(part)
                scores = jnp.concatenate(parts, axis=0)
                top = jnp.max(scores, axis=0, keepdims=True)
                weights = jnp.exp2((scores - top) * log_scale)
                total = jnp.sum(weights, axis=0, keepdims=True)
                acc = jnp.dot(
                    jnp.concatenate([values[begin + u] for u in range(most)], axis=1),
                    weights.astype(jnp.bfloat16),
                    preferred_element_type=jnp.float32,
                )
                result = (acc / total).astype(outs.dtype)
                log = top * scale + jnp.log(total)
                for j in range(wide):
                    outs[q_begin + j] = result[:, j * width : (j + 1) * width]
                    logs[pl.ds(q_begin + j, 1), :] = log[:, j * width : (j + 1) * width]

            for wide in (2, 4):
                for k, most in enumerate(sizes):
                    below = sizes[k - 1] if k else 0

                    fits = (q_count > wide - 2) & (q_count <= wide)

                    @pl.when(fits & (length > below) & (length <= most))
                    def _(wide=wide, most=most, below=below):
                        tile(wide, most, below)

            if not own:

                @pl.when(length == 0)
                def _():
                    def empty(i, carry):
                        outs[q_begin + i] = jnp.zeros((width, width), outs.dtype)
                        logs[pl.ds(q_begin + i, 1), :] = jnp.full((1, width), NEG, jnp.float32)
                        return carry

                    lax.fori_loop(0, q_count, empty, 0)

            return carry

        lax.fori_loop(0, cluster_count, cluster, 0)
        for g, out_ref in enumerate(out_refs):
            for b in range(per_shard):
                mine[b : b + 1, :] = logs[pl.ds(tab[q_row, shards[g] * per_shard + b], 1), :]
            rest = mine[...]
            if merging:
                other = log_of(earlier[g], per_shard * width)
                top = jnp.maximum(rest, other)
                share, other_share = jnp.exp(rest - top), jnp.exp(other - top)
                total = share + other_share
                share, other_share = share / total, other_share / total
                rest = jnp.maximum(top + jnp.log(total), NEG)
            for b in range(per_shard):
                lines = slice(b * width, (b + 1) * width)
                block = outs[tab[q_row, shards[g] * per_shard + b]]
                if merging:
                    block = block.astype(jnp.float32) * share[b : b + 1]
                    block += earlier[g][lines, :].astype(jnp.float32) * other_share[b : b + 1]
                out_ref[lines, :] = block.astype(jnp.bfloat16)
            pieces = []
            for _ in range(3):
                piece = rest.astype(jnp.bfloat16).astype(jnp.float32)
                rest = rest - piece
                pieces.append(piece)
            pieces.append(jnp.zeros_like(rest))
            out_ref[per_shard * width :, :] = jnp.concatenate(pieces, axis=0).astype(jnp.bfloat16)

    if own:
        body()
    else:

        @pl.when(plane == (2 if kind == "near" else 1))
        def _():
            body()


def low_near_kernel(per_shard, cluster_count, sizes, tab, *refs):
    low, near, shared = refs[:6], refs[6:12], refs[12:]
    attend_kernel("far_low", per_shard, cluster_count, sizes[0], tab, *low, *shared)
    attend_kernel("near", per_shard, cluster_count, sizes[1], tab, *near, *shared)


def both_kernel(per_shard, cluster_count, sizes, tab, *refs):
    passed, refs = refs[9], refs[:9] + refs[10:]
    attend_kernel("far_both", per_shard, cluster_count, sizes, tab, *refs)

    @pl.when(tab[WHERE, 1] == 2)
    def _():
        refs[9][...] = passed[...]


def log_of(ref, rows):
    tail = ref[rows:, :].astype(jnp.float32)
    step = tail.shape[0] // 4
    return tail[:step] + tail[step : 2 * step] + tail[2 * step : 3 * step]


def attend(kind, cluster_count, tables, operands):
    rows, width = operands[0].shape
    per_shard = rows // width
    kinds = ("far_low", "near") if kind == "low_near" else (kind,)
    sizes = tuple(tuple(q * per_shard // 4 for q in KINDS[k][3]) for k in kinds)
    held = max(KINDS[k][2] * per_shard + size[-1] for k, size in zip(kinds, sizes))
    if kind == "low_near":
        kernel = functools.partial(low_near_kernel, per_shard, cluster_count, sizes)
    elif kind == "far_both":
        kernel = functools.partial(both_kernel, per_shard, cluster_count, sizes[0])
    else:
        kernel = functools.partial(attend_kernel, kind, per_shard, cluster_count, sizes[0])
    smem = pl.BlockSpec(memory_space=pltpu.SMEM)
    vmem = pl.BlockSpec(memory_space=pltpu.VMEM)
    out = jax.ShapeDtypeStruct((per_shard * (width + 4), width), jnp.bfloat16)
    tile = (width, width)
    return pl.pallas_call(
        kernel,
        in_specs=[smem] + [vmem] * len(operands),
        out_specs=[vmem] * 2,
        out_shape=[out] * 2,
        scratch_shapes=[
            pltpu.VMEM((held,) + tile, jnp.bfloat16),
            pltpu.VMEM((held,) + tile, jnp.bfloat16),
            pltpu.VMEM((2 * per_shard + 4,) + tile, jnp.bfloat16),
            pltpu.VMEM((2 * per_shard + 4,) + tile, jnp.bfloat16),
            pltpu.VMEM((2 * per_shard + 8, width), jnp.float32),
            pltpu.VMEM((per_shard, width), jnp.float32),
        ],
        compiler_params=pltpu.CompilerParams(vmem_limit_bytes=VMEM_BYTES),
    )(tables, *operands)


def combine_kernel(ids_ref, own, up, third, out_ref):
    plane = ids_ref[0, 1]
    rows, width = out_ref.shape
    own_log = log_of(own, rows)
    up_log = jnp.where(plane > 1, log_of(up, rows), NEG)
    far_log = jnp.where(plane == 3, log_of(third, rows), NEG)
    top = jnp.maximum(jnp.maximum(own_log, up_log), far_log)
    own_part = jnp.exp(own_log - top)
    up_part = jnp.exp(up_log - top)
    far_part = jnp.exp(far_log - top)
    share = 1.0 / (own_part + up_part + far_part)
    own_part, up_part, far_part = own_part * share, up_part * share, far_part * share
    for b in range(rows // width):
        lines = slice(b * width, (b + 1) * width)
        mixed = (
            own[lines, :].astype(jnp.float32) * own_part[b : b + 1]
            + up[lines, :].astype(jnp.float32) * up_part[b : b + 1]
            + third[lines, :].astype(jnp.float32) * far_part[b : b + 1]
        )
        out_ref[lines, :] = mixed.T.astype(jnp.bfloat16)


def combine(ids, values):
    size, width = values[-1].shape
    rows = size // (width + 4) * width
    vmem = pl.BlockSpec(memory_space=pltpu.VMEM)
    return pl.pallas_call(
        combine_kernel,
        in_specs=[pl.BlockSpec(memory_space=pltpu.SMEM)] + [vmem] * len(values),
        out_specs=vmem,
        out_shape=jax.ShapeDtypeStruct((rows, width), jnp.bfloat16),
        compiler_params=pltpu.CompilerParams(vmem_limit_bytes=VMEM_BYTES),
        name="combine",
    )(ids, *values)


def project_kernel(which, ids_ref, weight_ref, *refs):
    group = ids_ref[0, 2]
    column = ids_ref[0, 0]
    heads = (column, 1 - column)
    out_ref = refs[-1]
    features = refs[: len(which)]
    given = refs[len(which)] if len(refs) > len(which) + 1 else None
    depth = features[0].shape[1]
    cols = out_ref.shape[1]
    here = pl.ds(pl.multiple_of(pl.program_id(0) * cols, cols), cols)
    lines = [
        pl.ds(pl.multiple_of(((group ^ j) * 2 + heads[part]) * depth, depth), depth)
        for part, j in which
    ]
    right = jnp.concatenate([weight_ref[at, here] for at in lines], axis=0)
    chunk = 512
    for start in range(0, out_ref.shape[0], chunk):
        rows = slice(start, start + chunk)
        left = jnp.concatenate([f[rows, :] for f in features], axis=1)
        acc = jnp.dot(left, right, preferred_element_type=jnp.float32)
        if given is not None:
            acc = acc + given[rows, here]
        out_ref[rows, :] = acc.astype(out_ref.dtype)


def project(final, which, ids, weight, features, given):
    rows = features[0].shape[0]
    vmem = pl.BlockSpec(memory_space=pltpu.VMEM)
    given = [] if given is None else [given]
    width = weight.shape[1]
    step = width // 2 if final else width
    return pl.pallas_call(
        functools.partial(project_kernel, which),
        grid=(width // step,),
        in_specs=[pl.BlockSpec(memory_space=pltpu.SMEM)]
        + [vmem] * (1 + len(features) + len(given)),
        out_specs=pl.BlockSpec((rows, step), lambda i: (0, i)),
        out_shape=jax.ShapeDtypeStruct((rows, width), jnp.bfloat16 if final else jnp.float32),
        compiler_params=pltpu.CompilerParams(vmem_limit_bytes=VMEM_BYTES),
        name="project",
    )(ids, weight, *features, *given)


def planes_plan(qkv_heads, clusters, out_weight):
    seq_count = lax.axis_size("seq")
    head_count = lax.axis_size("head")
    shard = lax.axis_index("seq")
    group = lax.axis_index("head")
    tok_rows, _, triple = qkv_heads.shape
    width = triple // 3
    ids = jnp.stack([shard % 2, shard // 2, group]).astype(jnp.int32).reshape(1, 3)

    swap = [(c, c ^ 1) for c in range(seq_count)]

    def hop(*moves, cross=0):
        return [(2 * a + x, 2 * b + (x ^ cross)) for a, b in moves for x in range(2)]

    def send(value, pairs):
        return lax.ppermute(value, "seq", pairs)

    def across(value, flip):
        return lax.ppermute(value, "head", [(g, g ^ flip) for g in range(head_count)])

    by_head = qkv_heads.transpose(1, 0, 2)
    q_keep, kv_keep, give1, give2, give3 = split_heads(ids, by_head)

    first = send(give1, swap)
    low_keep = send(kv_keep, hop((0, 1)))
    far2_keep = send(q_keep, hop((2, 1)))
    far3_keep = send(q_keep, hop((3, 1)))
    second = send(give2, swap)
    third = send(give3, swap)
    near_keep = send(q_keep, hop((3, 2)))
    low_first = send(first, hop((0, 1)))
    far2_swap = send(first, hop((2, 1)))
    far3_swap = send(first, hop((3, 1)))
    low_second = send(second, hop((0, 1)))
    near_swap = send(first, hop((3, 2)))

    per_shard = tok_rows // width
    cluster_count = clusters.shape[1] // per_shard
    tables = block_tables(ids, clusters, per_shard)

    def meet(kind, *operands):
        return attend(kind, cluster_count, tables, operands)

    plane_kv = (kv_keep, first, second, third)
    both_kv = plane_kv + (low_keep, low_first, low_second)
    started = meet("far_high", far2_keep, far3_keep, *plane_kv, low_keep)
    one, two = meet(
        "low_near", far2_keep, far3_keep, low_first, low_second, *started,
        near_keep, near_swap, *plane_kv,
    )
    far_kept = send(two, hop((1, 3)))
    one_up = send(one, hop((1, 2), (2, 3)))
    back2_swap, back3_swap = meet("far_both", far2_swap, far3_swap, *both_kv, two)
    far_other = send(back3_swap, hop((1, 3), cross=1))
    one_up_other = send(back2_swap, hop((1, 2), (2, 3), cross=1))
    own_keep, own_swap = meet("own", q_keep, *both_kv)
    own_other = send(own_swap, swap)
    half = head_count // 2
    out = None
    pieces = []
    for part, values in enumerate(
        (
            (own_keep, one_up, far_kept),
            (own_other, one_up_other, far_other),
        )
    ):
        local = combine(ids, values)
        over = across(local, half)
        beside = across(local, 1)
        over_beside = across(over, 1)
        pieces += [((part, 0), local), ((part, 1), beside), ((part, 2), over), ((part, 3), over_beside)]
    for step, chosen in enumerate((pieces[:2], pieces[2:6], pieces[6:])):
        which, features = zip(*chosen)
        out = project(step == 2, which, ids, out_weight, features, out)
    return out


def solution(mesh):
    in_specs = (P("seq", "head", None), P("head", None), P(None, "head"))
    out_specs = P("seq", "head")
    by_planes = mesh.shape["seq"] == 8 and mesh.shape["head"] == 4
    plan = planes_plan if by_planes else routed_plan

    return jax.shard_map(plan, mesh=mesh, in_specs=in_specs, out_specs=out_specs, check_vma=False)
```

```python
import functools
import math

import jax
import jax.numpy as jnp
from jax import lax
from jax.experimental import pallas as pl
from jax.experimental.pallas import tpu as pltpu
from jax.sharding import PartitionSpec as P


NEG = -1e30


def softmax_rows(query_part, query_pos, key_rows, value_rows, key_pos, usable, score_scale):
    scores = jnp.dot(query_part, key_rows.T, preferred_element_type=jnp.float32) * score_scale
    allowed = usable[None, :] & (key_pos[None, :] <= query_pos[:, None])
    scores = jnp.where(allowed, scores, -1e30)
    highest = jnp.max(scores, axis=1, keepdims=True)
    weights = jnp.exp(scores - highest)
    totals = jnp.sum(weights, axis=1, keepdims=True)
    probabilities = weights.astype(jnp.bfloat16)
    attended = jnp.dot(probabilities, value_rows, preferred_element_type=jnp.float32) / totals
    return attended.astype(jnp.bfloat16)


def attend_all(queries, key_rows, value_rows, positions, usable):
    length = queries.shape[0]
    rows_step = min(512, length)
    score_scale = 1.0 / math.sqrt(queries.shape[1])
    pieces = []
    for step_index in range(length // rows_step):
        first_row = step_index * rows_step
        key_end = first_row + rows_step
        pieces.append(
            softmax_rows(
                queries[first_row : first_row + rows_step],
                positions[first_row : first_row + rows_step],
                key_rows[:key_end],
                value_rows[:key_end],
                positions[:key_end],
                usable[:key_end],
                score_scale,
            )
        )
    return jnp.concatenate(pieces, axis=0)


def slot_tables(owners, myself, pair_slots):
    source_count, item_count = owners.shape
    item_ids = jnp.arange(item_count, dtype=jnp.int32)
    before = item_ids[None, :] < item_ids[:, None]
    same_owner = owners[:, :, None] == owners[:, None, :]
    rank_within = jnp.sum((same_owner & before[None]).astype(jnp.int32), axis=2)
    own_owner = lax.dynamic_index_in_dim(owners, myself, 0, keepdims=False)
    own_rank = lax.dynamic_index_in_dim(rank_within, myself, 0, keepdims=False)
    own_slot = own_owner * pair_slots + own_rank
    slot_ids = jnp.arange(source_count * pair_slots, dtype=jnp.int32)
    slot_match = own_slot[None, :] == slot_ids[:, None]
    source_item = jnp.sum(slot_match.astype(jnp.int32) * item_ids[None, :], axis=1)
    filled = jnp.any(slot_match, axis=1)
    rank_ids = jnp.arange(pair_slots, dtype=jnp.int32)
    arriving = (owners == myself)[:, None, :] & (rank_within[:, None, :] == rank_ids[None, :, None])
    arrived_item = jnp.sum(arriving.astype(jnp.int32) * item_ids[None, None, :], axis=2).reshape(-1)
    arrived = jnp.any(arriving, axis=2).reshape(-1)
    return (own_slot, source_item, filled, arrived_item, arrived)


def routed_plan(qkv_heads, clusters, out_weight):
    seq_count = lax.axis_size("seq")
    myself = lax.axis_index("seq")
    tok_rows, head_local, triple = qkv_heads.shape
    head_width = triple // 3
    block_total = clusters.shape[1]
    per_shard = block_total // seq_count
    block_len = tok_rows // per_shard
    capacity = 2 * per_shard
    cluster_table = clusters.reshape(head_local, seq_count, per_shard)
    blocks = qkv_heads.reshape(per_shard, block_len, head_local, triple).transpose(2, 0, 1, 3)
    pair_slots = (head_local * capacity + seq_count - 1) // seq_count
    owners = cluster_table.transpose(1, 0, 2).reshape(seq_count, head_local * per_shard)
    own_slot, source_item, filled, arrived_item, arrived = slot_tables(owners, myself, pair_slots)
    flat_blocks = blocks.reshape(head_local * per_shard, block_len, triple)
    outgoing = jnp.take(flat_blocks, source_item, axis=0)
    outgoing = jnp.where(filled[:, None, None], outgoing, jnp.zeros((), outgoing.dtype))
    incoming = lax.all_to_all(outgoing, "seq", split_axis=0, concat_axis=0, tiled=True)
    slot_head = arrived_item // per_shard
    slot_source = jnp.arange(seq_count * pair_slots, dtype=jnp.int32) // pair_slots
    slot_block = slot_source * per_shard + arrived_item % per_shard
    slot_count = incoming.shape[0]
    slot_ids = jnp.arange(slot_count, dtype=jnp.int32)
    compact_ids = jnp.arange(capacity, dtype=jnp.int32)
    place_all = jnp.zeros((slot_count,), jnp.int32)
    padded_parts = []
    for head_index in range(head_local):
        belongs = arrived & (slot_head == head_index)
        belongs_int = belongs.astype(jnp.int32)
        places = jnp.cumsum(belongs_int) - belongs_int
        chosen = belongs[None, :] & (places[None, :] == compact_ids[:, None])
        chosen_int = chosen.astype(jnp.int32)
        pick_slot = jnp.sum(chosen_int * slot_ids[None, :], axis=1)
        kept_valid = jnp.any(chosen, axis=1)
        kept_ids = jnp.sum(chosen_int * slot_block[None, :], axis=1)
        gathered = jnp.take(incoming, pick_slot, axis=0).reshape(capacity * block_len, triple)
        positions = (
            kept_ids[:, None] * block_len + jnp.arange(block_len, dtype=jnp.int32)[None, :]
        ).reshape(-1)
        usable = jnp.repeat(kept_valid, block_len)
        attended = attend_all(
            gathered[:, :head_width],
            gathered[:, head_width : 2 * head_width],
            gathered[:, 2 * head_width :],
            positions,
            usable,
        )
        padded_parts.append(attended.reshape(capacity, block_len, head_width))
        padded_parts.append(jnp.zeros((1, block_len, head_width), jnp.bfloat16))
        place_all = place_all + jnp.where(belongs, places, 0)
    padded_all = jnp.concatenate(padded_parts, axis=0)
    back_index = jnp.where(arrived, slot_head * (capacity + 1) + place_all, capacity)
    outbound = jnp.take(padded_all, back_index, axis=0)
    home_slots = lax.all_to_all(outbound, "seq", split_axis=0, concat_axis=0, tiled=True)
    own_blocks = jnp.take(home_slots, own_slot, axis=0).reshape(
        head_local, per_shard, block_len, head_width
    )
    features = own_blocks.transpose(1, 2, 0, 3).reshape(tok_rows, head_local * head_width)
    summed = jnp.dot(
        lax.all_gather(features, "head", axis=1, tiled=True),
        out_weight,
        preferred_element_type=jnp.float32,
    )
    return summed.astype(jnp.bfloat16)


VMEM_BYTES = 24 * 1024 * 1024


def split_kernel(ids_ref, qkv_ref, q_keep, kv_keep, first, second, third):
    column = ids_ref[0, 0]
    plane = ids_ref[0, 1]
    rows, width = q_keep.shape

    def pieces(head):
        yield lambda: qkv_ref[head, :, :width]
        yield lambda: qkv_ref[head, :, width : 2 * width]
        yield lambda: jnp.concatenate(
            [
                qkv_ref[head, b * width : (b + 1) * width, 2 * width :].T
                for b in range(rows // width)
            ],
            axis=0,
        )

    query, key, value = pieces(column)
    q_keep[...] = query()
    kv_keep[0] = key()
    kv_keep[1] = value()
    query, key, value = pieces(1 - column)

    @pl.when(plane == 0)
    def _():
        first[...] = key()
        second[...] = value()
        third[...] = query()

    @pl.when(plane > 0)
    def _():
        first[...] = query()
        second[...] = key()
        third[...] = value()


def split_heads(ids, by_head):
    heads, rows, triple = by_head.shape
    width = triple // 3
    step = rows // 4
    one = jax.ShapeDtypeStruct((rows, width), by_head.dtype)
    two = jax.ShapeDtypeStruct((2, rows, width), by_head.dtype)
    spec = pl.BlockSpec((step, width), lambda i: (i, 0))
    return pl.pallas_call(
        split_kernel,
        grid=(rows // step,),
        in_specs=[
            pl.BlockSpec(memory_space=pltpu.SMEM),
            pl.BlockSpec((heads, step, triple), lambda i: (0, i, 0)),
        ],
        out_specs=[spec, pl.BlockSpec((2, step, width), lambda i: (0, i, 0)), spec, spec, spec],
        out_shape=[one, two, one, one, one],
        compiler_params=pltpu.CompilerParams(vmem_limit_bytes=VMEM_BYTES),
        name="split_heads",
    )(ids, by_head)


OWN, UPPER, REST, BOTH, NEAR, KEPT, SWAPPED = range(0, 21, 3)
WHERE = 21
TABLE_ROWS = 24


def tables_kernel(per_shard, cluster_count, ids_ref, table_ref, out_ref):
    column = ids_ref[0, 0]
    plane = ids_ref[0, 1]
    blocks = table_ref.shape[1]
    span = 2 * per_shard
    out_ref[...] = jnp.zeros_like(out_ref)
    slot = lax.broadcasted_iota(jnp.int32, (1, 2 * blocks), 1)
    out_ref[WHERE : WHERE + 1, :] = jnp.where(slot == 0, column, plane)
    labels = jnp.where(column == 0, table_ref[0:1, :], table_ref[1:2, :])
    down = lax.broadcasted_iota(jnp.int32, (blocks, blocks), 0)
    along = lax.broadcasted_iota(jnp.int32, (blocks, blocks), 1)
    wide = jnp.broadcast_to(labels, (blocks, blocks))
    tall = jnp.sum(jnp.where(down == along, wide, 0), axis=1, keepdims=True)
    before = (tall < wide) | ((tall == wide) & (down < along))
    cluster = lax.broadcasted_iota(jnp.int32, (blocks, cluster_count), 1)
    block = lax.broadcasted_iota(jnp.int32, (blocks, 1), 0)
    in_plane = block // span
    side = lax.rem(block // per_shard, 2)
    high = (in_plane == 2) | (in_plane == 3)
    for row, member in (
        (OWN, in_plane == plane),
        (UPPER, (in_plane == plane) | ((in_plane == plane - 1) & (side == column))),
        (REST, (in_plane == plane - 1) & (side != column)),
        (BOTH, (in_plane == plane) | (in_plane == plane - 1)),
        (NEAR, in_plane == plane + 1),
        (KEPT, high & (side == column)),
        (SWAPPED, high & (side != column)),
    ):
        one = member.astype(jnp.int32)
        place = jnp.sum(jnp.where(before, one, 0), axis=0, keepdims=True)
        start = jnp.sum(jnp.where(tall < cluster, one, 0), axis=0, keepdims=True)
        count = jnp.sum(jnp.where(tall == cluster, one, 0), axis=0, keepdims=True)
        out_ref[row : row + 1, :blocks] = place
        out_ref[row + 1 : row + 2, :cluster_count] = start
        out_ref[row + 2 : row + 3, :cluster_count] = count


def block_tables(ids, table, per_shard):
    cluster_count = table.shape[1] // per_shard
    vmem = pl.BlockSpec(memory_space=pltpu.VMEM)
    return pl.pallas_call(
        functools.partial(tables_kernel, per_shard, cluster_count),
        in_specs=[pl.BlockSpec(memory_space=pltpu.SMEM), vmem],
        out_specs=vmem,
        out_shape=jax.ShapeDtypeStruct((TABLE_ROWS, 2 * table.shape[1]), jnp.int32),
        compiler_params=pltpu.CompilerParams(vmem_limit_bytes=VMEM_BYTES),
        name="block_tables",
    )(ids, table)


KINDS = {
    "own": (OWN, OWN, 4, (1, 2, 4)),
    "near": (OWN, NEAR, 2, (1, 2)),
    "far_high": (UPPER, KEPT, 3, (1, 2, 3)),
    "far_low": (REST, KEPT, 1, (1,)),
    "far_both": (BOTH, SWAPPED, 4, (2, 4)),
}


def attend_kernel(kind, per_shard, cluster_count, sizes, tab, *refs):
    own = kind == "own"
    kv_row, q_row = KINDS[kind][:2]
    plane_keys = kind != "far_low"
    low_kept = kind in ("own", "far_high", "far_both")
    low_rest = kind in ("own", "far_low", "far_both")
    merging = kind == "far_low"
    q_count = 1 if own else 2
    kv_count = 4 * plane_keys + low_kept + 2 * low_rest
    q_refs = refs[:q_count]
    kv_refs = refs[q_count : q_count + kv_count]
    refs = refs[q_count + kv_count :]
    earlier, refs = (refs[:2], refs[2:]) if merging else ((), refs)
    out_refs = refs[:2]
    keys, values, queries, outs, logs, mine = refs[2:]
    column = tab[WHERE, 0]
    plane = tab[WHERE, 1]
    width = keys.shape[2]
    scale = 1.0 / math.sqrt(width)
    log_scale = scale / math.log(2.0)
    if own:
        kv_row = jnp.where(plane == 1, BOTH, OWN)

    def body():
        used = tab[kv_row + 1, cluster_count - 1] + tab[kv_row + 2, cluster_count - 1]

        def bring(shard, key_ref, value_ref):
            for b in range(per_shard):
                to = tab[kv_row, shard * per_shard + b]
                keys[to] = key_ref[b * width : (b + 1) * width, :]
                values[to] = value_ref[b * width : (b + 1) * width, :]

        if plane_keys:
            next_shard = 2 * plane + 1 - column
            kept, first, second, third = kv_refs[:4]
            bring(2 * plane + column, kept.at[0], kept.at[1])

            @pl.when(plane == 0)
            def _():
                bring(next_shard, first, second)

            @pl.when(plane > 0)
            def _():
                bring(next_shard, second, third)

        def bring_low():
            if low_kept:
                low_keep = kv_refs[4]
                bring(2 * plane - 2 + column, low_keep.at[0], low_keep.at[1])
            if low_rest:
                bring(2 * plane - 1 - column, kv_refs[-2], kv_refs[-1])

        if own:
            pl.when(plane == 1)(bring_low)
        else:
            bring_low()

        def blank(i, carry):
            keys[used + i] = jnp.zeros(keys.shape[1:], keys.dtype)
            values[used + i] = jnp.zeros(values.shape[1:], values.dtype)
            return carry

        lax.fori_loop(0, sizes[-1], blank, 0)

        if own:
            shards = (2 * plane + column, 2 * plane + 1 - column)
        elif kind == "near":
            shards = (2 * plane + 2 + column, 2 * plane + 3 - column)
        elif kind == "far_both":
            shards = (2 * plane + 3 - column, 2 * plane + 5 - column)
        else:
            shards = (2 * plane + 2 + column, 2 * plane + 4 + column)

        def bring_query(shard, q_ref):
            for b in range(per_shard):
                to = tab[q_row, shard * per_shard + b]
                queries[to] = q_ref[b * width : (b + 1) * width, :]

        bring_query(shards[0], q_refs[0])
        if own:

            @pl.when(plane == 0)
            def _():
                bring_query(shards[1], third)

            @pl.when(plane > 0)
            def _():
                bring_query(shards[1], first)
        else:
            bring_query(shards[1], q_refs[1])

        if own:
            ahead = lax.broadcasted_iota(jnp.int32, (width, 4 * width), 0)
            ahead -= lax.broadcasted_iota(jnp.int32, (width, 4 * width), 1)

        def cluster(c, carry):
            begin = tab[kv_row + 1, c]
            length = tab[kv_row + 2, c]
            q_begin = tab[q_row + 1, c]
            q_count = tab[q_row + 2, c]

            def tile(wide, most, below):
                query = queries[pl.ds(q_begin, wide)].reshape(wide * width, width)
                parts = []
                for u in range(most):
                    part = lax.dot_general(
                        keys[begin + u],
                        query,
                        (((1,), (1,)), ((), ())),
                        preferred_element_type=jnp.float32,
                    )
                    if own:
                        allowed = ahead[:, : wide * width] <= (length - q_count - u) * width
                        part = jnp.where(allowed, part, NEG)
                    elif u > below:
                        part = jnp.where(u < length, part, NEG)
                    parts.append(part)
                scores = jnp.concatenate(parts, axis=0)
                top = jnp.max(scores, axis=0, keepdims=True)
                weights = jnp.exp2((scores - top) * log_scale)
                total = jnp.sum(weights, axis=0, keepdims=True)
                acc = jnp.dot(
                    jnp.concatenate([values[begin + u] for u in range(most)], axis=1),
                    weights.astype(jnp.bfloat16),
                    preferred_element_type=jnp.float32,
                )
                result = (acc / total).astype(outs.dtype)
                log = top * scale + jnp.log(total)
                for j in range(wide):
                    outs[q_begin + j] = result[:, j * width : (j + 1) * width]
                    logs[pl.ds(q_begin + j, 1), :] = log[:, j * width : (j + 1) * width]

            for wide in (2, 4):
                for k, most in enumerate(sizes):
                    below = sizes[k - 1] if k else 0

                    fits = (q_count > wide - 2) & (q_count <= wide)

                    @pl.when(fits & (length > below) & (length <= most))
                    def _(wide=wide, most=most, below=below):
                        tile(wide, most, below)

            if not own:

                @pl.when(length == 0)
                def _():
                    def empty(i, carry):
                        outs[q_begin + i] = jnp.zeros((width, width), outs.dtype)
                        logs[pl.ds(q_begin + i, 1), :] = jnp.full((1, width), NEG, jnp.float32)
                        return carry

                    lax.fori_loop(0, q_count, empty, 0)

            return carry

        lax.fori_loop(0, cluster_count, cluster, 0)
        for g, out_ref in enumerate(out_refs):
            for b in range(per_shard):
                mine[b : b + 1, :] = logs[pl.ds(tab[q_row, shards[g] * per_shard + b], 1), :]
            rest = mine[...]
            if merging:
                other = log_of(earlier[g], per_shard * width)
                top = jnp.maximum(rest, other)
                share, other_share = jnp.exp(rest - top), jnp.exp(other - top)
                total = share + other_share
                share, other_share = share / total, other_share / total
                rest = jnp.maximum(top + jnp.log(total), NEG)
            for b in range(per_shard):
                lines = slice(b * width, (b + 1) * width)
                block = outs[tab[q_row, shards[g] * per_shard + b]]
                if merging:
                    block = block.astype(jnp.float32) * share[b : b + 1]
                    block += earlier[g][lines, :].astype(jnp.float32) * other_share[b : b + 1]
                out_ref[lines, :] = block.astype(jnp.bfloat16)
            pieces = []
            for _ in range(3):
                piece = rest.astype(jnp.bfloat16).astype(jnp.float32)
                rest = rest - piece
                pieces.append(piece)
            pieces.append(jnp.zeros_like(rest))
            out_ref[per_shard * width :, :] = jnp.concatenate(pieces, axis=0).astype(jnp.bfloat16)

    if own:
        body()
    else:

        @pl.when(plane == (2 if kind == "near" else 1))
        def _():
            body()


def both_near_kernel(per_shard, cluster_count, sizes, tab, *refs):
    both, near, outs, scratch = refs[:9], refs[9:15], refs[15:17], refs[17:]
    attend_kernel("far_both", per_shard, cluster_count, sizes[0], tab, *both, *outs, *scratch)
    attend_kernel("near", per_shard, cluster_count, sizes[1], tab, *near, *outs[::-1], *scratch)


def log_of(ref, rows):
    tail = ref[rows:, :].astype(jnp.float32)
    step = tail.shape[0] // 4
    return tail[:step] + tail[step : 2 * step] + tail[2 * step : 3 * step]


def attend(kind, cluster_count, tables, operands):
    rows, width = operands[0].shape
    per_shard = rows // width
    kinds = ("far_both", "near") if kind == "both_near" else (kind,)
    sizes = tuple(tuple(q * per_shard // 4 for q in KINDS[k][3]) for k in kinds)
    held = max(KINDS[k][2] * per_shard + size[-1] for k, size in zip(kinds, sizes))
    if kind == "both_near":
        kernel = functools.partial(both_near_kernel, per_shard, cluster_count, sizes)
    else:
        kernel = functools.partial(attend_kernel, kind, per_shard, cluster_count, sizes[0])
    smem = pl.BlockSpec(memory_space=pltpu.SMEM)
    vmem = pl.BlockSpec(memory_space=pltpu.VMEM)
    out = jax.ShapeDtypeStruct((per_shard * (width + 4), width), jnp.bfloat16)
    tile = (width, width)
    return pl.pallas_call(
        kernel,
        in_specs=[smem] + [vmem] * len(operands),
        out_specs=[vmem] * 2,
        out_shape=[out] * 2,
        scratch_shapes=[
            pltpu.VMEM((held,) + tile, jnp.bfloat16),
            pltpu.VMEM((held,) + tile, jnp.bfloat16),
            pltpu.VMEM((2 * per_shard + 4,) + tile, jnp.bfloat16),
            pltpu.VMEM((2 * per_shard + 4,) + tile, jnp.bfloat16),
            pltpu.VMEM((2 * per_shard + 8, width), jnp.float32),
            pltpu.VMEM((per_shard, width), jnp.float32),
        ],
        compiler_params=pltpu.CompilerParams(vmem_limit_bytes=VMEM_BYTES),
    )(tables, *operands)


def combine_kernel(ids_ref, own, up2, up3, third, out_ref):
    plane = ids_ref[0, 1]
    rows, width = out_ref.shape
    own_log = log_of(own, rows)
    up_log = jnp.where(plane == 3, log_of(up3, rows), log_of(up2, rows))
    up_log = jnp.where(plane > 1, up_log, NEG)
    far_log = jnp.where(plane == 3, log_of(third, rows), NEG)
    top = jnp.maximum(jnp.maximum(own_log, up_log), far_log)
    own_part = jnp.exp(own_log - top)
    up_part = jnp.exp(up_log - top)
    far_part = jnp.exp(far_log - top)
    share = 1.0 / (own_part + up_part + far_part)
    own_part, up_part, far_part = own_part * share, up_part * share, far_part * share
    for b in range(rows // width):
        lines = slice(b * width, (b + 1) * width)
        up = jnp.where(plane == 3, up3[lines, :], up2[lines, :])
        mixed = (
            own[lines, :].astype(jnp.float32) * own_part[b : b + 1]
            + up.astype(jnp.float32) * up_part[b : b + 1]
            + third[lines, :].astype(jnp.float32) * far_part[b : b + 1]
        )
        out_ref[lines, :] = mixed.T.astype(jnp.bfloat16)


def combine(ids, values):
    size, width = values[-1].shape
    rows = size // (width + 4) * width
    vmem = pl.BlockSpec(memory_space=pltpu.VMEM)
    return pl.pallas_call(
        combine_kernel,
        in_specs=[pl.BlockSpec(memory_space=pltpu.SMEM)] + [vmem] * len(values),
        out_specs=vmem,
        out_shape=jax.ShapeDtypeStruct((rows, width), jnp.bfloat16),
        compiler_params=pltpu.CompilerParams(vmem_limit_bytes=VMEM_BYTES),
        name="combine",
    )(ids, *values)


def project_kernel(which, ids_ref, weight_ref, *refs):
    group = ids_ref[0, 2]
    column = ids_ref[0, 0]
    heads = (column, 1 - column)
    out_ref = refs[-1]
    features = refs[: len(which)]
    given = refs[len(which)] if len(refs) > len(which) + 1 else None
    depth = features[0].shape[1]
    cols = out_ref.shape[1]
    here = pl.ds(pl.multiple_of(pl.program_id(0) * cols, cols), cols)
    lines = [
        pl.ds(pl.multiple_of(((group ^ j) * 2 + heads[part]) * depth, depth), depth)
        for part, j in which
    ]
    right = jnp.concatenate([weight_ref[at, here] for at in lines], axis=0)
    chunk = 512
    for start in range(0, out_ref.shape[0], chunk):
        rows = slice(start, start + chunk)
        left = jnp.concatenate([f[rows, :] for f in features], axis=1)
        acc = jnp.dot(left, right, preferred_element_type=jnp.float32)
        if given is not None:
            acc = acc + given[rows, here]
        out_ref[rows, :] = acc.astype(out_ref.dtype)


def project(final, which, ids, weight, features, given):
    rows = features[0].shape[0]
    vmem = pl.BlockSpec(memory_space=pltpu.VMEM)
    given = [] if given is None else [given]
    width = weight.shape[1]
    step = width // 2 if final else width
    return pl.pallas_call(
        functools.partial(project_kernel, which),
        grid=(width // step,),
        in_specs=[pl.BlockSpec(memory_space=pltpu.SMEM)]
        + [vmem] * (1 + len(features) + len(given)),
        out_specs=pl.BlockSpec((rows, step), lambda i: (0, i)),
        out_shape=jax.ShapeDtypeStruct((rows, width), jnp.bfloat16 if final else jnp.float32),
        compiler_params=pltpu.CompilerParams(vmem_limit_bytes=VMEM_BYTES),
        name="project",
    )(ids, weight, *features, *given)


def planes_plan(qkv_heads, clusters, out_weight):
    seq_count = lax.axis_size("seq")
    head_count = lax.axis_size("head")
    shard = lax.axis_index("seq")
    group = lax.axis_index("head")
    tok_rows, _, triple = qkv_heads.shape
    width = triple // 3
    ids = jnp.stack([shard % 2, shard // 2, group]).astype(jnp.int32).reshape(1, 3)

    swap = [(c, c ^ 1) for c in range(seq_count)]

    def hop(*moves, cross=0):
        return [(2 * a + x, 2 * b + (x ^ cross)) for a, b in moves for x in range(2)]

    def send(value, pairs):
        return lax.ppermute(value, "seq", pairs)

    def across(value, flip):
        return lax.ppermute(value, "head", [(g, g ^ flip) for g in range(head_count)])

    by_head = qkv_heads.transpose(1, 0, 2)
    q_keep, kv_keep, give1, give2, give3 = split_heads(ids, by_head)

    first = send(give1, swap)
    low_keep = send(kv_keep, hop((0, 1)))
    far2_keep = send(q_keep, hop((2, 1)))
    far3_keep = send(q_keep, hop((3, 1)))
    second = send(give2, swap)
    third = send(give3, swap)
    near_keep = send(q_keep, hop((3, 2)))
    low_first = send(first, hop((0, 1)))
    far2_swap = send(first, hop((2, 1)))
    far3_swap = send(first, hop((3, 1)))
    low_second = send(second, hop((0, 1)))
    near_swap = send(first, hop((3, 2)))

    per_shard = tok_rows // width
    cluster_count = clusters.shape[1] // per_shard
    tables = block_tables(ids, clusters, per_shard)

    def meet(kind, *operands):
        return attend(kind, cluster_count, tables, operands)

    plane_kv = (kv_keep, first, second, third)
    both_kv = plane_kv + (low_keep, low_first, low_second)
    started = meet("far_high", far2_keep, far3_keep, *plane_kv, low_keep)
    back2_keep, back3_keep = meet(
        "far_low", far2_keep, far3_keep, low_first, low_second, *started
    )
    far_kept = send(back3_keep, hop((1, 3)))
    up2_kept = send(back2_keep, hop((1, 2)))
    one, two = meet(
        "both_near", far2_swap, far3_swap, *both_kv, near_keep, near_swap, *plane_kv
    )
    far_other = send(two, hop((1, 3), cross=1))
    up_other = send(one, hop((1, 2), (2, 3), cross=1))
    up3_kept = send(two, hop((2, 3)))
    own_keep, own_swap = meet("own", q_keep, *both_kv)
    own_other = send(own_swap, swap)
    half = head_count // 2
    out = None
    pieces = []
    for part, values in enumerate(
        (
            (own_keep, up2_kept, up3_kept, far_kept),
            (own_other, up_other, up_other, far_other),
        )
    ):
        local = combine(ids, values)
        over = across(local, half)
        beside = across(local, 1)
        over_beside = across(over, 1)
        pieces += [((part, 0), local), ((part, 1), beside), ((part, 2), over), ((part, 3), over_beside)]
    for step, chosen in enumerate((pieces[:2], pieces[2:6], pieces[6:])):
        which, features = zip(*chosen)
        out = project(step == 2, which, ids, out_weight, features, out)
    return out


def solution(mesh):
    in_specs = (P("seq", "head", None), P("head", None), P(None, "head"))
    out_specs = P("seq", "head")
    by_planes = mesh.shape["seq"] == 8 and mesh.shape["head"] == 4
    plan = planes_plan if by_planes else routed_plan

    return jax.shard_map(plan, mesh=mesh, in_specs=in_specs, out_specs=out_specs, check_vma=False)
```
